512 devices in a mesh: cells: 128 (over z, y, core), mem: 4 (over x).
Axes of the slice: x: 4, y: 4, z: 16, core: 2. Of those that a mesh axis runs over, the one named last changes fastest.
Arguments:
- ensemble: float32 [512, 262144], P('mem', 'cells'), may hold values from -6 to 6
- observed: float32 [262144], P('cells'), may hold values from -6 to 6
- obs_sigma: float32 [262144], P('cells'), may hold values from 0.1 to 1
- obs_index: int32 [262144], P('cells'), may hold values from 0 to 2047
- member_seeds: int32 [512], P('mem'), may hold values from 1 to 65520
Outputs:
- updated: float32 [512, 262144], P('mem', 'cells')
The draws below stay inside these ranges and needn't reach their ends.
All inputs are finite; a program needn't handle non-finite values.
Results may differ from the reference program's by a relative error of at most 0.0003.
Values sent between devices are 32-bit elements; how exact they have to be, the bound alone decides.
A program may use at most 64 MiB of HBM per device.

```python
import math
import jax
import jax.numpy as jnp
from jax import lax

NE = 512
SECTION = 1
CELL_DEV = 2048
OBS_DEV = 2048
CELLS = 262144
OBS = 262144


def place_ends(result, key, smallest, high):
    shape = result.shape
    spot = [jax.random.randint(jax.random.fold_in(key, axis), (), 0, shape[axis]) for axis in range(len(shape))]
    result = result.at[tuple(spot)].set(smallest)
    longest = shape.index(max(shape))
    spot[longest] = (spot[longest] + 1) % shape[longest]
    return result.at[tuple(spot)].set(high)


def block_scale(key, shape, split, smallest, largest):
    def one(dim, parts):
        heights = jax.random.uniform(jax.random.fold_in(jax.random.fold_in(key, 6), dim), (parts,), jnp.float32, smallest / len(split), largest / len(split))
        return jnp.repeat(jnp.exp(heights), shape[dim] // parts).reshape((-1,) + (1,) * (len(shape) - dim - 1))

    gain = one(*split[0])
    for cut in split[1:]:
        gain = gain * one(*cut)
    return gain


def gaussian(rng, dims, spread, bound, cuts=(), held_as=jnp.bfloat16):
    array = spread * jax.random.normal(rng, dims, jnp.float32)
    if cuts:
        array = array * block_scale(rng, dims, cuts, -0.22, 0.18)
    return jnp.clip(array, -bound, bound).astype(held_as)


def setup_inputs(seed: int = 0) -> dict:
    seeds = jax.random.split(jax.random.key(seed), 6)
    return {
        "ensemble": gaussian(seeds[0], (NE, CELLS), 1.0, 6.0, ((0, 4), (1, 128)), jnp.float32),
        "observed": gaussian(seeds[1], (OBS,), 1.0, 6.0, ((0, 128),), jnp.float32),
        "obs_sigma": jnp.clip(jnp.exp(math.log(1.0) - 2.3025851 * jax.random.uniform(seeds[2], (OBS,), jnp.float32) ** block_scale(seeds[2], (OBS,), ((0, 128),), -0.2, 0.2)), 0.1, 1.0),
        "obs_index": place_ends(jax.random.randint(seeds[3], (OBS,), 0, CELL_DEV), jax.random.fold_in(seeds[3], 1), 0, CELL_DEV - 1).astype(jnp.int32),
        "member_seeds": place_ends(jax.random.randint(seeds[4], (NE,), 1, 65521), jax.random.fold_in(seeds[4], 1), 1, 65520).astype(jnp.int32),
    }


plan = (28.0 / 3.0, 7.0, 4.0, 2.0)

def perturbation(member_seeds, positions):
    seeds_col = member_seeds[:, None].astype(jnp.int32)
    where_row = positions[None, :].astype(jnp.int32)
    hashed = (seeds_col * 389 % 65521 + where_row % 65521 * (seeds_col % 997 + 1)) % 65521
    return math.sqrt(2.0) * jnp.cos(2.0 * math.pi / 65521.0 * hashed.astype(jnp.float32))

def reference(ensemble, observed, obs_sigma, obs_index, member_seeds):
    highest = lax.Precision.HIGHEST
    alpha = jnp.float32(plan[SECTION])
    positions = jnp.arange(OBS, dtype=jnp.int32)
    cell_of = (obs_index + positions // OBS_DEV * CELL_DEV).astype(jnp.int32)
    value = ensemble[:, cell_of]
    predicted = jnp.tanh(value) + 0.5 * value
    noise = perturbation(member_seeds, positions)
    scaled = (predicted - lax.optimization_barrier(jnp.mean(predicted, axis=0))) / (obs_sigma * math.sqrt(NE - 1.0))
    innovation = observed / obs_sigma + jnp.sqrt(alpha) * noise - predicted / obs_sigma
    gram_matrix = jnp.dot(scaled, scaled.T, precision=highest)
    cross_terms = jnp.dot(scaled, innovation.T, precision=highest)
    factor = jnp.linalg.cholesky(gram_matrix + alpha * jnp.eye(NE, dtype=jnp.float32))
    weights = jax.scipy.linalg.cho_solve((factor, True), cross_terms)
    anomalies = ensemble - lax.optimization_barrier(jnp.mean(ensemble, axis=0))
    return ensemble + jnp.dot(weights.T, anomalies, precision=highest) / math.sqrt(NE - 1.0)
```

```python
import functools
import math

import jax
import jax.numpy as jnp
from jax import lax
from jax.experimental import pallas as pl
from jax.experimental.pallas import tpu as pltpu
from jax.sharding import Mesh
from jax.sharding import PartitionSpec as P

SECTION = 1
CELLS = ("cells_0", "cells_1", "cells_2")
AXES = ("cells_0", "cells_1", "cells_2", "mem")
PLAN = (28.0 / 3.0, 7.0, 4.0, 2.0)
HI = lax.Precision.HIGHEST
MESH = pl.DeviceIdType.MESH
VM = pl.BlockSpec(memory_space=pltpu.VMEM)
ANY = pl.BlockSpec(memory_space=pl.ANY)
F32 = jnp.float32


def remote(src, dst, send, recv, where):
    return pltpu.make_async_remote_copy(
        src_ref=src, dst_ref=dst, send_sem=send, recv_sem=recv, device_id=where, device_id_type=MESH
    )


def at_axis(axis, index):
    return {axis: index}


def greet(peers):
    barrier = pltpu.get_barrier_semaphore()
    for peer in peers:
        pl.semaphore_signal(barrier, inc=1, device_id=peer, device_id_type=MESH)
    pl.semaphore_wait(barrier, len(peers))


def order_of(n):
    return sorted(range(1, n), key=lambda d: -min(d, n - d))


def exchange_kernel(nx, p_ref, s_ref, o_ref, so_ref, send, recv, own):
    x = lax.axis_index("mem")
    rows, width = p_ref.shape[0], p_ref.shape[1] // nx
    greet([at_axis("mem", lax.rem(x + d, nx)) for d in range(1, nx)])
    mine = pl.ds(pl.multiple_of(x * rows, rows), rows)
    copies = []
    for d in order_of(nx):
        to = lax.rem(x + d, nx)
        copies.append(remote(s_ref, so_ref.at[x], send.at[1, d], recv.at[1, d], at_axis("mem", to)))
        cols = pl.ds(pl.multiple_of(to * width, width), width)
        copies.append(remote(p_ref.at[:, cols], o_ref.at[mine, :], send.at[0, d], recv.at[0, d], at_axis("mem", to)))
    for c in copies:
        c.start()
    a = pltpu.make_async_copy(p_ref.at[:, pl.ds(pl.multiple_of(x * width, width), width)], o_ref.at[mine, :], own.at[0])
    b = pltpu.make_async_copy(s_ref, so_ref.at[x], own.at[1])
    a.start()
    b.start()
    a.wait()
    b.wait()
    for c in copies:
        c.wait()


def exchange(predicted, seeds, nx):
    rows, width = predicted.shape
    return pl.pallas_call(
        functools.partial(exchange_kernel, nx),
        out_shape=(
            jax.ShapeDtypeStruct((rows * nx, width // nx), F32),
            jax.ShapeDtypeStruct((nx, 8, rows), F32),
        ),
        in_specs=[VM, VM],
        out_specs=(VM, VM),
        scratch_shapes=[pltpu.SemaphoreType.DMA((2, nx))] * 2 + [pltpu.SemaphoreType.DMA((2,))],
        compiler_params=pltpu.CompilerParams(collective_id=0, has_side_effects=True),
        name="exchange",
    )(predicted, seeds)


def mod_prime(v):
    q = jnp.floor(v.astype(F32) * (1.0 / 65521.0)).astype(jnp.int32)
    r = v - q * 65521
    r = jnp.where(r < 0, r + 65521, r)
    return jnp.where(r >= 65521, r - 65521, r)


def cosine(h):
    h = jnp.minimum(h, 65521 - h)
    v = (65521 - 4 * h).astype(F32) * (math.pi / (2.0 * 65521.0))
    s = v * v
    poly = jnp.full_like(s, -1.0 / 39916800.0)
    for k in (9, 7, 5, 3, 1):
        poly = poly * s + (-1.0) ** ((k - 1) // 2) / math.factorial(k)
    return poly * v


def local_kernel(nx, alpha, p_ref, s_ref, ob_ref, sg_ref, gp_ref, dp_ref, sc, mm):
    members, width = p_ref.shape
    mean = jnp.sum(p_ref[...], axis=0, keepdims=True) * (1.0 / members)
    x = lax.axis_index("mem")
    part = pl.ds(pl.multiple_of(x * width, width), width)
    inv = 1.0 / sg_ref[:, part]
    scale = inv * (1.0 / math.sqrt(members - 1.0))
    shift = (ob_ref[:, part] - mean) * inv
    base = lax.axis_index(CELLS) * ob_ref.shape[1] + x * width
    where = mod_prime(lax.broadcasted_iota(jnp.int32, (1, width), 1) + base)
    reps = p_ref.shape[1] // 128

    def block(b, _):
        rows = pl.ds(pl.multiple_of(b * 128, 128), 128)
        seed = jnp.broadcast_to(s_ref[b, 0:1, :], (128, 128)).T.astype(jnp.int32)
        first = mod_prime(seed * 389)
        second = seed - 997 * jnp.floor((seed.astype(F32) + 0.5) * (1.0 / 997.0)).astype(jnp.int32) + 1
        sc[rows, :] = (p_ref[rows, :] - mean) * scale
        for c in range(reps):
            cols = slice(128 * c, 128 * c + 128)
            h = mod_prime(first + where[:, cols] * second)
            mm[rows, cols] = cosine(h) * math.sqrt(2.0 * alpha) + shift[:, cols]
        return 0

    lax.fori_loop(0, members // 128, block, 0)
    dn = (((1,), (1,)), ((), ()))

    def product(b, _):
        rows = pl.ds(pl.multiple_of(b * 128, 128), 128)
        left = sc[rows, :]
        groups = pl.ds(pl.multiple_of(b * 16, 16), 16)
        half, within = b // 2, pl.ds(pl.multiple_of(lax.rem(b, 2) * 16, 16), 16)
        for c in range(members // 128):
            cols = pl.ds(128 * c, 128)
            g = lax.dot_general(left, sc[cols, :], dn, precision=HI, preferred_element_type=F32)
            gp_ref[groups, c] = g.reshape(16, 8, 128)
            d = lax.dot_general(left, mm[cols, :], dn, precision=HI, preferred_element_type=F32)
            dp_ref[half, c, within] = d.reshape(16, 8, 128)
        return 0

    lax.fori_loop(0, members // 128, product, 0)


def local_products(pred, seeds, obs, sigma, nx, alpha):
    members, width = pred.shape
    return pl.pallas_call(
        functools.partial(local_kernel, nx, alpha),
        out_shape=(
            jax.ShapeDtypeStruct((members // 8, members // 128, 8, 128), F32),
            jax.ShapeDtypeStruct((2, members // 128, members // 16, 8, 128), F32),
        ),
        in_specs=[VM] * 4,
        out_specs=(VM, VM),
        scratch_shapes=[pltpu.VMEM((members, width), F32)] * 2,
        name="local_products",
    )(pred, seeds, obs, sigma)


def reduce_kernel(n, gp, dp, e_ref, go, do, left, right, rg0, rd0, sg0, sd0, rg1, rd1, sg1, sd1, rg2, rd2, zs, rz, zg,
                  cs, cr, xs, xr, ys, yr, zss, zsr, es, er):
    nx, ny, nz = n
    z, y, c, x = (lax.axis_index(a) for a in AXES)
    oc = 1 - c

    def xat(d):
        return lax.rem(x + d, nx)

    def yat(d):
        return lax.rem(y + d, ny)

    def zat(d):
        return lax.rem(z + d, nz)

    core = at_axis("cells_2", oc)
    greet(
        [core]
        + [at_axis("mem", xat(d)) for d in range(1, nx)]
        + [at_axis("cells_1", yat(d)) for d in range(1, ny)]
        + [at_axis("cells_0", zat(d)) for d in range(1, nz)]
    )
    ox, oy, oz = order_of(nx) + [0], order_of(ny) + [0], order_of(nz)
    sent = []

    def go_(copy):
        copy.start()
        sent.append(copy)
        return copy

    c0d, c0g = {}, {}
    for i in range(max(nx, ny)):
        if i < nx:
            d = ox[i]
            c0d[d] = go_(remote(dp.at[oc, xat(d)], rd0.at[xat(d)], cs.at[0, d], cr.at[0, d], core))
        if i < ny:
            d = oy[i]
            c0g[d] = go_(remote(gp.at[oc, yat(d)], rg0.at[yat(d)], cs.at[1, d], cr.at[1, d], core))
    d1, g1 = {}, {}
    for i in range(max(nx, ny)):
        if i < nx:
            d = ox[i]
            c0d[d].wait_recv()
            sd0[xat(d)] = dp[c, xat(d)] + rd0[xat(d)]
            if d:
                d1[d] = go_(remote(sd0.at[xat(d)], rd1.at[d], xs.at[0, d], xr.at[0, d], at_axis("mem", xat(d))))
        if i < ny:
            d = oy[i]
            c0g[d].wait_recv()
            sg0[yat(d)] = gp[c, yat(d)] + rg0[yat(d)]
            if d:
                g1[d] = go_(remote(sg0.at[yat(d)], rg1.at[d], ys.at[0, d], yr.at[0, d], at_axis("cells_1", yat(d))))
    d2, g2 = {}, {}
    for d in ox[:-1]:
        d1[d].wait_recv()
    for d in oy:
        total = sd0[x, yat(d)]
        for k in range(1, nx):
            total = total + rd1[k, yat(d)]
        sd1[yat(d)] = total
        if d:
            d2[d] = go_(remote(sd1.at[yat(d)], rd2.at[d], ys.at[1, d], yr.at[1, d], at_axis("cells_1", yat(d))))
    for d in oy[:-1]:
        g1[d].wait_recv()
    for d in ox:
        total = sg0[y, xat(d)]
        for k in range(1, ny):
            total = total + rg1[k, xat(d)]
        sg1[xat(d)] = total
        if d:
            g2[d] = go_(remote(sg1.at[xat(d)], rg2.at[d], xs.at[1, d], xr.at[1, d], at_axis("mem", xat(d))))
    half = e_ref.shape[0] // 2
    eo = []
    for h in range(2):
        part = e_ref.at[pl.ds(h * half, half), :]
        eo.append(go_(remote(part, left.at[h], es.at[0, h], er.at[0, h], at_axis("mem", xat(1)))))
        eo.append(go_(remote(part, right.at[h], es.at[1, h], er.at[1, h], at_axis("mem", xat(nx - 1)))))
    for d in oy[:-1]:
        d2[d].wait_recv()
    td, tg = sd1.shape[1], sg1.shape[1]
    q = zs.shape[1]
    total = sd1[y]
    for k in range(1, ny):
        total = total + rd2[k]
    for t in range(td):
        zs[t // q, t % q] = total[t]
    for d in ox[:-1]:
        g2[d].wait_recv()
    total = sg1[x]
    for k in range(1, nx):
        total = total + rg2[k]
    for t in range(tg):
        zs[(td + t) // q, (td + t) % q] = total[t]
    z1 = [go_(remote(zs.at[zat(d)], rz.at[d], zss.at[0, d], zsr.at[0, d], at_axis("cells_0", zat(d)))) for d in oz]
    for w in z1:
        w.wait_recv()
    total = zs[z]
    for k in range(1, nz):
        total = total + rz[k]
    zg[z] = total
    z2 = [go_(remote(zg.at[z], zg.at[z], zss.at[1, d], zsr.at[1, d], at_axis("cells_0", zat(d)))) for d in oz]
    for w in z2:
        w.wait_recv()
    nd = td // q
    for t in range(td):
        do[c, y, t // q, t % q] = zg[t // q, t % q]
    for t in range(tg):
        go[c, y, x, t // q, t % q] = zg[nd + t // q, t % q]
    dy, gx, gy = {}, {}, {}
    for d in ox[:-1]:
        gx[d] = go_(remote(zg.at[pl.ds(nd, tg // q)], go.at[c, y, x], xs.at[2, d], xr.at[2, d], at_axis("mem", xat(d))))
    for d in oy[:-1]:
        dy[d] = go_(remote(zg.at[pl.ds(0, nd)], do.at[c, y], ys.at[2, d], yr.at[2, d], at_axis("cells_1", yat(d))))
    last = [go_(remote(zg.at[pl.ds(0, nd)], do.at[c, y], cs.at[2, 0], cr.at[2, 0], core))]
    for d in ox[:-1]:
        gx[d].wait_recv()
    for d in oy[:-1]:
        gy[d] = go_(remote(go.at[c, y], go.at[c, y], ys.at[3, d], yr.at[3, d], at_axis("cells_1", yat(d))))
    last.append(go_(remote(go.at[c, y], go.at[c, y], cs.at[3, 0], cr.at[3, 0], core)))
    for d in sorted(oy[:-1]):
        frm = yat(ny - d)
        dy[d].wait_recv()
        last.append(go_(remote(do.at[c, frm], do.at[c, frm], cs.at[2, d], cr.at[2, d], core)))
    for d in (1, ny - 1) + tuple(range(2, ny - 1)):
        if d in gy:
            frm = yat(ny - d)
            g = gy.pop(d)
            g.wait_recv()
            last.append(go_(remote(go.at[c, frm], go.at[c, frm], cs.at[3, d], cr.at[3, d], core)))
    for w in last:
        w.wait_recv()
    for w in eo:
        w.wait_recv()
    for w in sent:
        w.wait_send()


def reduce_all(gp, dp, e, nx, ny, nz):
    tg, td = gp.shape[3], dp.shape[3]
    q = (tg + td) // nz
    tile = (8, 128)
    m = max(nx, ny)
    half = (2, e.shape[0] // 2, e.shape[1])
    dma = pltpu.SemaphoreType.DMA
    return pl.pallas_call(
        functools.partial(reduce_kernel, (nx, ny, nz)),
        out_shape=(
            jax.ShapeDtypeStruct((2, ny, nx, tg // q, q, *tile), F32),
            jax.ShapeDtypeStruct((2, ny, td // q, q, *tile), F32),
            jax.ShapeDtypeStruct(half, F32),
            jax.ShapeDtypeStruct(half, F32),
        ),
        in_specs=[VM, VM, ANY],
        out_specs=(VM, VM, ANY, ANY),
        scratch_shapes=[
            pltpu.VMEM((ny, nx, tg, *tile), F32),
            pltpu.VMEM((nx, ny, td, *tile), F32),
            pltpu.VMEM((ny, nx, tg, *tile), F32),
            pltpu.VMEM((nx, ny, td, *tile), F32),
            pltpu.VMEM((ny, nx, tg, *tile), F32),
            pltpu.VMEM((nx, ny, td, *tile), F32),
            pltpu.VMEM((nx, tg, *tile), F32),
            pltpu.VMEM((ny, td, *tile), F32),
            pltpu.VMEM((nx, tg, *tile), F32),
            pltpu.VMEM((ny, td, *tile), F32),
            pltpu.VMEM((nz, q, *tile), F32),
            pltpu.VMEM((nz, q, *tile), F32),
            pltpu.VMEM((nz, q, *tile), F32),
            dma((4, m)), dma((4, m)), dma((3, nx)), dma((3, nx)), dma((4, ny)), dma((4, ny)), dma((2, nz)), dma((2, nz)),
            dma((2, 2)), dma((2, 2)),
        ],
        compiler_params=pltpu.CompilerParams(collective_id=1, has_side_effects=True),
        name="reduce_all",
    )(gp, dp, e)


def factor_block(blk):
    lane = lax.broadcasted_iota(jnp.int32, (8, 128), 1)
    sub = lax.broadcasted_iota(jnp.int32, (8, 128), 0)
    n = list(blk)
    dv = [None] * 16
    def lb(x, c):
        return jnp.broadcast_to(x[:, c:c + 1], (8, 128))
    def sb(x, k):
        return jnp.broadcast_to(x[k:k + 1, :], (8, 128))
    for p in range(16):
        base = 8 * p
        t = [lb(n[p], base + k) for k in range(8)]
        mult = {}
        rows = []
        cur = n[p]
        dvp = None
        for k in range(8):
            rec = 1.0 / sb(t[k], k)
            low = jnp.where(sub > k, t[k], 0.0)
            at = lane == base + k
            r = sb(cur, k)
            sr = jnp.where(at, rec, r * rec)
            rows.append(sr if k == 7 else jnp.where((lane > base + k) & (lane < base + 8), 0.0, sr))
            dvp = rec if dvp is None else jnp.where(sub == k, rec, dvp)
            for q in range(k + 1, 8):
                m = sb(t[q], k) * rec
                mult[k, q] = m
                t[q] = t[q] - low * m
            if k < 7:
                cur = jnp.where(at & (sub > k), 0.0, cur) - low * sr
        dv[p] = dvp
        n[p] = cur
        inp = (lane >= base) & (lane < base + 8)
        for i in range(p + 1, 16):
            x = [lb(n[i], base + k) for k in range(8)]
            acc = jnp.where(inp, 0.0, n[i])
            for k in range(8):
                for q in range(k + 1, 8):
                    x[q] = x[q] - x[k] * mult[k, q]
                acc = acc - x[k] * rows[k]
            n[i] = acc
    low = []
    for i in range(16):
        r = sub + 8 * i
        low.append(jnp.where(lane < r, n[i], jnp.where(lane == r, 1.0, 0.0)))
    return low, dv

def mm(a, b, ta=False):
    dn = (((0,), (0,)), ((), ())) if ta else (((1,), (0,)), ((), ()))
    return lax.dot_general(a, b, dn, precision=HI, preferred_element_type=F32)


def solve_kernel(alpha, g_ref, d_ref, out_ref, a, bb, li, w, u):
    nb = out_ref.shape[0]
    n = nb * 128
    x = lax.axis_index("mem")
    r = lax.broadcasted_iota(jnp.int32, (128, 128), 0)
    c = lax.broadcasted_iota(jnp.int32, (128, 128), 1)
    for i in range(nb):
        for j in range(i, nb):
            blk = g_ref[pl.ds(16 * i, 16), j].reshape(128, 128)
            a[i, j] = blk + jnp.where(r == c, alpha, 0.0) if i == j else blk
    unit = jnp.where(r == c, alpha * math.sqrt(n - 1.0), 0.0)
    for i in range(nb):
        bb[i] = d_ref[pl.ds(16 * i, 16)].reshape(128, 128) + jnp.where(x == i, unit, 0.0)

    def step(b, _):
        low, dv = factor_block([a[b, b, pl.ds(8 * i, 8), :] for i in range(16)])
        for i in range(16):
            li[b, pl.ds(8 * i, 8), :] = low[i]
            u[pl.ds(8 * i, 8), :] = low[i] * dv[i]
        for s in range(nb):

            @pl.when(b == s)
            def _():
                cols = [a[s, j] for j in range(s + 1, nb)] + [bb[s]]
                us = [mm(li[s], v) for v in cols]
                ws = [mm(u[...], v) for v in cols]
                for t, j in enumerate(range(s + 1, nb)):
                    w[s, j] = ws[t]
                w[s, nb] = ws[-1]
                for t, i in enumerate(range(s + 1, nb)):
                    for q, j in enumerate(range(s + 1, nb)):
                        if j >= i:
                            a[i, j] = a[i, j] - mm(us[t], ws[q], True)
                    bb[i] = bb[i] - mm(us[t], ws[-1], True)

        return 0

    lax.fori_loop(0, nb, step, 0)
    xs = [None] * nb
    for s in reversed(range(nb)):
        acc = w[s, nb]
        for j in range(s + 1, nb):
            acc = acc - mm(w[s, j], xs[j])
        xs[s] = mm(li[s], acc, True)
    tot = sum(jnp.sum(v, axis=0, keepdims=True) for v in xs) * (1.0 / n)
    for s in range(nb):
        out_ref[lax.rem(x + nb - s, nb)] = (xs[s] - tot) * (1.0 / math.sqrt(n - 1.0)) + 1.0 / n


def solve(g, d, alpha):
    nb = g.shape[1]
    block = (128, 128)
    return pl.pallas_call(
        functools.partial(solve_kernel, alpha),
        out_shape=jax.ShapeDtypeStruct((nb, *block), F32),
        in_specs=[VM, VM],
        out_specs=VM,
        scratch_shapes=[
            pltpu.VMEM((nb, nb, *block), F32),
            pltpu.VMEM((nb, *block), F32),
            pltpu.VMEM((nb, *block), F32),
            pltpu.VMEM((nb, nb + 1, *block), F32),
            pltpu.VMEM(block, F32),
        ],
        cost_estimate=pl.CostEstimate(flops=20_000_000_000, bytes_accessed=60_000_000, transcendentals=0),
        name="factor_and_solve",
    )(g, d)


def update_kernel(u_ref, e_ref, l_ref, r_ref, o0_ref, o1_ref, out_ref):
    out_ref[...] = (
        mm(u_ref[0], e_ref[...], True)
        + mm(u_ref[1], l_ref[...].reshape(e_ref.shape), True)
        + mm(u_ref[3], r_ref[...].reshape(e_ref.shape), True)
        + mm(u_ref[2], jnp.concatenate([o0_ref[...], o1_ref[...]], axis=0), True)
    )


def update(u, e, left, right, o0, o1):
    rows, width = e.shape
    t = 512
    return pl.pallas_call(
        update_kernel,
        grid=(width // t,),
        out_shape=jax.ShapeDtypeStruct(e.shape, F32),
        in_specs=[
            pl.BlockSpec(u.shape, lambda i: (0, 0, 0)),
            pl.BlockSpec((rows, t), lambda i: (0, i)),
            pl.BlockSpec((2, rows // 2, t), lambda i: (0, 0, i)),
            pl.BlockSpec((2, rows // 2, t), lambda i: (0, 0, i)),
            pl.BlockSpec((rows // 2, t), lambda i: (0, i)),
            pl.BlockSpec((rows // 2, t), lambda i: (0, i)),
        ],
        out_specs=pl.BlockSpec((rows, t), lambda i: (0, i)),
        name="update",
    )(u, e, left, right, o0, o1)


def shards(ensemble, observed, obs_sigma, obs_index, member_seeds):
    alpha = PLAN[SECTION]
    nx, ny, nz = (lax.axis_size(a) for a in ("mem", "cells_1", "cells_0"))
    own = ensemble.shape[0]
    value = ensemble[:, obs_index]
    predicted = jnp.tanh(value) + 0.5 * value
    seeds = jnp.broadcast_to(member_seeds.astype(F32)[None, :], (8, own))
    pred, all_seeds = exchange(predicted, seeds, nx)
    gp, dp = local_products(pred, all_seeds, observed[None, :], obs_sigma[None, :], nx, alpha)
    tg, td = 256 // (2 * ny * nx), 64 // (2 * ny)
    gp = gp.reshape(2, ny, nx, tg, 8, 128)
    dp = dp.reshape(2, nx, ny, td, 8, 128)
    g, d, left, right = reduce_all(gp, dp, ensemble, nx, ny, nz)
    o0 = lax.ppermute(left[0], "mem", [(i, (i + 1) % nx) for i in range(nx)])
    o1 = lax.ppermute(right[1], "mem", [(i, (i - 1) % nx) for i in range(nx)])
    u = solve(g.reshape(64, 4, 8, 128), d.reshape(64, 8, 128), alpha)
    return update(u, ensemble, left, right, o0, o1)


def solution(mesh):
    finer = Mesh(mesh.devices.reshape(16, 4, 2, mesh.shape["mem"]), AXES)
    placed = (P("mem", CELLS), P(CELLS), P(CELLS), P(CELLS), P("mem"))
    return jax.shard_map(shards, mesh=finer, in_specs=placed, out_specs=P("mem", CELLS), check_vma=False)
```

```python
import functools
import math

import jax
import jax.numpy as jnp
from jax import lax
from jax.experimental import pallas as pl
from jax.experimental.pallas import tpu as pltpu
from jax.sharding import Mesh
from jax.sharding import PartitionSpec as P

SECTION = 1
CELLS = ("cells_0", "cells_1", "cells_2")
AXES = ("cells_0", "cells_1", "cells_2", "mem")
PLAN = (28.0 / 3.0, 7.0, 4.0, 2.0)
HI = lax.Precision.HIGHEST
BF = jnp.bfloat16
MESH = pl.DeviceIdType.MESH
VM = pl.BlockSpec(memory_space=pltpu.VMEM)
ANY = pl.BlockSpec(memory_space=pl.ANY)
F32 = jnp.float32


def remote(src, dst, send, recv, where):
    return pltpu.make_async_remote_copy(
        src_ref=src, dst_ref=dst, send_sem=send, recv_sem=recv, device_id=where, device_id_type=MESH
    )


def at_axis(axis, index):
    return {axis: index}


def greet(peers):
    barrier = pltpu.get_barrier_semaphore()
    for peer in peers:
        pl.semaphore_signal(barrier, inc=1, device_id=peer, device_id_type=MESH)
    pl.semaphore_wait(barrier, len(peers))


def order_of(n):
    return sorted(range(1, n), key=lambda d: -min(d, n - d))


def mod_prime(v):
    q = jnp.floor(v.astype(F32) * (1.0 / 65521.0)).astype(jnp.int32)
    r = v - q * 65521
    r = jnp.where(r < 0, r + 65521, r)
    return jnp.where(r >= 65521, r - 65521, r)


def cosine(h):
    h = jnp.minimum(h, 65521 - h)
    v = (65521 - 4 * h).astype(F32) * (math.pi / (2.0 * 65521.0))
    s = v * v
    poly = jnp.full_like(s, -1.0 / 39916800.0)
    for k in (9, 7, 5, 3, 1):
        poly = poly * s + (-1.0) ** ((k - 1) // 2) / math.factorial(k)
    return poly * v


def halves(v):
    high = v.astype(BF)
    return high, (v - high.astype(F32)).astype(BF)


def bdot(a, b, dims=((1,), (0,))):
    return lax.dot_general(a, b, (dims, ((), ())), preferred_element_type=F32)


def observe_kernel(nx, alpha, e_ref, i_ref, s_ref, o_ref, n_ref, parts, hot, ready, seeds, send, recv):
    x = lax.axis_index("mem")
    rows, cells = e_ref.shape
    width = i_ref.shape[1] // nx
    barrier = pltpu.get_barrier_semaphore()
    for d in range(1, nx):
        pl.semaphore_signal(barrier, inc=1, device_id={"mem": lax.rem(x + d, nx)}, device_id_type=MESH)
    step = 512

    def split(k, _):
        cols = pl.ds(pl.multiple_of(k * step, step), step)
        v = e_ref[:, cols]
        high, rest = halves(v)
        parts[pl.ds(0, rows), cols] = high
        parts[pl.ds(rows, rows), cols] = rest
        parts[pl.ds(2 * rows, rows), cols] = (v - high.astype(F32) - rest.astype(F32)).astype(BF)
        return 0

    lax.fori_loop(0, cells // step, split, 0)
    lanes = 256
    copies = []
    for d in order_of(nx) + [0]:
        to = lax.rem(x + d, nx)

        def some(h, _):
            index = i_ref[:, pl.ds(pl.multiple_of(to * width + h * lanes, lanes), lanes)]

            def fill(k, _):
                at = pl.multiple_of(k * step, step)
                cell = lax.broadcasted_iota(jnp.int32, (step, lanes), 0) + at
                hot[pl.ds(at, step), :] = jnp.where(cell == index, 1.0, 0.0).astype(BF)
                return 0

            lax.fori_loop(0, cells // step, fill, 0)
            got = bdot(parts[...], hot[...])
            value = got[:rows] + got[rows : 2 * rows] + got[2 * rows :]
            ready[d, :, pl.ds(pl.multiple_of(h * lanes, lanes), lanes)] = jnp.tanh(value) + 0.5 * value
            return 0

        lax.fori_loop(0, width // lanes, some, 0)
        mine = pl.ds(pl.multiple_of(x * rows, rows), rows)
        if not copies:
            pl.semaphore_wait(barrier, nx - 1)
            for k in range(1, nx):
                there = {"mem": lax.rem(x + k, nx)}
                copies.append(remote(s_ref, seeds.at[x], send.at[1, k], recv.at[1, k], there))
                copies[-1].start()
        if d:
            copies.append(remote(ready.at[d], o_ref.at[mine, :], send.at[0, d], recv.at[0, d], {"mem": to}))
            copies[-1].start()
        else:
            o_ref[mine, :] = ready[0]
    seeds[x] = s_ref[...]
    for c in copies[: nx - 1]:
        c.wait_recv()
    base = lax.axis_index(CELLS) * i_ref.shape[1] + x * width
    where = mod_prime(lax.broadcasted_iota(jnp.int32, (1, width), 1) + base)

    def noise(b, _):
        at = pl.ds(pl.multiple_of(b * rows, rows), rows)
        seed = jnp.broadcast_to(seeds[b, 0:1, :], (rows, rows)).T.astype(jnp.int32)
        first = mod_prime(seed * 389)
        second = seed - 997 * jnp.floor((seed.astype(F32) + 0.5) * (1.0 / 997.0)).astype(jnp.int32) + 1
        for c in range(width // 128):
            cols = slice(128 * c, 128 * c + 128)
            n_ref[at, cols] = cosine(mod_prime(first + where[:, cols] * second)) * math.sqrt(2.0 * alpha)
        return 0

    lax.fori_loop(0, nx, noise, 0)
    for c in copies[nx - 1 :]:
        c.wait_recv()
    for c in copies:
        c.wait_send()


def observe(e, index, seeds, nx, alpha):
    rows, cells = e.shape
    width = index.shape[1] // nx
    whole = jax.ShapeDtypeStruct((rows * nx, width), F32)
    return pl.pallas_call(
        functools.partial(observe_kernel, nx, alpha),
        out_shape=(whole, whole),
        in_specs=[VM, VM, VM],
        out_specs=(VM, VM),
        scratch_shapes=[
            pltpu.VMEM((3 * rows, cells), BF),
            pltpu.VMEM((cells, 256), BF),
            pltpu.VMEM((nx, rows, width), F32),
            pltpu.VMEM((nx, 8, rows), F32),
            pltpu.SemaphoreType.DMA((2, nx)),
            pltpu.SemaphoreType.DMA((2, nx)),
        ],
        compiler_params=pltpu.CompilerParams(collective_id=0, has_side_effects=True),
        name="observe",
    )(e, index, seeds)


def product_fills(p_ref, n_ref, ob_ref, sg_ref, gp, dp, sh, sl, mh, ml):
    members, width = p_ref.shape
    blocks = members // 128

    def prepare():
        mean = jnp.sum(p_ref[...], axis=0, keepdims=True) * (1.0 / members)
        part = pl.ds(pl.multiple_of(lax.axis_index("mem") * width, width), width)
        inv = 1.0 / sg_ref[:, part]
        scale = inv * (1.0 / math.sqrt(members - 1.0))
        shift = (ob_ref[:, part] - mean) * inv

        def block(b, _):
            rows = pl.ds(pl.multiple_of(b * 64, 64), 64)
            sh[rows, :], sl[rows, :] = halves((p_ref[rows, :] - mean) * scale)
            mh[rows, :], ml[rows, :] = halves(n_ref[rows, :] + shift)
            return 0

        lax.fori_loop(0, members // 64, block, 0)

    both = ((1,), (1,))

    def fill_d():
        def block(b, _):
            rows = pl.ds(pl.multiple_of(b * 128, 128), 128)
            within = pl.ds(pl.multiple_of(lax.rem(b, 2) * 16, 16), 16)
            d = bdot(sh[rows, :], mh[...], both) + bdot(sh[rows, :], ml[...], both) + bdot(sl[rows, :], mh[...], both)
            for c in range(blocks):
                dp[b // 2, c, within] = d[:, 128 * c : 128 * c + 128].reshape(16, 8, 128)
            return 0

        lax.fori_loop(0, blocks, block, 0)

    def fill_g():
        at = 0
        for b in range(blocks):
            rows, rest = pl.ds(128 * b, 128), pl.ds(128 * b, members - 128 * b)
            g = (
                bdot(sh[rows, :], sh[rest, :], both)
                + bdot(sl[rows, :], sh[rest, :], both)
                + bdot(sh[rows, :], sl[rest, :], both)
                + bdot(sl[rows, :], sl[rest, :], both)
            )
            for c in range(blocks - b):
                gp[pl.ds(at, 16)] = g[:, 128 * c : 128 * c + 128].reshape(16, 8, 128)
                at += 16

    return prepare, fill_d, fill_g


def reduce_kernel(n, fills, n_in, *refs):
    nx, ny, nz = n
    (e_ref, go, do, left, right, opp, gp, dp, rg0, rd0, sg0, sd0, rg1, rd1, sg1, sd1, rg2, rd2, zs, rz, zg,
     cs, cr, xs, xr, ys, yr, zss, zsr, es, er) = refs[n_in : n_in + 31]
    prepare, fill_d, fill_g = fills(*refs[:n_in], gp, dp, *refs[n_in + 31 :])
    z, y, c, x = (lax.axis_index(a) for a in AXES)
    oc = 1 - c

    def xat(d):
        return lax.rem(x + d, nx)

    def yat(d):
        return lax.rem(y + d, ny)

    def zat(d):
        return lax.rem(z + d, nz)

    core = {"cells_2": oc}
    peers = (
        [{"cells_0": zat(d)} for d in range(1, nz)]
        + [{"mem": xat(d)} for d in range(1, nx)]
        + [{"cells_1": yat(d)} for d in range(1, ny)]
        + [core]
    )
    barrier = pltpu.get_barrier_semaphore()
    for peer in peers:
        pl.semaphore_signal(barrier, inc=1, device_id=peer, device_id_type=MESH)
    ox, oy, oz = order_of(nx) + [0], order_of(ny) + [0], order_of(nz)
    sent = []

    def start(copy):
        copy.start()
        sent.append(copy)
        return copy

    prepare()
    fill_d()
    td, tg = rd2.shape[1], rg2.shape[1]
    q = zs.shape[0] // nz

    def g_of(core_, yq):
        return pl.ds((core_ * ny + yq) * nx * tg, nx * tg)

    pl.semaphore_wait(barrier, len(peers))
    c0d, c0g = {}, {}
    for d in ox:
        c0d[d] = start(remote(dp.at[oc, xat(d)], rd0.at[xat(d)], cs.at[0, d], cr.at[0, d], core))
    fill_g()
    for d in oy:
        c0g[d] = start(remote(gp.at[g_of(oc, yat(d))], rg0.at[yat(d)], cs.at[1, d], cr.at[1, d], core))
    d1, g1 = {}, {}
    for d in ox:
        c0d[d].wait_recv()
        sd0[xat(d)] = dp[c, xat(d)] + rd0[xat(d)]
        if d:
            d1[d] = start(remote(sd0.at[xat(d)], rd1.at[d], xs.at[0, d], xr.at[0, d], {"mem": xat(d)}))
    for d in oy:
        c0g[d].wait_recv()
        sg0[yat(d)] = gp[g_of(c, yat(d))] + rg0[yat(d)]
        if d:
            g1[d] = start(remote(sg0.at[yat(d)], rg1.at[d], ys.at[0, d], yr.at[0, d], {"cells_1": yat(d)}))
    d2, g2 = {}, {}
    for d in oy[:-1]:
        g1[d].wait_recv()
    for d in ox:
        piece = pl.ds(xat(d) * tg, tg)
        total = sg0[y, piece]
        for k in range(1, ny):
            total = total + rg1[k, piece]
        sg1[xat(d)] = total
        if d:
            g2[d] = start(remote(sg1.at[xat(d)], rg2.at[d], xs.at[1, d], xr.at[1, d], {"mem": xat(d)}))
    for d in ox[:-1]:
        d1[d].wait_recv()
    for d in oy:
        piece = pl.ds(yat(d) * td, td)
        total = sd0[x, piece]
        for k in range(1, nx):
            total = total + rd1[k, piece]
        sd1[yat(d)] = total
        if d:
            d2[d] = start(remote(sd1.at[yat(d)], rd2.at[d], ys.at[1, d], yr.at[1, d], {"cells_1": yat(d)}))
    half = e_ref.shape[0] // 2
    eo = {}

    def ensemble(h):
        part = e_ref.at[pl.ds(h * half, half), :]
        eo[0, h] = start(remote(part, left.at[h], es.at[0, h], er.at[0, h], {"mem": xat(1)}))
        other = e_ref.at[pl.ds((1 - h) * half, half), :]
        eo[1, h] = start(remote(other, right.at[1 - h], es.at[1, h], er.at[1, h], {"mem": xat(nx - 1)}))

    ensemble(0)
    ensemble(1)
    for t in range(td + tg, nz * q):
        zs[t] = jnp.zeros_like(zs[t])
    for d in ox[:-1]:
        g2[d].wait_recv()
    total = sg1[x]
    for k in range(1, nx):
        total = total + rg2[k]
    zs[pl.ds(td, tg)] = total
    for d in oy[:-1]:
        d2[d].wait_recv()
    total = sd1[y]
    for k in range(1, ny):
        total = total + rd2[k]
    zs[pl.ds(0, td)] = total
    z1 = [
        start(remote(zs.at[pl.ds(zat(d) * q, q)], rz.at[d], zss.at[0, d], zsr.at[0, d], {"cells_0": zat(d)})) for d in oz
    ]
    for w in z1:
        w.wait_recv()
    own = pl.ds(z * q, q)
    total = zs[own]
    for k in range(1, nz):
        total = total + rz[k]
    zg[own] = total
    z2 = [start(remote(zg.at[own], zg.at[own], zss.at[1, d], zsr.at[1, d], {"cells_0": zat(d)})) for d in oz]
    for w in z2:
        w.wait_recv()

    def go_of(yq):
        return pl.ds((c * ny + yq) * nx * tg, nx * tg)

    def do_of(yq):
        return pl.ds((c * ny + yq) * td, td)

    mine = pl.ds(((c * ny + y) * nx + x) * tg, tg)
    go[mine] = zg[pl.ds(td, tg)]
    do[do_of(y)] = zg[pl.ds(0, td)]
    dy, gx, gy = {}, {}, {}
    for d in ox[:-1]:
        gx[d] = start(remote(zg.at[pl.ds(td, tg)], go.at[mine], xs.at[2, d], xr.at[2, d], {"mem": xat(d)}))
    for d in oy[:-1]:
        dy[d] = start(remote(zg.at[pl.ds(0, td)], do.at[do_of(y)], ys.at[2, d], yr.at[2, d], {"cells_1": yat(d)}))
    last = [start(remote(zg.at[pl.ds(0, td)], do.at[do_of(y)], cs.at[2, 0], cr.at[2, 0], core))]
    for d in ox[:-1]:
        gx[d].wait_recv()
    for d in oy[:-1]:
        gy[d] = start(remote(go.at[go_of(y)], go.at[go_of(y)], ys.at[3, d], yr.at[3, d], {"cells_1": yat(d)}))
    last.append(start(remote(go.at[go_of(y)], go.at[go_of(y)], cs.at[3, 0], cr.at[3, 0], core)))
    eo[0, 0].wait_recv()
    eo[1, 0].wait_recv()
    far = [
        start(remote(left.at[0], opp.at[0], es.at[2, 0], er.at[2, 0], {"mem": xat(1)})),
        start(remote(right.at[1], opp.at[1], es.at[2, 1], er.at[2, 1], {"mem": xat(nx - 1)})),
    ]
    for d in sorted(oy[:-1]):
        dy[d].wait_recv()
        frm = do_of(yat(ny - d))
        last.append(start(remote(do.at[frm], do.at[frm], cs.at[2, d], cr.at[2, d], core)))
    for d in reversed(oy[:-1]):
        gy[d].wait_recv()
        frm = go_of(yat(ny - d))
        last.append(start(remote(go.at[frm], go.at[frm], cs.at[3, d], cr.at[3, d], core)))
    for w in last + far + [eo[0, 1], eo[1, 1]]:
        w.wait_recv()
    for w in sent:
        w.wait_send()


def reduce_all(inputs, fills, extra, e, tg, td, nx, ny, nz):
    q = -(-(tg + td) // nz)
    tile = (8, 128)
    m = max(nx, ny)
    half = (2, e.shape[0] // 2, e.shape[1])
    dma = pltpu.SemaphoreType.DMA

    def tiles(*lead):
        return pltpu.VMEM((*lead, *tile), F32)

    return pl.pallas_call(
        functools.partial(reduce_kernel, (nx, ny, nz), fills, len(inputs)),
        out_shape=(
            jax.ShapeDtypeStruct((2 * ny * nx * tg, *tile), F32),
            jax.ShapeDtypeStruct((2 * ny * td, *tile), F32),
            jax.ShapeDtypeStruct(half, F32),
            jax.ShapeDtypeStruct(half, F32),
            jax.ShapeDtypeStruct(half, F32),
        ),
        in_specs=[VM] * len(inputs) + [ANY],
        out_specs=(VM, VM, ANY, ANY, ANY),
        scratch_shapes=[
            tiles(2 * ny * nx * tg),
            tiles(2, nx, ny * td),
            tiles(ny, nx * tg),
            tiles(nx, ny * td),
            tiles(ny, nx * tg),
            tiles(nx, ny * td),
            tiles(ny, nx * tg),
            tiles(nx, ny * td),
            tiles(nx, tg),
            tiles(ny, td),
            tiles(nx, tg),
            tiles(ny, td),
            tiles(nz * q),
            tiles(nz, q),
            tiles(nz * q),
            dma((4, m)), dma((4, m)), dma((3, nx)), dma((3, nx)), dma((4, ny)), dma((4, ny)), dma((2, nz)), dma((2, nz)),
            dma((3, 2)), dma((3, 2)),
            *extra,
        ],
        compiler_params=pltpu.CompilerParams(collective_id=1, has_side_effects=True),
        name="reduce_all",
    )(*inputs, e)


def factor_block(blk):
    lane = lax.broadcasted_iota(jnp.int32, (8, 128), 1)
    sub = lax.broadcasted_iota(jnp.int32, (8, 128), 0)
    n = list(blk)
    dv = [None] * 16
    def lb(x, c):
        return jnp.broadcast_to(x[:, c:c + 1], (8, 128))
    def sb(x, k):
        return jnp.broadcast_to(x[k:k + 1, :], (8, 128))
    for p in range(16):
        base = 8 * p
        t = [lb(n[p], base + k) for k in range(8)]
        mult = {}
        rows = []
        cur = n[p]
        dvp = None
        for k in range(8):
            rec = 1.0 / sb(t[k], k)
            low = jnp.where(sub > k, t[k], 0.0)
            at = lane == base + k
            r = sb(cur, k)
            sr = jnp.where(at, rec, r * rec)
            rows.append(sr if k == 7 else jnp.where((lane > base + k) & (lane < base + 8), 0.0, sr))
            dvp = rec if dvp is None else jnp.where(sub == k, rec, dvp)
            for q in range(k + 1, 8):
                m = sb(t[q], k) * rec
                mult[k, q] = m
                t[q] = t[q] - low * m
            if k < 7:
                cur = jnp.where(at & (sub > k), 0.0, cur) - low * sr
        dv[p] = dvp
        n[p] = cur
        inp = (lane >= base) & (lane < base + 8)
        for i in range(p + 1, 16):
            x = [lb(n[i], base + k) for k in range(8)]
            acc = jnp.where(inp, 0.0, n[i])
            for k in range(8):
                for q in range(k + 1, 8):
                    x[q] = x[q] - x[k] * mult[k, q]
                acc = acc - x[k] * rows[k]
            n[i] = acc
    low = []
    for i in range(16):
        r = sub + 8 * i
        low.append(jnp.where(lane < r, n[i], jnp.where(lane == r, 1.0, 0.0)))
    return low, dv

def mm(a, b, ta=False):
    dn = (((0,), (0,)), ((), ())) if ta else (((1,), (0,)), ((), ()))
    return lax.dot_general(a, b, dn, precision=HI, preferred_element_type=F32)


def solve_kernel(alpha, g_ref, d_ref, out_ref, a, bb, li, w, u):
    nb = out_ref.shape[0]
    n = nb * 128
    first = 0
    x = lax.axis_index("mem")
    r = lax.broadcasted_iota(jnp.int32, (128, 128), 0)
    c = lax.broadcasted_iota(jnp.int32, (128, 128), 1)
    for i in range(nb):
        for j in range(i, nb):
            blk = g_ref[pl.ds(first, 16)].reshape(128, 128)
            first += 16
            a[i, j] = blk + jnp.where(r == c, alpha, 0.0) if i == j else blk
    unit = jnp.where(r == c, alpha * math.sqrt(n - 1.0), 0.0)
    for i in range(nb):
        bb[i] = d_ref[pl.ds(16 * i, 16)].reshape(128, 128) + jnp.where(x == i, unit, 0.0)

    def step(b, _):
        low, dv = factor_block([a[b, b, pl.ds(8 * i, 8), :] for i in range(16)])
        for i in range(16):
            li[b, pl.ds(8 * i, 8), :] = low[i]
            u[pl.ds(8 * i, 8), :] = low[i] * dv[i]
        for s in range(nb):

            @pl.when(b == s)
            def _():
                cols = [a[s, j] for j in range(s + 1, nb)] + [bb[s]]
                us = [mm(li[s], v) for v in cols]
                ws = [mm(u[...], v) for v in cols]
                for t, j in enumerate(range(s + 1, nb)):
                    w[s, j] = ws[t]
                w[s, nb] = ws[-1]
                for t, i in enumerate(range(s + 1, nb)):
                    for q, j in enumerate(range(s + 1, nb)):
                        if j >= i:
                            a[i, j] = a[i, j] - mm(us[t], ws[q], True)
                    bb[i] = bb[i] - mm(us[t], ws[-1], True)

        return 0

    lax.fori_loop(0, nb, step, 0)
    xs = [None] * nb
    for s in reversed(range(nb)):
        acc = w[s, nb]
        for j in range(s + 1, nb):
            acc = acc - mm(w[s, j], xs[j])
        xs[s] = mm(li[s], acc, True)
    tot = sum(jnp.sum(v, axis=0, keepdims=True) for v in xs) * (1.0 / n)
    for s in range(nb):
        out_ref[lax.rem(x + nb - s, nb)] = (xs[s] - tot) * (1.0 / math.sqrt(n - 1.0)) + 1.0 / n


def solve(g, d, alpha):
    nb = d.shape[0] // 16
    block = (128, 128)
    return pl.pallas_call(
        functools.partial(solve_kernel, alpha),
        out_shape=jax.ShapeDtypeStruct((nb, *block), F32),
        in_specs=[VM, VM],
        out_specs=VM,
        scratch_shapes=[
            pltpu.VMEM((nb, nb, *block), F32),
            pltpu.VMEM((nb, *block), F32),
            pltpu.VMEM((nb, *block), F32),
            pltpu.VMEM((nb, nb + 1, *block), F32),
            pltpu.VMEM(block, F32),
        ],
        cost_estimate=pl.CostEstimate(flops=20_000_000_000, bytes_accessed=60_000_000, transcendentals=0),
        name="factor_and_solve",
    )(g, d)


def update_kernel(u_ref, e_ref, l_ref, r_ref, o_ref, out_ref):
    total = None
    for d, ref in ((0, e_ref), (1, l_ref), (2, o_ref), (3, r_ref)):
        uh, ul = halves(u_ref[d])
        eh, el = halves(ref[...].reshape(e_ref.shape))
        for a, b in ((uh, eh), (uh, el), (ul, eh)):
            part = bdot(a, b, ((0,), (0,)))
            total = part if total is None else total + part
    out_ref[...] = total


def update(u, e, left, right, opp):
    rows, width = e.shape
    t = 512
    pair = pl.BlockSpec((2, rows // 2, t), lambda i: (0, 0, i))
    return pl.pallas_call(
        update_kernel,
        grid=(width // t,),
        out_shape=jax.ShapeDtypeStruct(e.shape, F32),
        in_specs=[
            pl.BlockSpec(u.shape, lambda i: (0, 0, 0)),
            pl.BlockSpec((rows, t), lambda i: (0, i)),
            pair,
            pair,
            pair,
        ],
        out_specs=pl.BlockSpec((rows, t), lambda i: (0, i)),
        name="update",
    )(u, e, left, right, opp)


def shards(ensemble, observed, obs_sigma, obs_index, member_seeds):
    alpha = PLAN[SECTION]
    nx, ny, nz = (lax.axis_size(a) for a in ("mem", "cells_1", "cells_0"))
    own = ensemble.shape[0]
    blocks = own * nx // 128
    seeds = jnp.broadcast_to(member_seeds.astype(F32)[None, :], (8, own))
    pred, noise = observe(ensemble, obs_index[None, :], seeds, nx, alpha)
    width = pred.shape[1]
    g, d, left, right, opp = reduce_all(
        (pred, noise, observed[None, :], obs_sigma[None, :]),
        product_fills,
        [pltpu.VMEM((own * nx, width), BF)] * 4,
        ensemble,
        16 * blocks * (blocks + 1) // 2 // (2 * ny * nx),
        16 * blocks // (2 * ny),
        nx,
        ny,
        nz,
    )
    return update(solve(g, d, alpha), ensemble, left, right, opp)


def solution(mesh):
    finer = Mesh(mesh.devices.reshape(16, 4, 2, mesh.shape["mem"]), AXES)
    placed = (P("mem", CELLS), P(CELLS), P(CELLS), P(CELLS), P("mem"))
    return jax.shard_map(shards, mesh=finer, in_specs=placed, out_specs=P("mem", CELLS), check_vma=False)
```

```python
import functools
import math

import jax
import jax.numpy as jnp
from jax import lax
from jax.experimental import pallas as pl
from jax.experimental.pallas import tpu as pltpu
from jax.sharding import Mesh
from jax.sharding import PartitionSpec as P

SECTION = 1
CELLS = ("cells_0", "cells_1", "cells_2")
AXES = ("cells_0", "cells_1", "cells_2", "mem")
PLAN = (28.0 / 3.0, 7.0, 4.0, 2.0)
HI = lax.Precision.HIGHEST
BF = jnp.bfloat16
MESH = pl.DeviceIdType.MESH
VM = pl.BlockSpec(memory_space=pltpu.VMEM)
ANY = pl.BlockSpec(memory_space=pl.ANY)
F32 = jnp.float32


def remote(src, dst, send, recv, where):
    return pltpu.make_async_remote_copy(
        src_ref=src, dst_ref=dst, send_sem=send, recv_sem=recv, device_id=where, device_id_type=MESH
    )


def at_axis(axis, index):
    return {axis: index}


def greet(peers):
    barrier = pltpu.get_barrier_semaphore()
    for peer in peers:
        pl.semaphore_signal(barrier, inc=1, device_id=peer, device_id_type=MESH)
    pl.semaphore_wait(barrier, len(peers))


def order_of(n):
    return sorted(range(1, n), key=lambda d: -min(d, n - d))


def mod_prime(v):
    q = jnp.floor(v.astype(F32) * (1.0 / 65521.0)).astype(jnp.int32)
    r = v - q * 65521
    r = jnp.where(r < 0, r + 65521, r)
    return jnp.where(r >= 65521, r - 65521, r)


def cosine(h):
    h = jnp.minimum(h, 65521 - h)
    v = (65521 - 4 * h).astype(F32) * (math.pi / (2.0 * 65521.0))
    s = v * v
    poly = jnp.full_like(s, -1.0 / 39916800.0)
    for k in (9, 7, 5, 3, 1):
        poly = poly * s + (-1.0) ** ((k - 1) // 2) / math.factorial(k)
    return poly * v


def halves(v):
    high = v.astype(BF)
    return high, (v - high.astype(F32)).astype(BF)


def bdot(a, b, dims=((1,), (0,))):
    return lax.dot_general(a, b, (dims, ((), ())), preferred_element_type=F32)


def observe_stages(nx, alpha, e_ref, i_ref, s_ref, o_ref, n_ref, parts, hot, ready, seeds, send, recv):
    x = lax.axis_index("mem")
    rows, cells = e_ref.shape
    width = i_ref.shape[1] // nx
    step, lanes = 512, 256

    def split():
        def block(k, _):
            cols = pl.ds(pl.multiple_of(k * step, step), step)
            v = e_ref[:, cols]
            high, rest = halves(v)
            parts[pl.ds(0, rows), cols] = high
            parts[pl.ds(rows, rows), cols] = rest
            parts[pl.ds(2 * rows, rows), cols] = (v - high.astype(F32) - rest.astype(F32)).astype(BF)
            return 0

        lax.fori_loop(0, cells // step, block, 0)

    def predict(d):
        to = lax.rem(x + d, nx)

        def some(h, _):
            index = i_ref[:, pl.ds(pl.multiple_of(to * width + h * lanes, lanes), lanes)]

            def fill(k, _):
                at = pl.multiple_of(k * step, step)
                cell = lax.broadcasted_iota(jnp.int32, (step, lanes), 0) + at
                hot[pl.ds(at, step), :] = jnp.where(cell == index, 1.0, 0.0).astype(BF)
                return 0

            lax.fori_loop(0, cells // step, fill, 0)
            got = bdot(parts[...], hot[...])
            value = got[:rows] + got[rows : 2 * rows] + got[2 * rows :]
            ready[d, :, pl.ds(pl.multiple_of(h * lanes, lanes), lanes)] = jnp.tanh(value) + 0.5 * value
            return 0

        lax.fori_loop(0, width // lanes, some, 0)

    def copies():
        mine = pl.ds(pl.multiple_of(x * rows, rows), rows)
        s, p = [], []
        for d in order_of(nx):
            there = {"mem": lax.rem(x + d, nx)}
            s.append(remote(s_ref, seeds.at[x], send.at[1, d], recv.at[1, d], there))
            p.append(remote(ready.at[d], o_ref.at[mine, :], send.at[0, d], recv.at[0, d], there))
        return s, p

    def keep():
        o_ref[pl.ds(pl.multiple_of(x * rows, rows), rows), :] = ready[0]
        seeds[x] = s_ref[...]

    def noise():
        base = lax.axis_index(CELLS) * i_ref.shape[1] + x * width
        where = mod_prime(lax.broadcasted_iota(jnp.int32, (1, width), 1) + base)

        def block(b, _):
            at = pl.ds(pl.multiple_of(b * rows, rows), rows)
            seed = jnp.broadcast_to(seeds[b, 0:1, :], (rows, rows)).T.astype(jnp.int32)
            first = mod_prime(seed * 389)
            second = seed - 997 * jnp.floor((seed.astype(F32) + 0.5) * (1.0 / 997.0)).astype(jnp.int32) + 1
            for c in range(width // 128):
                cols = slice(128 * c, 128 * c + 128)
                n_ref[at, cols] = cosine(mod_prime(first + where[:, cols] * second)) * math.sqrt(2.0 * alpha)
            return 0

        lax.fori_loop(0, nx, block, 0)

    return split, predict, copies, keep, noise


def product_fills(p_ref, n_ref, ob_ref, sg_ref, gp, dp, sh, sl, mh, ml):
    members, width = p_ref.shape
    blocks = members // 128

    def prepare():
        mean = jnp.sum(p_ref[...], axis=0, keepdims=True) * (1.0 / members)
        part = pl.ds(pl.multiple_of(lax.axis_index("mem") * width, width), width)
        inv = 1.0 / sg_ref[:, part]
        scale = inv * (1.0 / math.sqrt(members - 1.0))
        shift = (ob_ref[:, part] - mean) * inv

        def block(b, _):
            rows = pl.ds(pl.multiple_of(b * 64, 64), 64)
            sh[rows, :], sl[rows, :] = halves((p_ref[rows, :] - mean) * scale)
            mh[rows, :], ml[rows, :] = halves(n_ref[rows, :] + shift)
            return 0

        lax.fori_loop(0, members // 64, block, 0)

    both = ((1,), (1,))

    def fill_d():
        def block(b, _):
            rows = pl.ds(pl.multiple_of(b * 128, 128), 128)
            within = pl.ds(pl.multiple_of(lax.rem(b, 2) * 16, 16), 16)
            d = bdot(sh[rows, :], mh[...], both) + bdot(sh[rows, :], ml[...], both) + bdot(sl[rows, :], mh[...], both)
            for c in range(blocks):
                dp[b // 2, c, within] = d[:, 128 * c : 128 * c + 128].reshape(16, 8, 128)
            return 0

        lax.fori_loop(0, blocks, block, 0)

    def fill_g():
        at = 0
        for b in range(blocks):
            rows, rest = pl.ds(128 * b, 128), pl.ds(128 * b, members - 128 * b)
            g = (
                bdot(sh[rows, :], sh[rest, :], both)
                + bdot(sl[rows, :], sh[rest, :], both)
                + bdot(sh[rows, :], sl[rest, :], both)
                + bdot(sl[rows, :], sl[rest, :], both)
            )
            for c in range(blocks - b):
                gp[pl.ds(at, 16)] = g[:, 128 * c : 128 * c + 128].reshape(16, 8, 128)
                at += 16

    return prepare, fill_d, fill_g


def all_fills(nx, alpha):
    def fills(e_ref, i_ref, s_ref, ob_ref, sg_ref, gp, dp, pred, noi, parts, hot, ready, seeds, send, recv, *split):
        stages = observe_stages(nx, alpha, e_ref, i_ref, s_ref, pred, noi, parts, hot, ready, seeds, send, recv)
        return stages, product_fills(pred, noi, ob_ref, sg_ref, gp, dp, *split)

    return fills


def all_scratch(rows, cells, width, nx):
    dma = pltpu.SemaphoreType.DMA
    whole = (rows * nx, width)
    return [
        pltpu.VMEM(whole, F32),
        pltpu.VMEM(whole, F32),
        pltpu.VMEM((3 * rows, cells), BF),
        pltpu.VMEM((cells, 256), BF),
        pltpu.VMEM((nx, rows, width), F32),
        pltpu.VMEM((nx, 8, rows), F32),
        dma((2, nx)),
        dma((2, nx)),
    ] + [pltpu.VMEM(whole, BF)] * 4


def reduce_kernel(n, fills, n_in, *refs):
    nx, ny, nz = n
    (e_ref, go, do, left, right, opp, gp, dp, rg0, rd0, sg0, sd0, rg1, rd1, sg1, sd1, rg2, rd2, zs, rz, zg,
     cs, cr, xs, xr, ys, yr, zss, zsr, es, er) = refs[n_in : n_in + 31]
    stages, (prepare, fill_d, fill_g) = fills(*refs[:n_in], gp, dp, *refs[n_in + 31 :])
    z, y, c, x = (lax.axis_index(a) for a in AXES)
    oc = 1 - c

    def xat(d):
        return lax.rem(x + d, nx)

    def yat(d):
        return lax.rem(y + d, ny)

    def zat(d):
        return lax.rem(z + d, nz)

    core = {"cells_2": oc}
    peers = (
        [{"cells_0": zat(d)} for d in range(1, nz)]
        + [{"mem": xat(d)} for d in range(1, nx)]
        + [{"cells_1": yat(d)} for d in range(1, ny)]
        + [core]
    )
    barrier = pltpu.get_barrier_semaphore()
    for peer in peers:
        pl.semaphore_signal(barrier, inc=1, device_id=peer, device_id_type=MESH)
    ox, oy, oz = order_of(nx) + [0], order_of(ny) + [0], order_of(nz)
    sent = []

    def start(copy):
        copy.start()
        sent.append(copy)
        return copy

    td, tg = rd2.shape[1], rg2.shape[1]
    q = zs.shape[0] // nz

    def g_of(core_, yq):
        return pl.ds((core_ * ny + yq) * nx * tg, nx * tg)

    half = e_ref.shape[0] // 2
    eo = {}

    def ensemble(h):
        part = e_ref.at[pl.ds(h * half, half), :]
        eo[0, h] = start(remote(part, left.at[h], es.at[0, h], er.at[0, h], {"mem": xat(1)}))
        other = e_ref.at[pl.ds((1 - h) * half, half), :]
        eo[1, h] = start(remote(other, right.at[1 - h], es.at[1, h], er.at[1, h], {"mem": xat(nx - 1)}))

    split, predict, copies, keep, noise = stages
    split()
    for d in ox[:-1]:
        predict(d)
    of_seeds, of_pred = copies()
    pl.semaphore_wait(barrier, len(peers))
    for w in of_seeds + of_pred:
        start(w)
    ensemble(0)
    predict(0)
    keep()
    for w in of_seeds:
        w.wait_recv()
    noise()
    for w in of_pred:
        w.wait_recv()
    prepare()
    fill_d()
    c0d, c0g = {}, {}
    for d in ox:
        c0d[d] = start(remote(dp.at[oc, xat(d)], rd0.at[xat(d)], cs.at[0, d], cr.at[0, d], core))
    fill_g()
    for d in oy:
        c0g[d] = start(remote(gp.at[g_of(oc, yat(d))], rg0.at[yat(d)], cs.at[1, d], cr.at[1, d], core))
    d1, g1 = {}, {}
    for d in ox:
        c0d[d].wait_recv()
        sd0[xat(d)] = dp[c, xat(d)] + rd0[xat(d)]
        if d:
            d1[d] = start(remote(sd0.at[xat(d)], rd1.at[d], xs.at[0, d], xr.at[0, d], {"mem": xat(d)}))
    for d in oy:
        c0g[d].wait_recv()
        sg0[yat(d)] = gp[g_of(c, yat(d))] + rg0[yat(d)]
        if d:
            g1[d] = start(remote(sg0.at[yat(d)], rg1.at[d], ys.at[0, d], yr.at[0, d], {"cells_1": yat(d)}))
    d2, g2 = {}, {}
    for d in oy[:-1]:
        g1[d].wait_recv()
    for d in ox:
        piece = pl.ds(xat(d) * tg, tg)
        total = sg0[y, piece]
        for k in range(1, ny):
            total = total + rg1[k, piece]
        sg1[xat(d)] = total
        if d:
            g2[d] = start(remote(sg1.at[xat(d)], rg2.at[d], xs.at[1, d], xr.at[1, d], {"mem": xat(d)}))
    for d in ox[:-1]:
        d1[d].wait_recv()
    for d in oy:
        piece = pl.ds(yat(d) * td, td)
        total = sd0[x, piece]
        for k in range(1, nx):
            total = total + rd1[k, piece]
        sd1[yat(d)] = total
        if d:
            d2[d] = start(remote(sd1.at[yat(d)], rd2.at[d], ys.at[1, d], yr.at[1, d], {"cells_1": yat(d)}))
    ensemble(1)
    for t in range(td + tg, nz * q):
        zs[t] = jnp.zeros_like(zs[t])
    for d in ox[:-1]:
        g2[d].wait_recv()
    total = sg1[x]
    for k in range(1, nx):
        total = total + rg2[k]
    zs[pl.ds(td, tg)] = total
    for d in oy[:-1]:
        d2[d].wait_recv()
    total = sd1[y]
    for k in range(1, ny):
        total = total + rd2[k]
    zs[pl.ds(0, td)] = total
    z1 = [
        start(remote(zs.at[pl.ds(zat(d) * q, q)], rz.at[d], zss.at[0, d], zsr.at[0, d], {"cells_0": zat(d)})) for d in oz
    ]
    for w in z1:
        w.wait_recv()
    own = pl.ds(z * q, q)
    total = zs[own]
    for k in range(1, nz):
        total = total + rz[k]
    zg[own] = total
    z2 = [start(remote(zg.at[own], zg.at[own], zss.at[1, d], zsr.at[1, d], {"cells_0": zat(d)})) for d in oz]
    for w in z2:
        w.wait_recv()

    def go_of(yq):
        return pl.ds((c * ny + yq) * nx * tg, nx * tg)

    def do_of(yq):
        return pl.ds((c * ny + yq) * td, td)

    mine = pl.ds(((c * ny + y) * nx + x) * tg, tg)
    go[mine] = zg[pl.ds(td, tg)]
    do[do_of(y)] = zg[pl.ds(0, td)]
    dy, gx, gy = {}, {}, {}
    for d in ox[:-1]:
        gx[d] = start(remote(zg.at[pl.ds(td, tg)], go.at[mine], xs.at[2, d], xr.at[2, d], {"mem": xat(d)}))
    for d in oy[:-1]:
        dy[d] = start(remote(zg.at[pl.ds(0, td)], do.at[do_of(y)], ys.at[2, d], yr.at[2, d], {"cells_1": yat(d)}))
    last = [start(remote(zg.at[pl.ds(0, td)], do.at[do_of(y)], cs.at[2, 0], cr.at[2, 0], core))]
    for d in ox[:-1]:
        gx[d].wait_recv()
    for d in oy[:-1]:
        gy[d] = start(remote(go.at[go_of(y)], go.at[go_of(y)], ys.at[3, d], yr.at[3, d], {"cells_1": yat(d)}))
    last.append(start(remote(go.at[go_of(y)], go.at[go_of(y)], cs.at[3, 0], cr.at[3, 0], core)))
    eo[0, 0].wait_recv()
    eo[1, 0].wait_recv()
    far = [
        start(remote(left.at[0], opp.at[0], es.at[2, 0], er.at[2, 0], {"mem": xat(1)})),
        start(remote(right.at[1], opp.at[1], es.at[2, 1], er.at[2, 1], {"mem": xat(nx - 1)})),
    ]
    for d in sorted(oy[:-1]):
        dy[d].wait_recv()
        frm = do_of(yat(ny - d))
        last.append(start(remote(do.at[frm], do.at[frm], cs.at[2, d], cr.at[2, d], core)))
    for d in reversed(oy[:-1]):
        gy[d].wait_recv()
        frm = go_of(yat(ny - d))
        last.append(start(remote(go.at[frm], go.at[frm], cs.at[3, d], cr.at[3, d], core)))
    for w in last + far + [eo[0, 1], eo[1, 1]]:
        w.wait_recv()
    for w in sent:
        w.wait_send()


def reduce_all(inputs, fills, extra, e, tg, td, nx, ny, nz):
    q = -(-(tg + td) // nz)
    tile = (8, 128)
    m = max(nx, ny)
    half = (2, e.shape[0] // 2, e.shape[1])
    dma = pltpu.SemaphoreType.DMA

    def tiles(*lead):
        return pltpu.VMEM((*lead, *tile), F32)

    return pl.pallas_call(
        functools.partial(reduce_kernel, (nx, ny, nz), fills, len(inputs)),
        out_shape=(
            jax.ShapeDtypeStruct((2 * ny * nx * tg, *tile), F32),
            jax.ShapeDtypeStruct((2 * ny * td, *tile), F32),
            jax.ShapeDtypeStruct(half, F32),
            jax.ShapeDtypeStruct(half, F32),
            jax.ShapeDtypeStruct(half, F32),
        ),
        in_specs=[VM] * len(inputs) + [ANY],
        out_specs=(VM, VM, ANY, ANY, ANY),
        scratch_shapes=[
            tiles(2 * ny * nx * tg),
            tiles(2, nx, ny * td),
            tiles(ny, nx * tg),
            tiles(nx, ny * td),
            tiles(ny, nx * tg),
            tiles(nx, ny * td),
            tiles(ny, nx * tg),
            tiles(nx, ny * td),
            tiles(nx, tg),
            tiles(ny, td),
            tiles(nx, tg),
            tiles(ny, td),
            tiles(nz * q),
            tiles(nz, q),
            tiles(nz * q),
            dma((4, m)), dma((4, m)), dma((3, nx)), dma((3, nx)), dma((4, ny)), dma((4, ny)), dma((2, nz)), dma((2, nz)),
            dma((3, 2)), dma((3, 2)),
            *extra,
        ],
        compiler_params=pltpu.CompilerParams(collective_id=1, has_side_effects=True),
        name="reduce_all",
    )(*inputs, e)


def factor_block(n_ref, low_ref, solved_ref, zero, span=4):
    lane = lax.broadcasted_iota(jnp.int32, (8, 128), 1)
    sub = lax.broadcasted_iota(jnp.int32, (8, 128), 0)

    def lb(v, c):
        return jnp.broadcast_to(v[:, c : c + 1], (8, 128))

    def sb(v, k):
        return jnp.broadcast_to(v[k : k + 1, :], (8, 128))

    for first in range(0, 16, span):
        end = 8 * (first + span)
        n = {i: n_ref[pl.ds(8 * i, 8), :] for i in range(first, first + span)}
        before, after = [], []
        for p in range(first, first + span):
            base = 8 * p
            cur = n[p]
            before.append(jnp.where(lane >= end, cur, 0.0))
            low_ref[pl.ds(base, 8), :] = jnp.where(lane < base, cur, jnp.where(lane == base + sub, 1.0, 0.0))
            t = [lb(cur, base + k) + zero for k in range(8)]
            for k in range(0, 8, 2):
                t0, t1 = t[k], t[k + 1]
                aa, ab, bb = sb(t0, k), sb(t1, k), sb(t1, k + 1)
                rec = 1.0 / (aa * bb - ab * ab)
                pair = (sub == k) | (sub == k + 1)
                top = sub == k
                x0, x1 = jnp.where(pair, 0.0, t0), jnp.where(pair, 0.0, t1)
                s0, s1 = lane == base + k, lane == base + k + 1
                r0 = jnp.where(s0, 1.0, jnp.where(s1, 0.0, sb(cur, k)))
                r1 = jnp.where(s1, 1.0, jnp.where(s0, 0.0, sb(cur, k + 1)))
                n0, n1 = bb * r0 - ab * r1, aa * r1 - ab * r0
                cur = jnp.where(pair, 0.0, jnp.where(s0 | s1, 0.0, cur)) - jnp.where(
                    pair, -jnp.where(top, n0, n1), x0 * n0 + x1 * n1
                ) * rec
                for q in range(k + 2, 8):
                    r0, r1 = sb(t[q], k), sb(t[q], k + 1)
                    n0, n1 = bb * r0 - ab * r1, aa * r1 - ab * r0
                    t[q] = jnp.where(pair, 0.0, t[q]) - jnp.where(pair, -jnp.where(top, n0, n1), x0 * n0 + x1 * n1) * rec
            solved_ref[pl.ds(base, 8), :] = jnp.where(lane < base + 8, cur, 0.0)
            after.append(jnp.where((lane >= base + 8) & (lane < end), 0.0, cur))
            rows = [sb(cur, k) for k in range(8)]
            inside = (lane >= base) & (lane < base + 8)
            for i in range(p + 1, first + span):
                acc = jnp.where(inside, 0.0, n[i])
                for k in range(8):
                    acc = acc - lb(n[i], base + k) * rows[k]
                n[i] = acc
        if end < 128:
            b = jnp.concatenate(before, axis=0)
            f = jnp.concatenate(after, axis=0)
            change = lax.dot_general(b, f, (((0,), (0,)), ((), ())), precision=HI, preferred_element_type=jnp.float32)
            keep = (lane < 8 * first) | (lane >= end)
            for i in range(first + span, 16):
                at = pl.ds(8 * i, 8)
                n_ref[at, :] = jnp.where(keep, n_ref[at, :], 0.0) - change[8 * i : 8 * i + 8]

def mm(a, b, ta=False):
    dn = (((0,), (0,)), ((), ())) if ta else (((1,), (0,)), ((), ()))
    return lax.dot_general(a, b, dn, precision=HI, preferred_element_type=F32)


def solve_kernel(alpha, g_ref, d_ref, out_ref, a, bb, li, w, u, zero):
    zero[...] = jnp.zeros_like(zero)
    nb = out_ref.shape[0]
    n = nb * 128
    first = 0
    x = lax.axis_index("mem")
    r = lax.broadcasted_iota(jnp.int32, (128, 128), 0)
    c = lax.broadcasted_iota(jnp.int32, (128, 128), 1)
    for i in range(nb):
        for j in range(i, nb):
            blk = g_ref[pl.ds(first, 16)].reshape(128, 128)
            first += 16
            a[i, j] = blk + jnp.where(r == c, alpha, 0.0) if i == j else blk
    unit = jnp.where(r == c, alpha * math.sqrt(n - 1.0), 0.0)
    for i in range(nb):
        bb[i] = d_ref[pl.ds(16 * i, 16)].reshape(128, 128) + jnp.where(x == i, unit, 0.0)

    def step(b, _):
        factor_block(a.at[b, b], li.at[b], u, zero[...])
        for s in range(nb):

            @pl.when(b == s)
            def _():
                cols = [a[s, j] for j in range(s + 1, nb)] + [bb[s]]
                us = [mm(li[s], v) for v in cols]
                ws = [mm(u[...], v) for v in cols]
                for t, j in enumerate(range(s + 1, nb)):
                    w[s, j] = ws[t]
                w[s, nb] = ws[-1]
                for t, i in enumerate(range(s + 1, nb)):
                    for q, j in enumerate(range(s + 1, nb)):
                        if j >= i:
                            a[i, j] = a[i, j] - mm(us[t], ws[q], True)
                    bb[i] = bb[i] - mm(us[t], ws[-1], True)

        return 0

    lax.fori_loop(0, nb, step, 0)
    xs = [None] * nb
    for s in reversed(range(nb)):
        acc = w[s, nb]
        for j in range(s + 1, nb):
            acc = acc - mm(w[s, j], xs[j])
        xs[s] = mm(li[s], acc, True)
    tot = sum(jnp.sum(v, axis=0, keepdims=True) for v in xs) * (1.0 / n)
    for s in range(nb):
        out_ref[lax.rem(x + nb - s, nb)] = (xs[s] - tot) * (1.0 / math.sqrt(n - 1.0)) + 1.0 / n


def solve(g, d, alpha):
    nb = d.shape[0] // 16
    block = (128, 128)
    return pl.pallas_call(
        functools.partial(solve_kernel, alpha),
        out_shape=jax.ShapeDtypeStruct((nb, *block), F32),
        in_specs=[VM, VM],
        out_specs=VM,
        scratch_shapes=[
            pltpu.VMEM((nb, nb, *block), F32),
            pltpu.VMEM((nb, *block), F32),
            pltpu.VMEM((nb, *block), F32),
            pltpu.VMEM((nb, nb + 1, *block), F32),
            pltpu.VMEM(block, F32),
            pltpu.VMEM((8, 128), F32),
        ],
        cost_estimate=pl.CostEstimate(flops=20_000_000_000, bytes_accessed=60_000_000, transcendentals=0),
        name="factor_and_solve",
    )(g, d)


def update_kernel(u_ref, e_ref, l_ref, r_ref, o_ref, out_ref):
    total = None
    for d, ref in ((0, e_ref), (1, l_ref), (2, o_ref), (3, r_ref)):
        uh, ul = halves(u_ref[d])
        eh, el = halves(ref[...].reshape(e_ref.shape))
        for a, b in ((uh, eh), (uh, el), (ul, eh)):
            part = bdot(a, b, ((0,), (0,)))
            total = part if total is None else total + part
    out_ref[...] = total


def update(u, e, left, right, opp):
    rows, width = e.shape
    t = 512
    pair = pl.BlockSpec((2, rows // 2, t), lambda i: (0, 0, i))
    return pl.pallas_call(
        update_kernel,
        grid=(width // t,),
        out_shape=jax.ShapeDtypeStruct(e.shape, F32),
        in_specs=[
            pl.BlockSpec(u.shape, lambda i: (0, 0, 0)),
            pl.BlockSpec((rows, t), lambda i: (0, i)),
            pair,
            pair,
            pair,
        ],
        out_specs=pl.BlockSpec((rows, t), lambda i: (0, i)),
        name="update",
    )(u, e, left, right, opp)


def shards(ensemble, observed, obs_sigma, obs_index, member_seeds):
    alpha = PLAN[SECTION]
    nx, ny, nz = (lax.axis_size(a) for a in ("mem", "cells_1", "cells_0"))
    own = ensemble.shape[0]
    blocks = own * nx // 128
    width = obs_index.shape[0] // nx
    seeds = jnp.broadcast_to(member_seeds.astype(F32)[None, :], (8, own))
    g, d, left, right, opp = reduce_all(
        (ensemble, obs_index[None, :], seeds, observed[None, :], obs_sigma[None, :]),
        all_fills(nx, alpha),
        all_scratch(own, ensemble.shape[1], width, nx),
        ensemble,
        16 * blocks * (blocks + 1) // 2 // (2 * ny * nx),
        16 * blocks // (2 * ny),
        nx,
        ny,
        nz,
    )
    return update(solve(g, d, alpha), ensemble, left, right, opp)


def solution(mesh):
    finer = Mesh(mesh.devices.reshape(16, 4, 2, mesh.shape["mem"]), AXES)
    placed = (P("mem", CELLS), P(CELLS), P(CELLS), P(CELLS), P("mem"))
    return jax.shard_map(shards, mesh=finer, in_specs=placed, out_specs=P("mem", CELLS), check_vma=False)
```

```python
import functools
import math

import jax
import jax.numpy as jnp
from jax import lax
from jax.experimental import pallas as pl
from jax.experimental.pallas import tpu as pltpu
from jax.sharding import Mesh
from jax.sharding import PartitionSpec as P

SECTION = 1
CELLS = ("cells_0", "cells_1", "cells_2")
AXES = ("cells_0", "cells_1", "cells_2", "mem")
PLAN = (28.0 / 3.0, 7.0, 4.0, 2.0)
HI = lax.Precision.HIGHEST
BF = jnp.bfloat16
MESH = pl.DeviceIdType.MESH
VM = pl.BlockSpec(memory_space=pltpu.VMEM)
ANY = pl.BlockSpec(memory_space=pl.ANY)
F32 = jnp.float32


def remote(src, dst, send, recv, where):
    return pltpu.make_async_remote_copy(
        src_ref=src, dst_ref=dst, send_sem=send, recv_sem=recv, device_id=where, device_id_type=MESH
    )


def at_axis(axis, index):
    return {axis: index}


def greet(peers):
    barrier = pltpu.get_barrier_semaphore()
    for peer in peers:
        pl.semaphore_signal(barrier, inc=1, device_id=peer, device_id_type=MESH)
    pl.semaphore_wait(barrier, len(peers))


def order_of(n):
    return sorted(range(1, n), key=lambda d: -min(d, n - d))


def mod_prime(v):
    q = jnp.floor(v.astype(F32) * (1.0 / 65521.0)).astype(jnp.int32)
    r = v - q * 65521
    r = jnp.where(r < 0, r + 65521, r)
    return jnp.where(r >= 65521, r - 65521, r)


def cosine(h):
    h = jnp.minimum(h, 65521 - h)
    v = (65521 - 4 * h).astype(F32) * (math.pi / (2.0 * 65521.0))
    s = v * v
    poly = jnp.full_like(s, -1.0 / 39916800.0)
    for k in (9, 7, 5, 3, 1):
        poly = poly * s + (-1.0) ** ((k - 1) // 2) / math.factorial(k)
    return poly * v


def halves(v):
    high = v.astype(BF)
    return high, (v - high.astype(F32)).astype(BF)


def bdot(a, b, dims=((1,), (0,))):
    return lax.dot_general(a, b, (dims, ((), ())), preferred_element_type=F32)


def observe_stages(nx, alpha, e_ref, i_ref, s_ref, o_ref, n_ref, parts, hot, ready, mine_s, seeds, send, recv):
    x = lax.axis_index("mem")
    rows, cells = e_ref.shape
    width = i_ref.shape[1] // nx
    step, lanes = 512, 256

    def split():
        mine_s[...] = jnp.broadcast_to(s_ref[0:1, :].astype(F32), mine_s.shape)

        def block(k, _):
            cols = pl.ds(pl.multiple_of(k * step, step), step)
            v = e_ref[:, cols]
            high, rest = halves(v)
            parts[pl.ds(0, rows), cols] = high
            parts[pl.ds(rows, rows), cols] = rest
            parts[pl.ds(2 * rows, rows), cols] = (v - high.astype(F32) - rest.astype(F32)).astype(BF)
            return 0

        lax.fori_loop(0, cells // step, block, 0)

    def predict(d):
        to = lax.rem(x + d, nx)

        def some(h, _):
            index = i_ref[:, pl.ds(pl.multiple_of(to * width + h * lanes, lanes), lanes)]

            def fill(k, _):
                at = pl.multiple_of(k * step, step)
                cell = lax.broadcasted_iota(jnp.int32, (step, lanes), 0) + at
                hot[pl.ds(at, step), :] = jnp.where(cell == index, 1.0, 0.0).astype(BF)
                return 0

            lax.fori_loop(0, cells // step, fill, 0)
            got = bdot(parts[...], hot[...])
            value = got[:rows] + got[rows : 2 * rows] + got[2 * rows :]
            ready[d, :, pl.ds(pl.multiple_of(h * lanes, lanes), lanes)] = jnp.tanh(value) + 0.5 * value
            return 0

        lax.fori_loop(0, width // lanes, some, 0)

    def copies():
        mine = pl.ds(pl.multiple_of(x * rows, rows), rows)
        s, p = [], []
        for d in order_of(nx):
            there = {"mem": lax.rem(x + d, nx)}
            s.append(remote(mine_s, seeds.at[x], send.at[1, d], recv.at[1, d], there))
            p.append(remote(ready.at[d], o_ref.at[mine, :], send.at[0, d], recv.at[0, d], there))
        return s, p

    def keep():
        o_ref[pl.ds(pl.multiple_of(x * rows, rows), rows), :] = ready[0]
        seeds[x] = mine_s[...]

    def noise():
        base = lax.axis_index(CELLS) * i_ref.shape[1] + x * width
        where = mod_prime(lax.broadcasted_iota(jnp.int32, (1, width), 1) + base)

        def block(b, _):
            at = pl.ds(pl.multiple_of(b * rows, rows), rows)
            seed = jnp.broadcast_to(seeds[b, 0:1, :], (rows, rows)).T.astype(jnp.int32)
            first = mod_prime(seed * 389)
            second = seed - 997 * jnp.floor((seed.astype(F32) + 0.5) * (1.0 / 997.0)).astype(jnp.int32) + 1
            for c in range(width // 128):
                cols = slice(128 * c, 128 * c + 128)
                n_ref[at, cols] = cosine(mod_prime(first + where[:, cols] * second)) * math.sqrt(2.0 * alpha)
            return 0

        lax.fori_loop(0, nx, block, 0)

    return split, predict, copies, keep, noise


def product_fills(p_ref, n_ref, ob_ref, sg_ref, gp, dp, sh, sl, mh, ml):
    members, width = p_ref.shape
    blocks = members // 128

    def prepare():
        mean = jnp.sum(p_ref[...], axis=0, keepdims=True) * (1.0 / members)
        part = pl.ds(pl.multiple_of(lax.axis_index("mem") * width, width), width)
        inv = 1.0 / sg_ref[:, part]
        scale = inv * (1.0 / math.sqrt(members - 1.0))
        shift = (ob_ref[:, part] - mean) * inv

        def block(b, _):
            rows = pl.ds(pl.multiple_of(b * 64, 64), 64)
            sh[rows, :], sl[rows, :] = halves((p_ref[rows, :] - mean) * scale)
            mh[rows, :], ml[rows, :] = halves(n_ref[rows, :] + shift)
            return 0

        lax.fori_loop(0, members // 64, block, 0)

    both = ((1,), (1,))

    def fill_d():
        def block(b, _):
            rows = pl.ds(pl.multiple_of(b * 128, 128), 128)
            within = pl.ds(pl.multiple_of(lax.rem(b, 2) * 16, 16), 16)
            d = bdot(sh[rows, :], mh[...], both) + bdot(sh[rows, :], ml[...], both) + bdot(sl[rows, :], mh[...], both)
            for c in range(blocks):
                dp[b // 2, c, within] = d[:, 128 * c : 128 * c + 128].reshape(16, 8, 128)
            return 0

        lax.fori_loop(0, blocks, block, 0)

    def fill_g():
        at = 0
        for b in range(blocks):
            rows, rest = pl.ds(128 * b, 128), pl.ds(128 * b, members - 128 * b)
            g = (
                bdot(sh[rows, :], sh[rest, :], both)
                + bdot(sl[rows, :], sh[rest, :], both)
                + bdot(sh[rows, :], sl[rest, :], both)
                + bdot(sl[rows, :], sl[rest, :], both)
            )
            for c in range(blocks - b):
                gp[pl.ds(at, 16)] = g[:, 128 * c : 128 * c + 128].reshape(16, 8, 128)
                at += 16

    return prepare, fill_d, fill_g


def all_fills(nx, alpha):
    def fills(e_ref, i_ref, s_ref, ob_ref, sg_ref, gp, dp, pred, noi, parts, hot, ready, mine_s, seeds, send, recv, *split):
        stages = observe_stages(nx, alpha, e_ref, i_ref, s_ref, pred, noi, parts, hot, ready, mine_s, seeds, send, recv)
        return stages, product_fills(pred, noi, ob_ref, sg_ref, gp, dp, *split)

    return fills


def all_scratch(rows, cells, width, nx):
    dma = pltpu.SemaphoreType.DMA
    whole = (rows * nx, width)
    return [
        pltpu.VMEM(whole, F32),
        pltpu.VMEM(whole, F32),
        pltpu.VMEM((3 * rows, cells), BF),
        pltpu.VMEM((cells, 256), BF),
        pltpu.VMEM((nx, rows, width), F32),
        pltpu.VMEM((8, rows), F32),
        pltpu.VMEM((nx, 8, rows), F32),
        dma((2, nx)),
        dma((2, nx)),
    ] + [pltpu.VMEM(whole, BF)] * 4


def reduce_kernel(n, fills, n_in, *refs):
    nx, ny, nz = n
    (e_ref, go, do, left, right, opp, gp, dp, rg0, rd0, sg0, sd0, rg1, rd1, sg1, sd1, rg2, rd2, zs, rz, zg,
     cs, cr, xs, xr, ys, yr, zss, zsr, es, er, heard) = refs[n_in : n_in + 32]
    stages, (prepare, fill_d, fill_g) = fills(*refs[:n_in], gp, dp, *refs[n_in + 32 :])
    z, y, c, x = (lax.axis_index(a) for a in AXES)
    oc = 1 - c

    def xat(d):
        return lax.rem(x + d, nx)

    def yat(d):
        return lax.rem(y + d, ny)

    def zat(d):
        return lax.rem(z + d, nz)

    core = {"cells_2": oc}
    beside = [{"cells_0": zat(d)} for d in sorted({1, nz - 1} - {0})] if nz > 1 else []
    peers = (
        [{"mem": xat(d)} for d in range(1, nx)] + [{"cells_1": yat(d)} for d in range(1, ny)] + [core] + beside
    )
    barrier = pltpu.get_barrier_semaphore()
    for peer in peers:
        pl.semaphore_signal(barrier, inc=1, device_id=peer, device_id_type=MESH)
    rounds = list(range(nz // 2 - 1))

    def spread(count=1):
        for r in rounds[:count]:
            for peer in beside:
                pl.semaphore_signal(heard.at[r], inc=1, device_id=peer, device_id_type=MESH)
            pl.semaphore_wait(heard.at[r], len(beside))
        del rounds[:count]

    ox, oy, oz = order_of(nx) + [0], order_of(ny) + [0], order_of(nz)
    sent = []

    def start(copy):
        copy.start()
        sent.append(copy)
        return copy

    td, tg = rd2.shape[1], rg2.shape[1]
    q = zs.shape[0] // nz

    def g_of(core_, yq):
        return pl.ds((core_ * ny + yq) * nx * tg, nx * tg)

    half = e_ref.shape[0] // 2
    eo = {}

    def ensemble(h):
        part = e_ref.at[pl.ds(h * half, half), :]
        eo[0, h] = start(remote(part, left.at[h], es.at[0, h], er.at[0, h], {"mem": xat(1)}))
        other = e_ref.at[pl.ds((1 - h) * half, half), :]
        eo[1, h] = start(remote(other, right.at[1 - h], es.at[1, h], er.at[1, h], {"mem": xat(nx - 1)}))

    split, predict, copies, keep, noise = stages
    split()
    for d in ox[:-1]:
        predict(d)
    of_seeds, of_pred = copies()
    pl.semaphore_wait(barrier, len(peers))
    for w in of_seeds + of_pred:
        start(w)
    ensemble(0)
    spread()
    predict(0)
    spread()
    keep()
    for w in of_seeds:
        w.wait_recv()
    spread()
    noise()
    spread()
    for w in of_pred:
        w.wait_recv()
        spread()
    prepare()
    spread(nz)
    fill_d()
    c0d, c0g = {}, {}
    for d in ox:
        c0d[d] = start(remote(dp.at[oc, xat(d)], rd0.at[xat(d)], cs.at[0, d], cr.at[0, d], core))
    fill_g()
    for d in oy:
        c0g[d] = start(remote(gp.at[g_of(oc, yat(d))], rg0.at[yat(d)], cs.at[1, d], cr.at[1, d], core))
    d1, g1 = {}, {}
    for d in ox:
        c0d[d].wait_recv()
        sd0[xat(d)] = dp[c, xat(d)] + rd0[xat(d)]
        if d:
            d1[d] = start(remote(sd0.at[xat(d)], rd1.at[d], xs.at[0, d], xr.at[0, d], {"mem": xat(d)}))
    for d in oy:
        c0g[d].wait_recv()
        sg0[yat(d)] = gp[g_of(c, yat(d))] + rg0[yat(d)]
        if d:
            g1[d] = start(remote(sg0.at[yat(d)], rg1.at[d], ys.at[0, d], yr.at[0, d], {"cells_1": yat(d)}))
    d2, g2 = {}, {}
    for d in oy[:-1]:
        g1[d].wait_recv()
    for d in ox:
        piece = pl.ds(xat(d) * tg, tg)
        total = sg0[y, piece]
        for k in range(1, ny):
            total = total + rg1[k, piece]
        sg1[xat(d)] = total
        if d:
            g2[d] = start(remote(sg1.at[xat(d)], rg2.at[d], xs.at[1, d], xr.at[1, d], {"mem": xat(d)}))
    for d in ox[:-1]:
        d1[d].wait_recv()
    for d in oy:
        piece = pl.ds(yat(d) * td, td)
        total = sd0[x, piece]
        for k in range(1, nx):
            total = total + rd1[k, piece]
        sd1[yat(d)] = total
        if d:
            d2[d] = start(remote(sd1.at[yat(d)], rd2.at[d], ys.at[1, d], yr.at[1, d], {"cells_1": yat(d)}))
    ensemble(1)
    for t in range(td + tg, nz * q):
        zs[t] = jnp.zeros_like(zs[t])
    for d in ox[:-1]:
        g2[d].wait_recv()
    total = sg1[x]
    for k in range(1, nx):
        total = total + rg2[k]
    zs[pl.ds(td, tg)] = total
    for d in oy[:-1]:
        d2[d].wait_recv()
    total = sd1[y]
    for k in range(1, ny):
        total = total + rd2[k]
    zs[pl.ds(0, td)] = total
    z1 = [
        start(remote(zs.at[pl.ds(zat(d) * q, q)], rz.at[d], zss.at[0, d], zsr.at[0, d], {"cells_0": zat(d)})) for d in oz
    ]
    for w in z1:
        w.wait_recv()
    own = pl.ds(z * q, q)
    total = zs[own]
    for k in range(1, nz):
        total = total + rz[k]
    zg[own] = total
    z2 = [start(remote(zg.at[own], zg.at[own], zss.at[1, d], zsr.at[1, d], {"cells_0": zat(d)})) for d in oz]
    for w in z2:
        w.wait_recv()

    def go_of(yq):
        return pl.ds((c * ny + yq) * nx * tg, nx * tg)

    def do_of(yq):
        return pl.ds((c * ny + yq) * td, td)

    mine = pl.ds(((c * ny + y) * nx + x) * tg, tg)
    go[mine] = zg[pl.ds(td, tg)]
    do[do_of(y)] = zg[pl.ds(0, td)]
    dy, gx, gy = {}, {}, {}
    for d in ox[:-1]:
        gx[d] = start(remote(zg.at[pl.ds(td, tg)], go.at[mine], xs.at[2, d], xr.at[2, d], {"mem": xat(d)}))
    for d in oy[:-1]:
        dy[d] = start(remote(zg.at[pl.ds(0, td)], do.at[do_of(y)], ys.at[2, d], yr.at[2, d], {"cells_1": yat(d)}))
    last = [start(remote(zg.at[pl.ds(0, td)], do.at[do_of(y)], cs.at[2, 0], cr.at[2, 0], core))]
    for d in ox[:-1]:
        gx[d].wait_recv()
    for d in oy[:-1]:
        gy[d] = start(remote(go.at[go_of(y)], go.at[go_of(y)], ys.at[3, d], yr.at[3, d], {"cells_1": yat(d)}))
    last.append(start(remote(go.at[go_of(y)], go.at[go_of(y)], cs.at[3, 0], cr.at[3, 0], core)))
    eo[0, 0].wait_recv()
    eo[1, 0].wait_recv()
    far = [
        start(remote(left.at[0], opp.at[0], es.at[2, 0], er.at[2, 0], {"mem": xat(1)})),
        start(remote(right.at[1], opp.at[1], es.at[2, 1], er.at[2, 1], {"mem": xat(nx - 1)})),
    ]
    for d in sorted(oy[:-1]):
        dy[d].wait_recv()
        frm = do_of(yat(ny - d))
        last.append(start(remote(do.at[frm], do.at[frm], cs.at[2, d], cr.at[2, d], core)))
    for d in reversed(oy[:-1]):
        gy[d].wait_recv()
        frm = go_of(yat(ny - d))
        last.append(start(remote(go.at[frm], go.at[frm], cs.at[3, d], cr.at[3, d], core)))
    for w in last + far + [eo[0, 1], eo[1, 1]]:
        w.wait_recv()
    for w in sent:
        w.wait_send()


def reduce_all(inputs, fills, extra, e, tg, td, nx, ny, nz):
    q = -(-(tg + td) // nz)
    tile = (8, 128)
    m = max(nx, ny)
    half = (2, e.shape[0] // 2, e.shape[1])
    dma = pltpu.SemaphoreType.DMA

    def tiles(*lead):
        return pltpu.VMEM((*lead, *tile), F32)

    return pl.pallas_call(
        functools.partial(reduce_kernel, (nx, ny, nz), fills, len(inputs)),
        out_shape=(
            jax.ShapeDtypeStruct((2 * ny * nx * tg, *tile), F32),
            jax.ShapeDtypeStruct((2 * ny * td, *tile), F32),
            jax.ShapeDtypeStruct(half, F32),
            jax.ShapeDtypeStruct(half, F32),
            jax.ShapeDtypeStruct(half, F32),
        ),
        in_specs=[VM] * len(inputs) + [ANY],
        out_specs=(VM, VM, ANY, ANY, ANY),
        scratch_shapes=[
            tiles(2 * ny * nx * tg),
            tiles(2, nx, ny * td),
            tiles(ny, nx * tg),
            tiles(nx, ny * td),
            tiles(ny, nx * tg),
            tiles(nx, ny * td),
            tiles(ny, nx * tg),
            tiles(nx, ny * td),
            tiles(nx, tg),
            tiles(ny, td),
            tiles(nx, tg),
            tiles(ny, td),
            tiles(nz * q),
            tiles(nz, q),
            tiles(nz * q),
            dma((4, m)), dma((4, m)), dma((3, nx)), dma((3, nx)), dma((4, ny)), dma((4, ny)), dma((2, nz)), dma((2, nz)),
            dma((3, 2)), dma((3, 2)), pltpu.SemaphoreType.REGULAR((max(nz // 2 - 1, 1),)),
            *extra,
        ],
        compiler_params=pltpu.CompilerParams(collective_id=1, has_side_effects=True),
        name="reduce_all",
    )(*inputs, e)


def factor_block(n_ref, low_ref, solved_ref, zero, span=4):
    lane = lax.broadcasted_iota(jnp.int32, (8, 128), 1)
    sub = lax.broadcasted_iota(jnp.int32, (8, 128), 0)

    def lb(v, c):
        return jnp.broadcast_to(v[:, c : c + 1], (8, 128))

    def sb(v, k):
        return jnp.broadcast_to(v[k : k + 1, :], (8, 128))

    for first in range(0, 16, span):
        end = 8 * (first + span)
        n = {i: n_ref[pl.ds(8 * i, 8), :] for i in range(first, first + span)}
        before, after = [], []
        for p in range(first, first + span):
            base = 8 * p
            cur = n[p]
            before.append(jnp.where(lane >= end, cur, 0.0))
            low_ref[pl.ds(base, 8), :] = jnp.where(lane < base, cur, jnp.where(lane == base + sub, 1.0, 0.0))
            t = [lb(cur, base + k) + zero for k in range(8)]
            for k in range(0, 8, 2):
                t0, t1 = t[k], t[k + 1]
                aa, ab, bb = sb(t0, k), sb(t1, k), sb(t1, k + 1)
                rec = 1.0 / (aa * bb - ab * ab)
                pair = (sub == k) | (sub == k + 1)
                top = sub == k
                x0, x1 = jnp.where(pair, 0.0, t0), jnp.where(pair, 0.0, t1)
                s0, s1 = lane == base + k, lane == base + k + 1
                r0 = jnp.where(s0, 1.0, jnp.where(s1, 0.0, sb(cur, k)))
                r1 = jnp.where(s1, 1.0, jnp.where(s0, 0.0, sb(cur, k + 1)))
                n0, n1 = bb * r0 - ab * r1, aa * r1 - ab * r0
                cur = jnp.where(pair, 0.0, jnp.where(s0 | s1, 0.0, cur)) - jnp.where(
                    pair, -jnp.where(top, n0, n1), x0 * n0 + x1 * n1
                ) * rec
                for q in range(k + 2, 8):
                    r0, r1 = sb(t[q], k), sb(t[q], k + 1)
                    n0, n1 = bb * r0 - ab * r1, aa * r1 - ab * r0
                    t[q] = jnp.where(pair, 0.0, t[q]) - jnp.where(pair, -jnp.where(top, n0, n1), x0 * n0 + x1 * n1) * rec
            solved_ref[pl.ds(base, 8), :] = jnp.where(lane < base + 8, cur, 0.0)
            after.append(jnp.where((lane >= base + 8) & (lane < end), 0.0, cur))
            rows = [sb(cur, k) for k in range(8)]
            inside = (lane >= base) & (lane < base + 8)
            for i in range(p + 1, first + span):
                acc = jnp.where(inside, 0.0, n[i])
                for k in range(8):
                    acc = acc - lb(n[i], base + k) * rows[k]
                n[i] = acc
        if end < 128:
            b = jnp.concatenate(before, axis=0)
            f = jnp.concatenate(after, axis=0)
            change = lax.dot_general(b, f, (((0,), (0,)), ((), ())), precision=HI, preferred_element_type=jnp.float32)
            keep = (lane < 8 * first) | (lane >= end)
            for i in range(first + span, 16):
                at = pl.ds(8 * i, 8)
                n_ref[at, :] = jnp.where(keep, n_ref[at, :], 0.0) - change[8 * i : 8 * i + 8]

def mm(a, b, ta=False):
    dn = (((0,), (0,)), ((), ())) if ta else (((1,), (0,)), ((), ()))
    return lax.dot_general(a, b, dn, precision=HI, preferred_element_type=F32)


def solve_kernel(alpha, g_ref, d_ref, high_ref, low_ref, a, dg, li, u, w, zero):
    nb = dg.shape[0]
    n = nb * 128
    x = lax.axis_index("mem")
    r = lax.broadcasted_iota(jnp.int32, (128, 128), 0)
    c = lax.broadcasted_iota(jnp.int32, (128, 128), 1)
    zero[...] = jnp.zeros_like(zero)
    first = 0
    for i in range(nb):
        for j in range(i, nb):
            blk = g_ref[pl.ds(first, 16)].reshape(128, 128)
            first += 16
            if i == j:
                dg[i] = blk + jnp.where(r == c, alpha, 0.0)
            else:
                a[i, :, pl.ds(128 * j, 128)] = blk
    unit = jnp.where(r == c, alpha * math.sqrt(n - 1.0), 0.0)
    for i in range(nb):
        a[i, :, pl.ds(n, 128)] = d_ref[pl.ds(16 * i, 16)].reshape(128, 128) + jnp.where(x == i, unit, 0.0)

    def step(b, _):
        factor_block(dg.at[b], li.at[b], u, zero[...])
        for s in range(nb):

            @pl.when(b == s)
            def _():
                cols = a[s, :, pl.ds(128 * (s + 1), 128 * (nb - s))]
                us = mm(li[s], cols)
                ws = mm(u[...], cols)
                w[s, :, pl.ds(128 * (s + 1), 128 * (nb - s))] = ws
                for i in range(s + 1, nb):
                    at = 128 * (i - s - 1)
                    change = mm(us[:, at : at + 128], ws[:, at:], True)
                    dg[i] = dg[i] - change[:, :128]
                    rest = pl.ds(128 * (i + 1), 128 * (nb - i))
                    a[i, :, rest] = a[i, :, rest] - change[:, 128:]

        return 0

    lax.fori_loop(0, nb, step, 0)
    xs = [None] * nb
    for s in reversed(range(nb)):
        acc = w[s, :, pl.ds(n, 128)]
        if s < nb - 1:
            acc = acc - mm(w[s, :, pl.ds(128 * (s + 1), 128 * (nb - 1 - s))], jnp.concatenate(xs[s + 1 :], axis=0))
        xs[s] = mm(li[s], acc, True)
    tot = sum(jnp.sum(v, axis=0, keepdims=True) for v in xs) * (1.0 / n)
    for s in range(nb):
        at = pl.ds(pl.multiple_of(lax.rem(x + nb - s, nb) * 128, 128), 128)
        high_ref[:, at], low_ref[:, at] = halves(((xs[s] - tot) * (1.0 / math.sqrt(n - 1.0)) + 1.0 / n).T)


def solve(g, d, alpha):
    nb = d.shape[0] // 16
    block = (128, 128)
    wide = pltpu.VMEM((nb, 128, 128 * (nb + 1)), F32)
    return pl.pallas_call(
        functools.partial(solve_kernel, alpha),
        out_shape=(jax.ShapeDtypeStruct((128, 128 * nb), BF),) * 2,
        in_specs=[VM, VM],
        out_specs=(VM, VM),
        scratch_shapes=[
            wide,
            pltpu.VMEM((nb, *block), F32),
            pltpu.VMEM((nb, *block), F32),
            pltpu.VMEM(block, F32),
            wide,
            pltpu.VMEM((8, 128), F32),
        ],
        name="factor_and_solve",
    )(g, d)


def update_kernel(uh_ref, ul_ref, e_ref, l_ref, o_ref, r_ref, out_ref):
    shape = e_ref.shape
    e = jnp.concatenate([e_ref[...]] + [ref[...].reshape(shape) for ref in (l_ref, o_ref, r_ref)], axis=0)
    eh, el = halves(e)
    out_ref[...] = bdot(uh_ref[...], eh) + bdot(uh_ref[...], el) + bdot(ul_ref[...], eh)


def update(uh, ul, e, left, opp, right):
    rows, width = e.shape
    t = 512
    pair = pl.BlockSpec((2, rows // 2, t), lambda i: (0, 0, i))
    fixed = pl.BlockSpec(uh.shape, lambda i: (0, 0))
    return pl.pallas_call(
        update_kernel,
        grid=(width // t,),
        out_shape=jax.ShapeDtypeStruct(e.shape, F32),
        in_specs=[fixed, fixed, pl.BlockSpec((rows, t), lambda i: (0, i)), pair, pair, pair],
        out_specs=pl.BlockSpec((rows, t), lambda i: (0, i)),
        name="update",
    )(uh, ul, e, left, opp, right)


def shards(ensemble, observed, obs_sigma, obs_index, member_seeds):
    alpha = PLAN[SECTION]
    nx, ny, nz = (lax.axis_size(a) for a in ("mem", "cells_1", "cells_0"))
    own = ensemble.shape[0]
    blocks = own * nx // 128
    width = obs_index.shape[0] // nx
    g, d, left, right, opp = reduce_all(
        (ensemble, obs_index[None, :], member_seeds[None, :], observed[None, :], obs_sigma[None, :]),
        all_fills(nx, alpha),
        all_scratch(own, ensemble.shape[1], width, nx),
        ensemble,
        16 * blocks * (blocks + 1) // 2 // (2 * ny * nx),
        16 * blocks // (2 * ny),
        nx,
        ny,
        nz,
    )
    return update(*solve(g, d, alpha), ensemble, left, opp, right)


def solution(mesh):
    finer = Mesh(mesh.devices.reshape(16, 4, 2, mesh.shape["mem"]), AXES)
    placed = (P("mem", CELLS), P(CELLS), P(CELLS), P(CELLS), P("mem"))
    return jax.shard_map(shards, mesh=finer, in_specs=placed, out_specs=P("mem", CELLS), check_vma=False)
```

```python
import functools
import math

import jax
import jax.numpy as jnp
from jax import lax
from jax.experimental import pallas as pl
from jax.experimental.pallas import tpu as pltpu
from jax.sharding import Mesh
from jax.sharding import PartitionSpec as P

SECTION = 1
CELLS = ("cells_0", "cells_1", "cells_2")
AXES = ("cells_0", "cells_1", "cells_2", "mem")
PLAN = (28.0 / 3.0, 7.0, 4.0, 2.0)
HI = lax.Precision.HIGHEST
BF = jnp.bfloat16
MESH = pl.DeviceIdType.MESH
VM = pl.BlockSpec(memory_space=pltpu.VMEM)
ANY = pl.BlockSpec(memory_space=pl.ANY)
F32 = jnp.float32


def remote(src, dst, send, recv, where):
    return pltpu.make_async_remote_copy(
        src_ref=src, dst_ref=dst, send_sem=send, recv_sem=recv, device_id=where, device_id_type=MESH
    )


def at_axis(axis, index):
    return {axis: index}


def greet(peers):
    barrier = pltpu.get_barrier_semaphore()
    for peer in peers:
        pl.semaphore_signal(barrier, inc=1, device_id=peer, device_id_type=MESH)
    pl.semaphore_wait(barrier, len(peers))


def order_of(n):
    return sorted(range(1, n), key=lambda d: -min(d, n - d))


def mod_prime(v):
    q = jnp.floor(v.astype(F32) * (1.0 / 65521.0)).astype(jnp.int32)
    r = v - q * 65521
    r = jnp.where(r < 0, r + 65521, r)
    return jnp.where(r >= 65521, r - 65521, r)


def cosine(h):
    h = jnp.minimum(h, 65521 - h)
    v = (65521 - 4 * h).astype(F32) * (math.pi / (2.0 * 65521.0))
    s = v * v
    poly = jnp.full_like(s, -1.0 / 39916800.0)
    for k in (9, 7, 5, 3, 1):
        poly = poly * s + (-1.0) ** ((k - 1) // 2) / math.factorial(k)
    return poly * v


def halves(v):
    high = v.astype(BF)
    return high, (v - high.astype(F32)).astype(BF)


def bdot(a, b, dims=((1,), (0,))):
    return lax.dot_general(a, b, (dims, ((), ())), preferred_element_type=F32)


def observe_stages(nx, alpha, e_ref, i_ref, s_ref, o_ref, n_ref, parts, hot, ready, mine_s, seeds, send, recv):
    x = lax.axis_index("mem")
    rows, cells = e_ref.shape
    width = i_ref.shape[1] // nx
    step, lanes = 512, width // 2

    def split():
        mine_s[...] = jnp.broadcast_to(s_ref[0:1, :].astype(F32), mine_s.shape)

        def block(k, _):
            cols = pl.ds(pl.multiple_of(k * step, step), step)
            v = e_ref[:, cols]
            high, rest = halves(v)
            parts[pl.ds(0, rows), cols] = high
            parts[pl.ds(rows, rows), cols] = rest
            parts[pl.ds(2 * rows, rows), cols] = (v - high.astype(F32) - rest.astype(F32)).astype(BF)
            return 0

        lax.fori_loop(0, cells // step, block, 0)

    def predict(d, h):
        to = lax.rem(x + d, nx)
        index = i_ref[:, pl.ds(pl.multiple_of(to * width + h * lanes, lanes), lanes)]

        def fill(k, _):
            at = pl.multiple_of(k * step, step)
            cell = lax.broadcasted_iota(jnp.int32, (step, lanes), 0) + at
            hot[pl.ds(at, step), :] = jnp.where(cell == index, 1.0, 0.0).astype(BF)
            return 0

        lax.fori_loop(0, cells // step, fill, 0)
        got = bdot(parts[...], hot[...])
        value = got[:rows] + got[rows : 2 * rows] + got[2 * rows :]
        ready[d, h] = jnp.tanh(value) + 0.5 * value

    mine = pl.ds(pl.multiple_of(x * rows, rows), rows)

    def copy_of(d, h):
        there = {"mem": lax.rem(x + d, nx)}
        if h is None:
            return remote(mine_s, seeds.at[x], send.at[2, d], recv.at[2, d], there)
        return remote(ready.at[d, h], o_ref.at[h, mine, :], send.at[h, d], recv.at[h, d], there)

    def keep():
        for h in range(2):
            o_ref[h, mine, :] = ready[0, h]
        seeds[x] = mine_s[...]

    def noise():
        base = lax.axis_index(CELLS) * i_ref.shape[1] + x * width
        where = mod_prime(lax.broadcasted_iota(jnp.int32, (1, width), 1) + base)

        def block(b, _):
            at = pl.ds(pl.multiple_of(b * rows, rows), rows)
            seed = jnp.broadcast_to(seeds[b, 0:1, :], (rows, rows)).T.astype(jnp.int32)
            first = mod_prime(seed * 389)
            second = seed - 997 * jnp.floor((seed.astype(F32) + 0.5) * (1.0 / 997.0)).astype(jnp.int32) + 1
            for c in range(width // 128):
                cols = slice(128 * c, 128 * c + 128)
                n_ref[at, cols] = cosine(mod_prime(first + where[:, cols] * second)) * math.sqrt(2.0 * alpha)
            return 0

        lax.fori_loop(0, nx, block, 0)

    return split, predict, copy_of, keep, noise


def product_fills(p_ref, n_ref, ob_ref, sg_ref, gp, dp, sh, sl, mh, ml):
    _, members, lanes = p_ref.shape
    blocks = members // 128
    both = ((1,), (1,))

    def prepare(h):
        mean = jnp.sum(p_ref[h], axis=0, keepdims=True) * (1.0 / members)
        part = pl.ds(pl.multiple_of(lax.axis_index("mem") * 2 * lanes + h * lanes, lanes), lanes)
        inv = 1.0 / sg_ref[:, part]
        scale = inv * (1.0 / math.sqrt(members - 1.0))
        shift = (ob_ref[:, part] - mean) * inv
        cols = pl.ds(h * lanes, lanes)

        def block(b, _):
            rows = pl.ds(pl.multiple_of(b * 64, 64), 64)
            sh[rows, :], sl[rows, :] = halves((p_ref[h, rows, :] - mean) * scale)
            mh[rows, :], ml[rows, :] = halves(n_ref[rows, cols] + shift)
            return 0

        lax.fori_loop(0, members // 64, block, 0)

    def fill_d(h):
        def block(b, _):
            rows = pl.ds(pl.multiple_of(b * 128, 128), 128)
            within = pl.ds(pl.multiple_of(lax.rem(b, 2) * 16, 16), 16)
            d = bdot(sh[rows, :], mh[...], both) + bdot(sh[rows, :], ml[...], both) + bdot(sl[rows, :], mh[...], both)
            for c in range(blocks):
                tiles = d[:, 128 * c : 128 * c + 128].reshape(16, 8, 128)
                dp[b // 2, c, within] = dp[b // 2, c, within] + tiles if h else tiles
            return 0

        lax.fori_loop(0, blocks, block, 0)

    def fill_g(h):
        at = 0
        for b in range(blocks):
            rows, rest = pl.ds(128 * b, 128), pl.ds(128 * b, members - 128 * b)
            g = (
                bdot(sh[rows, :], sh[rest, :], both)
                + bdot(sl[rows, :], sh[rest, :], both)
                + bdot(sh[rows, :], sl[rest, :], both)
                + bdot(sl[rows, :], sl[rest, :], both)
            )
            for c in range(blocks - b):
                tiles = g[:, 128 * c : 128 * c + 128].reshape(16, 8, 128)
                gp[pl.ds(at, 16)] = gp[pl.ds(at, 16)] + tiles if h else tiles
                at += 16

    return prepare, fill_d, fill_g


def all_fills(nx, alpha):
    def fills(e_ref, i_ref, s_ref, ob_ref, sg_ref, gp, dp, pred, noi, parts, hot, ready, mine_s, seeds, send, recv, *split):
        stages = observe_stages(nx, alpha, e_ref, i_ref, s_ref, pred, noi, parts, hot, ready, mine_s, seeds, send, recv)
        return stages, product_fills(pred, noi, ob_ref, sg_ref, gp, dp, *split)

    return fills


def all_scratch(rows, cells, width, nx):
    dma = pltpu.SemaphoreType.DMA
    whole = (rows * nx, width)
    lanes = width // 2
    return [
        pltpu.VMEM((2, rows * nx, lanes), F32),
        pltpu.VMEM(whole, F32),
        pltpu.VMEM((3 * rows, cells), BF),
        pltpu.VMEM((cells, lanes), BF),
        pltpu.VMEM((nx, 2, rows, lanes), F32),
        pltpu.VMEM((8, rows), F32),
        pltpu.VMEM((nx, 8, rows), F32),
        dma((3, nx)),
        dma((3, nx)),
    ] + [pltpu.VMEM((rows * nx, lanes), BF)] * 4


def reduce_kernel(n, fills, n_in, *refs):
    nx, ny, nz = n
    (e_ref, go, do, left, right, opp, gp, dp, rg0, rd0, sg0, sd0, rg1, rd1, sg1, sd1, rg2, rd2, zs, rz, zg,
     cs, cr, xs, xr, ys, yr, zss, zsr, es, er, heard) = refs[n_in : n_in + 32]
    stages, (prepare, fill_d, fill_g) = fills(*refs[:n_in], gp, dp, *refs[n_in + 32 :])
    z, y, c, x = (lax.axis_index(a) for a in AXES)
    oc = 1 - c

    def xat(d):
        return lax.rem(x + d, nx)

    def yat(d):
        return lax.rem(y + d, ny)

    def zat(d):
        return lax.rem(z + d, nz)

    core = {"cells_2": oc}
    beside = [{"cells_0": zat(d)} for d in sorted({1, nz - 1} - {0})] if nz > 1 else []
    peers = (
        [{"mem": xat(d)} for d in range(1, nx)] + [{"cells_1": yat(d)} for d in range(1, ny)] + [core] + beside
    )
    barrier = pltpu.get_barrier_semaphore()
    for peer in peers:
        pl.semaphore_signal(barrier, inc=1, device_id=peer, device_id_type=MESH)
    rounds = list(range(nz // 2 - 1))

    def spread(count=1):
        for r in rounds[:count]:
            for peer in beside:
                pl.semaphore_signal(heard.at[r], inc=1, device_id=peer, device_id_type=MESH)
            pl.semaphore_wait(heard.at[r], len(beside))
        del rounds[:count]

    ox, oy, oz = order_of(nx) + [0], order_of(ny) + [0], order_of(nz)
    sent = []

    def start(copy):
        copy.start()
        sent.append(copy)
        return copy

    td, tg = rd2.shape[1], rg2.shape[1]
    q = zs.shape[0] // nz

    def g_of(core_, yq):
        return pl.ds((core_ * ny + yq) * nx * tg, nx * tg)

    half = e_ref.shape[0] // 2
    eo = {}

    def ensemble(h):
        part = e_ref.at[pl.ds(h * half, half), :]
        eo[0, h] = start(remote(part, left.at[h], es.at[0, h], er.at[0, h], {"mem": xat(1)}))
        other = e_ref.at[pl.ds((1 - h) * half, half), :]
        eo[1, h] = start(remote(other, right.at[1 - h], es.at[1, h], er.at[1, h], {"mem": xat(nx - 1)}))

    split, predict, copy_of, keep, noise = stages
    split()
    of_seeds, of_pred = [], ([], [])
    for h in range(2):
        for d in ox[:-1]:
            predict(d, h)
            if not of_pred[0]:
                pl.semaphore_wait(barrier, len(peers))
                of_seeds = [start(copy_of(k, None)) for k in ox[:-1]]
            of_pred[h].append(start(copy_of(d, h)))
    ensemble(0)
    spread()
    predict(0, 0)
    spread()
    predict(0, 1)
    spread()
    keep()
    for w in of_seeds:
        w.wait_recv()
    noise()
    spread()
    for w in of_pred[0]:
        w.wait_recv()
    prepare(0)
    spread()
    fill_d(0)
    spread()
    fill_g(0)
    for w in of_pred[1]:
        w.wait_recv()
    prepare(1)
    fill_d(1)
    spread(nz)
    c0d, c0g = {}, {}
    for d in ox:
        c0d[d] = start(remote(dp.at[oc, xat(d)], rd0.at[xat(d)], cs.at[0, d], cr.at[0, d], core))
    fill_g(1)
    for d in oy:
        c0g[d] = start(remote(gp.at[g_of(oc, yat(d))], rg0.at[yat(d)], cs.at[1, d], cr.at[1, d], core))
    d1, g1 = {}, {}
    for d in ox:
        c0d[d].wait_recv()
        sd0[xat(d)] = dp[c, xat(d)] + rd0[xat(d)]
        if d:
            d1[d] = start(remote(sd0.at[xat(d)], rd1.at[d], xs.at[0, d], xr.at[0, d], {"mem": xat(d)}))
    for d in oy:
        c0g[d].wait_recv()
        sg0[yat(d)] = gp[g_of(c, yat(d))] + rg0[yat(d)]
        if d:
            g1[d] = start(remote(sg0.at[yat(d)], rg1.at[d], ys.at[0, d], yr.at[0, d], {"cells_1": yat(d)}))
    d2, g2 = {}, {}
    for d in oy[:-1]:
        g1[d].wait_recv()
    for d in ox:
        piece = pl.ds(xat(d) * tg, tg)
        total = sg0[y, piece]
        for k in range(1, ny):
            total = total + rg1[k, piece]
        sg1[xat(d)] = total
        if d:
            g2[d] = start(remote(sg1.at[xat(d)], rg2.at[d], xs.at[1, d], xr.at[1, d], {"mem": xat(d)}))
    for d in ox[:-1]:
        d1[d].wait_recv()
    for d in oy:
        piece = pl.ds(yat(d) * td, td)
        total = sd0[x, piece]
        for k in range(1, nx):
            total = total + rd1[k, piece]
        sd1[yat(d)] = total
        if d:
            d2[d] = start(remote(sd1.at[yat(d)], rd2.at[d], ys.at[1, d], yr.at[1, d], {"cells_1": yat(d)}))
    ensemble(1)
    for t in range(td + tg, nz * q):
        zs[t] = jnp.zeros_like(zs[t])
    for d in ox[:-1]:
        g2[d].wait_recv()
    total = sg1[x]
    for k in range(1, nx):
        total = total + rg2[k]
    zs[pl.ds(td, tg)] = total
    for d in oy[:-1]:
        d2[d].wait_recv()
    total = sd1[y]
    for k in range(1, ny):
        total = total + rd2[k]
    zs[pl.ds(0, td)] = total
    z1 = [
        start(remote(zs.at[pl.ds(zat(d) * q, q)], rz.at[d], zss.at[0, d], zsr.at[0, d], {"cells_0": zat(d)})) for d in oz
    ]
    eo[0, 0].wait_recv()
    eo[1, 0].wait_recv()
    far = [
        start(remote(left.at[0], opp.at[0], es.at[2, 0], er.at[2, 0], {"mem": xat(1)})),
        start(remote(right.at[1], opp.at[1], es.at[2, 1], er.at[2, 1], {"mem": xat(nx - 1)})),
    ]
    for w in z1:
        w.wait_recv()
    own = pl.ds(z * q, q)
    total = zs[own]
    for k in range(1, nz):
        total = total + rz[k]
    zg[own] = total
    z2 = [start(remote(zg.at[own], zg.at[own], zss.at[1, d], zsr.at[1, d], {"cells_0": zat(d)})) for d in oz]
    for w in z2:
        w.wait_recv()

    def go_of(yq):
        return pl.ds((c * ny + yq) * nx * tg, nx * tg)

    def do_of(yq):
        return pl.ds((c * ny + yq) * td, td)

    mine = pl.ds(((c * ny + y) * nx + x) * tg, tg)
    go[mine] = zg[pl.ds(td, tg)]
    do[do_of(y)] = zg[pl.ds(0, td)]
    dy, gx, gy = {}, {}, {}
    for d in ox[:-1]:
        gx[d] = start(remote(zg.at[pl.ds(td, tg)], go.at[mine], xs.at[2, d], xr.at[2, d], {"mem": xat(d)}))
    for d in oy[:-1]:
        dy[d] = start(remote(zg.at[pl.ds(0, td)], do.at[do_of(y)], ys.at[2, d], yr.at[2, d], {"cells_1": yat(d)}))
    last = [start(remote(zg.at[pl.ds(0, td)], do.at[do_of(y)], cs.at[2, 0], cr.at[2, 0], core))]
    for d in ox[:-1]:
        gx[d].wait_recv()
    for d in oy[:-1]:
        gy[d] = start(remote(go.at[go_of(y)], go.at[go_of(y)], ys.at[3, d], yr.at[3, d], {"cells_1": yat(d)}))
    last.append(start(remote(go.at[go_of(y)], go.at[go_of(y)], cs.at[3, 0], cr.at[3, 0], core)))
    for d in sorted(oy[:-1]):
        dy[d].wait_recv()
        frm = do_of(yat(ny - d))
        last.append(start(remote(do.at[frm], do.at[frm], cs.at[2, d], cr.at[2, d], core)))
    for d in reversed(oy[:-1]):
        gy[d].wait_recv()
        frm = go_of(yat(ny - d))
        last.append(start(remote(go.at[frm], go.at[frm], cs.at[3, d], cr.at[3, d], core)))
    for w in last + far + [eo[0, 1], eo[1, 1]]:
        w.wait_recv()
    for w in sent:
        w.wait_send()


def reduce_all(inputs, fills, extra, e, tg, td, nx, ny, nz):
    q = -(-(tg + td) // nz)
    tile = (8, 128)
    m = max(nx, ny)
    half = (2, e.shape[0] // 2, e.shape[1])
    dma = pltpu.SemaphoreType.DMA

    def tiles(*lead):
        return pltpu.VMEM((*lead, *tile), F32)

    return pl.pallas_call(
        functools.partial(reduce_kernel, (nx, ny, nz), fills, len(inputs)),
        out_shape=(
            jax.ShapeDtypeStruct((2 * ny * nx * tg, *tile), F32),
            jax.ShapeDtypeStruct((2 * ny * td, *tile), F32),
            jax.ShapeDtypeStruct(half, F32),
            jax.ShapeDtypeStruct(half, F32),
            jax.ShapeDtypeStruct(half, F32),
        ),
        in_specs=[VM] * len(inputs) + [ANY],
        out_specs=(VM, VM, ANY, ANY, ANY),
        scratch_shapes=[
            tiles(2 * ny * nx * tg),
            tiles(2, nx, ny * td),
            tiles(ny, nx * tg),
            tiles(nx, ny * td),
            tiles(ny, nx * tg),
            tiles(nx, ny * td),
            tiles(ny, nx * tg),
            tiles(nx, ny * td),
            tiles(nx, tg),
            tiles(ny, td),
            tiles(nx, tg),
            tiles(ny, td),
            tiles(nz * q),
            tiles(nz, q),
            tiles(nz * q),
            dma((4, m)), dma((4, m)), dma((3, nx)), dma((3, nx)), dma((4, ny)), dma((4, ny)), dma((2, nz)), dma((2, nz)),
            dma((3, 2)), dma((3, 2)), pltpu.SemaphoreType.REGULAR((max(nz // 2 - 1, 1),)),
            *extra,
        ],
        compiler_params=pltpu.CompilerParams(collective_id=1, has_side_effects=True),
        name="reduce_all",
    )(*inputs, e)


def factor_block(n_ref, low_ref, solved_ref, zero, span=4):
    lane = lax.broadcasted_iota(jnp.int32, (8, 128), 1)
    sub = lax.broadcasted_iota(jnp.int32, (8, 128), 0)

    def lb(v, c):
        return jnp.broadcast_to(v[:, c : c + 1], (8, 128))

    def sb(v, k):
        return jnp.broadcast_to(v[k : k + 1, :], (8, 128))

    for first in range(0, 16, span):
        end = 8 * (first + span)
        n = {i: n_ref[pl.ds(8 * i, 8), :] for i in range(first, first + span)}
        before, after = [], []
        for p in range(first, first + span):
            base = 8 * p
            cur = n[p]
            before.append(jnp.where(lane >= end, cur, 0.0))
            low_ref[pl.ds(base, 8), :] = jnp.where(lane < base, cur, jnp.where(lane == base + sub, 1.0, 0.0))
            t = [lb(cur, base + k) + zero for k in range(8)]
            for k in range(0, 8, 2):
                t0, t1 = t[k], t[k + 1]
                aa, ab, bb = sb(t0, k), sb(t1, k), sb(t1, k + 1)
                rec = 1.0 / (aa * bb - ab * ab)
                pair = (sub == k) | (sub == k + 1)
                top = sub == k
                x0, x1 = jnp.where(pair, 0.0, t0), jnp.where(pair, 0.0, t1)
                s0, s1 = lane == base + k, lane == base + k + 1
                r0 = jnp.where(s0, 1.0, jnp.where(s1, 0.0, sb(cur, k)))
                r1 = jnp.where(s1, 1.0, jnp.where(s0, 0.0, sb(cur, k + 1)))
                n0, n1 = bb * r0 - ab * r1, aa * r1 - ab * r0
                cur = jnp.where(pair, 0.0, jnp.where(s0 | s1, 0.0, cur)) - jnp.where(
                    pair, -jnp.where(top, n0, n1), x0 * n0 + x1 * n1
                ) * rec
                for q in range(k + 2, 8):
                    r0, r1 = sb(t[q], k), sb(t[q], k + 1)
                    n0, n1 = bb * r0 - ab * r1, aa * r1 - ab * r0
                    t[q] = jnp.where(pair, 0.0, t[q]) - jnp.where(pair, -jnp.where(top, n0, n1), x0 * n0 + x1 * n1) * rec
            solved_ref[pl.ds(base, 8), :] = jnp.where(lane < base + 8, cur, 0.0)
            after.append(jnp.where((lane >= base + 8) & (lane < end), 0.0, cur))
            rows = [sb(cur, k) for k in range(8)]
            inside = (lane >= base) & (lane < base + 8)
            for i in range(p + 1, first + span):
                acc = jnp.where(inside, 0.0, n[i])
                for k in range(8):
                    acc = acc - lb(n[i], base + k) * rows[k]
                n[i] = acc
        if end < 128:
            b = jnp.concatenate(before, axis=0)
            f = jnp.concatenate(after, axis=0)
            change = lax.dot_general(b, f, (((0,), (0,)), ((), ())), precision=HI, preferred_element_type=jnp.float32)
            keep = (lane < 8 * first) | (lane >= end)
            for i in range(first + span, 16):
                at = pl.ds(8 * i, 8)
                n_ref[at, :] = jnp.where(keep, n_ref[at, :], 0.0) - change[8 * i : 8 * i + 8]

def mm(a, b, ta=False):
    dn = (((0,), (0,)), ((), ())) if ta else (((1,), (0,)), ((), ()))
    return lax.dot_general(a, b, dn, precision=HI, preferred_element_type=F32)


def solve_kernel(alpha, g_ref, d_ref, high_ref, low_ref, a, dg, li, u, w, zero):
    nb = dg.shape[0]
    n = nb * 128
    x = lax.axis_index("mem")
    r = lax.broadcasted_iota(jnp.int32, (128, 128), 0)
    c = lax.broadcasted_iota(jnp.int32, (128, 128), 1)
    zero[...] = jnp.zeros_like(zero)
    first = 0
    for i in range(nb):
        for j in range(i, nb):
            blk = g_ref[pl.ds(first, 16)].reshape(128, 128)
            first += 16
            if i == j:
                dg[i] = blk + jnp.where(r == c, alpha, 0.0)
            else:
                a[i, :, pl.ds(128 * j, 128)] = blk
    unit = jnp.where(r == c, alpha * math.sqrt(n - 1.0), 0.0)
    for i in range(nb):
        a[i, :, pl.ds(n, 128)] = d_ref[pl.ds(16 * i, 16)].reshape(128, 128) + jnp.where(x == i, unit, 0.0)

    def step(b, _):
        factor_block(dg.at[b], li.at[b], u, zero[...])
        for s in range(nb):

            @pl.when(b == s)
            def _():
                cols = a[s, :, pl.ds(128 * (s + 1), 128 * (nb - s))]
                us = mm(li[s], cols)
                ws = mm(u[...], cols)
                w[s, :, pl.ds(128 * (s + 1), 128 * (nb - s))] = ws
                for i in range(s + 1, nb):
                    at = 128 * (i - s - 1)
                    change = mm(us[:, at : at + 128], ws[:, at:], True)
                    dg[i] = dg[i] - change[:, :128]
                    rest = pl.ds(128 * (i + 1), 128 * (nb - i))
                    a[i, :, rest] = a[i, :, rest] - change[:, 128:]

        return 0

    lax.fori_loop(0, nb, step, 0)
    xs = [None] * nb
    for s in reversed(range(nb)):
        acc = w[s, :, pl.ds(n, 128)]
        if s < nb - 1:
            acc = acc - mm(w[s, :, pl.ds(128 * (s + 1), 128 * (nb - 1 - s))], jnp.concatenate(xs[s + 1 :], axis=0))
        xs[s] = mm(li[s], acc, True)
    tot = sum(jnp.sum(v, axis=0, keepdims=True) for v in xs) * (1.0 / n)
    for s in range(nb):
        at = pl.ds(pl.multiple_of(lax.rem(x + nb - s, nb) * 128, 128), 128)
        high_ref[:, at], low_ref[:, at] = halves(((xs[s] - tot) * (1.0 / math.sqrt(n - 1.0)) + 1.0 / n).T)


def solve(g, d, alpha):
    nb = d.shape[0] // 16
    block = (128, 128)
    wide = pltpu.VMEM((nb, 128, 128 * (nb + 1)), F32)
    return pl.pallas_call(
        functools.partial(solve_kernel, alpha),
        out_shape=(jax.ShapeDtypeStruct((128, 128 * nb), BF),) * 2,
        in_specs=[VM, VM],
        out_specs=(VM, VM),
        scratch_shapes=[
            wide,
            pltpu.VMEM((nb, *block), F32),
            pltpu.VMEM((nb, *block), F32),
            pltpu.VMEM(block, F32),
            wide,
            pltpu.VMEM((8, 128), F32),
        ],
        name="factor_and_solve",
    )(g, d)


def update_kernel(uh_ref, ul_ref, e_ref, l_ref, o_ref, r_ref, out_ref):
    shape = e_ref.shape
    e = jnp.concatenate([e_ref[...]] + [ref[...].reshape(shape) for ref in (l_ref, o_ref, r_ref)], axis=0)
    eh, el = halves(e)
    out_ref[...] = bdot(uh_ref[...], eh) + bdot(uh_ref[...], el) + bdot(ul_ref[...], eh)


def update(uh, ul, e, left, opp, right):
    rows, width = e.shape
    t = 512
    pair = pl.BlockSpec((2, rows // 2, t), lambda i: (0, 0, i))
    fixed = pl.BlockSpec(uh.shape, lambda i: (0, 0))
    return pl.pallas_call(
        update_kernel,
        grid=(width // t,),
        out_shape=jax.ShapeDtypeStruct(e.shape, F32),
        in_specs=[fixed, fixed, pl.BlockSpec((rows, t), lambda i: (0, i)), pair, pair, pair],
        out_specs=pl.BlockSpec((rows, t), lambda i: (0, i)),
        name="update",
    )(uh, ul, e, left, opp, right)


def shards(ensemble, observed, obs_sigma, obs_index, member_seeds):
    alpha = PLAN[SECTION]
    nx, ny, nz = (lax.axis_size(a) for a in ("mem", "cells_1", "cells_0"))
    own = ensemble.shape[0]
    blocks = own * nx // 128
    width = obs_index.shape[0] // nx
    g, d, left, right, opp = reduce_all(
        (ensemble, obs_index[None, :], member_seeds[None, :], observed[None, :], obs_sigma[None, :]),
        all_fills(nx, alpha),
        all_scratch(own, ensemble.shape[1], width, nx),
        ensemble,
        16 * blocks * (blocks + 1) // 2 // (2 * ny * nx),
        16 * blocks // (2 * ny),
        nx,
        ny,
        nz,
    )
    return update(*solve(g, d, alpha), ensemble, left, opp, right)


def solution(mesh):
    finer = Mesh(mesh.devices.reshape(16, 4, 2, mesh.shape["mem"]), AXES)
    placed = (P("mem", CELLS), P(CELLS), P(CELLS), P(CELLS), P("mem"))
    return jax.shard_map(shards, mesh=finer, in_specs=placed, out_specs=P("mem", CELLS), check_vma=False)
```

```python
import functools
import math

import jax
import jax.numpy as jnp
from jax import lax
from jax.experimental import pallas as pl
from jax.experimental.pallas import tpu as pltpu
from jax.sharding import Mesh
from jax.sharding import PartitionSpec as P

SECTION = 1
CELLS = ("cells_0", "cells_1", "cells_2")
AXES = ("cells_0", "cells_1", "cells_2", "mem")
PLAN = (28.0 / 3.0, 7.0, 4.0, 2.0)
HI = lax.Precision.HIGHEST
BF = jnp.bfloat16
MESH = pl.DeviceIdType.MESH
VM = pl.BlockSpec(memory_space=pltpu.VMEM)
ANY = pl.BlockSpec(memory_space=pl.ANY)
F32 = jnp.float32


def remote(src, dst, send, recv, where):
    return pltpu.make_async_remote_copy(
        src_ref=src, dst_ref=dst, send_sem=send, recv_sem=recv, device_id=where, device_id_type=MESH
    )


def at_axis(axis, index):
    return {axis: index}


def greet(peers):
    barrier = pltpu.get_barrier_semaphore()
    for peer in peers:
        pl.semaphore_signal(barrier, inc=1, device_id=peer, device_id_type=MESH)
    pl.semaphore_wait(barrier, len(peers))


def order_of(n):
    return sorted(range(1, n), key=lambda d: -min(d, n - d))


def mod_prime(v):
    q = jnp.floor(v.astype(F32) * (1.0 / 65521.0)).astype(jnp.int32)
    r = v - q * 65521
    r = jnp.where(r < 0, r + 65521, r)
    return jnp.where(r >= 65521, r - 65521, r)


def cosine(h):
    h = jnp.minimum(h, 65521 - h)
    v = (65521 - 4 * h).astype(F32) * (math.pi / (2.0 * 65521.0))
    s = v * v
    poly = jnp.full_like(s, -1.0 / 39916800.0)
    for k in (9, 7, 5, 3, 1):
        poly = poly * s + (-1.0) ** ((k - 1) // 2) / math.factorial(k)
    return poly * v


def halves(v):
    high = v.astype(BF)
    return high, (v - high.astype(F32)).astype(BF)


def bdot(a, b, dims=((1,), (0,))):
    return lax.dot_general(a, b, (dims, ((), ())), preferred_element_type=F32)


def observe_stages(nx, alpha, e_ref, i_ref, s_ref, o_ref, n_ref, parts, hot, ready, mine_s, seeds, send, recv):
    x = lax.axis_index("mem")
    rows, cells = e_ref.shape
    width = i_ref.shape[1] // nx
    step, lanes = 512, 256

    def split():
        mine_s[...] = jnp.broadcast_to(s_ref[0:1, :].astype(F32), mine_s.shape)

        def block(k, _):
            cols = pl.ds(pl.multiple_of(k * step, step), step)
            v = e_ref[:, cols]
            high, rest = halves(v)
            parts[pl.ds(0, rows), cols] = high
            parts[pl.ds(rows, rows), cols] = rest
            parts[pl.ds(2 * rows, rows), cols] = (v - high.astype(F32) - rest.astype(F32)).astype(BF)
            return 0

        lax.fori_loop(0, cells // step, block, 0)

    def predict(d):
        to = lax.rem(x + d, nx)

        def some(h, _):
            index = i_ref[:, pl.ds(pl.multiple_of(to * width + h * lanes, lanes), lanes)]

            def fill(k, _):
                at = pl.multiple_of(k * step, step)
                cell = lax.broadcasted_iota(jnp.int32, (step, lanes), 0) + at
                hot[pl.ds(at, step), :] = jnp.where(cell == index, 1.0, 0.0).astype(BF)
                return 0

            lax.fori_loop(0, cells // step, fill, 0)
            got = bdot(parts[...], hot[...])
            value = got[:rows] + got[rows : 2 * rows] + got[2 * rows :]
            ready[d, :, pl.ds(pl.multiple_of(h * lanes, lanes), lanes)] = jnp.tanh(value) + 0.5 * value
            return 0

        lax.fori_loop(0, width // lanes, some, 0)

    def copy_of(d, what):
        there = {"mem": lax.rem(x + d, nx)}
        if what:
            return remote(mine_s, seeds.at[x], send.at[1, d], recv.at[1, d], there)
        at = pl.ds(pl.multiple_of(x * rows, rows), rows)
        return remote(ready.at[d], o_ref.at[at, :], send.at[0, d], recv.at[0, d], there)

    def keep():
        o_ref[pl.ds(pl.multiple_of(x * rows, rows), rows), :] = ready[0]
        seeds[x] = mine_s[...]

    def noise():
        base = lax.axis_index(CELLS) * i_ref.shape[1] + x * width
        where = mod_prime(lax.broadcasted_iota(jnp.int32, (1, width), 1) + base)

        def block(b, _):
            at = pl.ds(pl.multiple_of(b * rows, rows), rows)
            seed = jnp.broadcast_to(seeds[b, 0:1, :], (rows, rows)).T.astype(jnp.int32)
            first = mod_prime(seed * 389)
            second = seed - 997 * jnp.floor((seed.astype(F32) + 0.5) * (1.0 / 997.0)).astype(jnp.int32) + 1
            for c in range(width // 128):
                cols = slice(128 * c, 128 * c + 128)
                n_ref[at, cols] = cosine(mod_prime(first + where[:, cols] * second)) * math.sqrt(2.0 * alpha)
            return 0

        lax.fori_loop(0, nx, block, 0)

    return split, predict, copy_of, keep, noise


def product_fills(p_ref, n_ref, ob_ref, sg_ref, gp, dp, sh, sl, mh, ml):
    members, width = p_ref.shape
    blocks = members // 128

    def prepare():
        mean = jnp.sum(p_ref[...], axis=0, keepdims=True) * (1.0 / members)
        part = pl.ds(pl.multiple_of(lax.axis_index("mem") * width, width), width)
        inv = 1.0 / sg_ref[:, part]
        scale = inv * (1.0 / math.sqrt(members - 1.0))
        shift = (ob_ref[:, part] - mean) * inv

        def block(b, _):
            rows = pl.ds(pl.multiple_of(b * 64, 64), 64)
            sh[rows, :], sl[rows, :] = halves((p_ref[rows, :] - mean) * scale)
            mh[rows, :], ml[rows, :] = halves(n_ref[rows, :] + shift)
            return 0

        lax.fori_loop(0, members // 64, block, 0)

    both = ((1,), (1,))

    def fill_d():
        def block(b, _):
            rows = pl.ds(pl.multiple_of(b * 128, 128), 128)
            within = pl.ds(pl.multiple_of(lax.rem(b, 2) * 16, 16), 16)
            d = bdot(sh[rows, :], mh[...], both) + bdot(sh[rows, :], ml[...], both) + bdot(sl[rows, :], mh[...], both)
            for c in range(blocks):
                dp[b // 2, c, within] = d[:, 128 * c : 128 * c + 128].reshape(16, 8, 128)
            return 0

        lax.fori_loop(0, blocks, block, 0)

    def fill_g():
        at = 0
        for b in range(blocks):
            rows, rest = pl.ds(128 * b, 128), pl.ds(128 * b, members - 128 * b)
            g = (
                bdot(sh[rows, :], sh[rest, :], both)
                + bdot(sl[rows, :], sh[rest, :], both)
                + bdot(sh[rows, :], sl[rest, :], both)
                + bdot(sl[rows, :], sl[rest, :], both)
            )
            for c in range(blocks - b):
                gp[pl.ds(at, 16)] = g[:, 128 * c : 128 * c + 128].reshape(16, 8, 128)
                at += 16

    return prepare, fill_d, fill_g


def all_fills(nx, alpha):
    def fills(e_ref, i_ref, s_ref, ob_ref, sg_ref, gp, dp, pred, noi, parts, hot, ready, mine_s, seeds, send, recv, *split):
        stages = observe_stages(nx, alpha, e_ref, i_ref, s_ref, pred, noi, parts, hot, ready, mine_s, seeds, send, recv)
        return stages, product_fills(pred, noi, ob_ref, sg_ref, gp, dp, *split)

    return fills


def all_scratch(rows, cells, width, nx):
    dma = pltpu.SemaphoreType.DMA
    whole = (rows * nx, width)
    return [
        pltpu.VMEM(whole, F32),
        pltpu.VMEM(whole, F32),
        pltpu.VMEM((3 * rows, cells), BF),
        pltpu.VMEM((cells, 256), BF),
        pltpu.VMEM((nx, rows, width), F32),
        pltpu.VMEM((8, rows), F32),
        pltpu.VMEM((nx, 8, rows), F32),
        dma((2, nx)),
        dma((2, nx)),
    ] + [pltpu.VMEM(whole, BF)] * 4


def reduce_kernel(n, fills, n_in, finish, *refs):
    nx, ny, nz = n
    (e_ref, high, low, left, right, opp, go, do, gp, dp, rg0, rd0, sg0, sd0, rg1, rd1, sg1, sd1, rg2, rd2, zs, rz, zg,
     cs, cr, xs, xr, ys, yr, zss, zsr, es, er, heard) = refs[n_in : n_in + 34]
    stages, (prepare, fill_d, fill_g) = fills(*refs[:n_in], gp, dp, *refs[n_in + 34 : -6])
    z, y, c, x = (lax.axis_index(a) for a in AXES)
    oc = 1 - c

    def xat(d):
        return lax.rem(x + d, nx)

    def yat(d):
        return lax.rem(y + d, ny)

    def zat(d):
        return lax.rem(z + d, nz)

    core = {"cells_2": oc}
    beside = [{"cells_0": zat(d)} for d in sorted({1, nz - 1} - {0})] if nz > 1 else []
    peers = (
        [{"mem": xat(d)} for d in range(1, nx)] + [{"cells_1": yat(d)} for d in range(1, ny)] + [core] + beside
    )
    barrier = pltpu.get_barrier_semaphore()
    for peer in peers:
        pl.semaphore_signal(barrier, inc=1, device_id=peer, device_id_type=MESH)
    rounds = list(range(nz // 2 - 1))

    def spread(count=1):
        for r in rounds[:count]:
            for peer in beside:
                pl.semaphore_signal(heard.at[r], inc=1, device_id=peer, device_id_type=MESH)
            pl.semaphore_wait(heard.at[r], len(beside))
        del rounds[:count]

    ox, oy, oz = order_of(nx) + [0], order_of(ny) + [0], order_of(nz)
    sent = []

    def start(copy):
        copy.start()
        sent.append(copy)
        return copy

    td, tg = rd2.shape[1], rg2.shape[1]
    q = zs.shape[0] // nz

    def g_of(core_, yq):
        return pl.ds((core_ * ny + yq) * nx * tg, nx * tg)

    half = e_ref.shape[0] // 2
    eo = {}

    def ensemble(h):
        part = e_ref.at[pl.ds(h * half, half), :]
        eo[0, h] = start(remote(part, left.at[h], es.at[0, h], er.at[0, h], {"mem": xat(1)}))
        other = e_ref.at[pl.ds((1 - h) * half, half), :]
        eo[1, h] = start(remote(other, right.at[1 - h], es.at[1, h], er.at[1, h], {"mem": xat(nx - 1)}))

    split, predict, copy_of, keep, noise = stages
    split()
    of_seeds, of_pred = [], []
    for d in ox[:-1]:
        predict(d)
        if not of_pred:
            pl.semaphore_wait(barrier, len(peers))
            of_seeds = [start(copy_of(k, True)) for k in ox[:-1]]
        of_pred.append(start(copy_of(d, False)))
    ensemble(0)
    spread()
    predict(0)
    spread()
    keep()
    for w in of_seeds:
        w.wait_recv()
    spread()
    noise()
    spread()
    for w in of_pred:
        w.wait_recv()
        spread()
    prepare()
    spread(nz)
    fill_d()
    c0d, c0g = {}, {}
    for d in ox:
        c0d[d] = start(remote(dp.at[oc, xat(d)], rd0.at[xat(d)], cs.at[0, d], cr.at[0, d], core))
    fill_g()
    for d in oy:
        c0g[d] = start(remote(gp.at[g_of(oc, yat(d))], rg0.at[yat(d)], cs.at[1, d], cr.at[1, d], core))
    d1, g1 = {}, {}
    for d in ox:
        c0d[d].wait_recv()
        sd0[xat(d)] = dp[c, xat(d)] + rd0[xat(d)]
        if d:
            d1[d] = start(remote(sd0.at[xat(d)], rd1.at[d], xs.at[0, d], xr.at[0, d], {"mem": xat(d)}))
    for d in oy:
        c0g[d].wait_recv()
        sg0[yat(d)] = gp[g_of(c, yat(d))] + rg0[yat(d)]
        if d:
            g1[d] = start(remote(sg0.at[yat(d)], rg1.at[d], ys.at[0, d], yr.at[0, d], {"cells_1": yat(d)}))
    d2, g2 = {}, {}
    for d in oy[:-1]:
        g1[d].wait_recv()
    for d in ox:
        piece = pl.ds(xat(d) * tg, tg)
        total = sg0[y, piece]
        for k in range(1, ny):
            total = total + rg1[k, piece]
        sg1[xat(d)] = total
        if d:
            g2[d] = start(remote(sg1.at[xat(d)], rg2.at[d], xs.at[1, d], xr.at[1, d], {"mem": xat(d)}))
    for d in ox[:-1]:
        d1[d].wait_recv()
    for d in oy:
        piece = pl.ds(yat(d) * td, td)
        total = sd0[x, piece]
        for k in range(1, nx):
            total = total + rd1[k, piece]
        sd1[yat(d)] = total
        if d:
            d2[d] = start(remote(sd1.at[yat(d)], rd2.at[d], ys.at[1, d], yr.at[1, d], {"cells_1": yat(d)}))
    ensemble(1)
    for t in range(td + tg, nz * q):
        zs[t] = jnp.zeros_like(zs[t])
    for d in ox[:-1]:
        g2[d].wait_recv()
    total = sg1[x]
    for k in range(1, nx):
        total = total + rg2[k]
    zs[pl.ds(td, tg)] = total
    for d in oy[:-1]:
        d2[d].wait_recv()
    total = sd1[y]
    for k in range(1, ny):
        total = total + rd2[k]
    zs[pl.ds(0, td)] = total
    z1 = [
        start(remote(zs.at[pl.ds(zat(d) * q, q)], rz.at[d], zss.at[0, d], zsr.at[0, d], {"cells_0": zat(d)})) for d in oz
    ]
    for w in z1:
        w.wait_recv()
    own = pl.ds(z * q, q)
    total = zs[own]
    for k in range(1, nz):
        total = total + rz[k]
    zg[own] = total
    z2 = [start(remote(zg.at[own], zg.at[own], zss.at[1, d], zsr.at[1, d], {"cells_0": zat(d)})) for d in oz]
    for w in z2:
        w.wait_recv()

    def go_of(yq):
        return pl.ds((c * ny + yq) * nx * tg, nx * tg)

    def do_of(yq):
        return pl.ds((c * ny + yq) * td, td)

    mine = pl.ds(((c * ny + y) * nx + x) * tg, tg)
    go[mine] = zg[pl.ds(td, tg)]
    do[do_of(y)] = zg[pl.ds(0, td)]
    dy, gx, gy = {}, {}, {}
    for d in ox[:-1]:
        gx[d] = start(remote(zg.at[pl.ds(td, tg)], go.at[mine], xs.at[2, d], xr.at[2, d], {"mem": xat(d)}))
    for d in oy[:-1]:
        dy[d] = start(remote(zg.at[pl.ds(0, td)], do.at[do_of(y)], ys.at[2, d], yr.at[2, d], {"cells_1": yat(d)}))
    last = [start(remote(zg.at[pl.ds(0, td)], do.at[do_of(y)], cs.at[2, 0], cr.at[2, 0], core))]
    for d in ox[:-1]:
        gx[d].wait_recv()
    for d in oy[:-1]:
        gy[d] = start(remote(go.at[go_of(y)], go.at[go_of(y)], ys.at[3, d], yr.at[3, d], {"cells_1": yat(d)}))
    last.append(start(remote(go.at[go_of(y)], go.at[go_of(y)], cs.at[3, 0], cr.at[3, 0], core)))
    eo[0, 0].wait_recv()
    eo[1, 0].wait_recv()
    far = [
        start(remote(left.at[0], opp.at[0], es.at[2, 0], er.at[2, 0], {"mem": xat(1)})),
        start(remote(right.at[1], opp.at[1], es.at[2, 1], er.at[2, 1], {"mem": xat(nx - 1)})),
    ]
    for d in sorted(oy[:-1]):
        dy[d].wait_recv()
        frm = do_of(yat(ny - d))
        last.append(start(remote(do.at[frm], do.at[frm], cs.at[2, d], cr.at[2, d], core)))
    for d in reversed(oy[:-1]):
        gy[d].wait_recv()
        frm = go_of(yat(ny - d))
        last.append(start(remote(go.at[frm], go.at[frm], cs.at[3, d], cr.at[3, d], core)))
    for w in last:
        w.wait_recv()
    finish(go, do, high, low, *refs[-6:])
    for w in far + [eo[0, 1], eo[1, 1]]:
        w.wait_recv()
    for w in sent:
        w.wait_send()


def reduce_all(inputs, fills, extra, finish, result, more, e, tg, td, nx, ny, nz):
    q = -(-(tg + td) // nz)
    tile = (8, 128)
    m = max(nx, ny)
    half = (2, e.shape[0] // 2, e.shape[1])
    dma = pltpu.SemaphoreType.DMA

    def tiles(*lead):
        return pltpu.VMEM((*lead, *tile), F32)

    return pl.pallas_call(
        functools.partial(reduce_kernel, (nx, ny, nz), fills, len(inputs), finish),
        out_shape=(
            result,
            result,
            jax.ShapeDtypeStruct(half, F32),
            jax.ShapeDtypeStruct(half, F32),
            jax.ShapeDtypeStruct(half, F32),
        ),
        in_specs=[VM] * len(inputs) + [ANY],
        out_specs=(VM, VM, ANY, ANY, ANY),
        scratch_shapes=[
            tiles(2 * ny * nx * tg),
            tiles(2 * ny * td),
            tiles(2 * ny * nx * tg),
            tiles(2, nx, ny * td),
            tiles(ny, nx * tg),
            tiles(nx, ny * td),
            tiles(ny, nx * tg),
            tiles(nx, ny * td),
            tiles(ny, nx * tg),
            tiles(nx, ny * td),
            tiles(nx, tg),
            tiles(ny, td),
            tiles(nx, tg),
            tiles(ny, td),
            tiles(nz * q),
            tiles(nz, q),
            tiles(nz * q),
            dma((4, m)), dma((4, m)), dma((3, nx)), dma((3, nx)), dma((4, ny)), dma((4, ny)), dma((2, nz)), dma((2, nz)),
            dma((3, 2)), dma((3, 2)), pltpu.SemaphoreType.REGULAR((max(nz // 2 - 1, 1),)),
            *extra,
            *more,
        ],
        compiler_params=pltpu.CompilerParams(collective_id=1, has_side_effects=True),
        name="reduce_all",
    )(*inputs, e)


def factor_block(n_ref, low_ref, solved_ref, zero, span=4):
    lane = lax.broadcasted_iota(jnp.int32, (8, 128), 1)
    sub = lax.broadcasted_iota(jnp.int32, (8, 128), 0)

    def lb(v, c):
        return jnp.broadcast_to(v[:, c : c + 1], (8, 128))

    def sb(v, k):
        return jnp.broadcast_to(v[k : k + 1, :], (8, 128))

    for first in range(0, 16, span):
        end = 8 * (first + span)
        n = {i: n_ref[pl.ds(8 * i, 8), :] for i in range(first, first + span)}
        before, after = [], []
        for p in range(first, first + span):
            base = 8 * p
            cur = n[p]
            before.append(jnp.where(lane >= end, cur, 0.0))
            low_ref[pl.ds(base, 8), :] = jnp.where(lane < base, cur, jnp.where(lane == base + sub, 1.0, 0.0))
            t = [lb(cur, base + k) + zero for k in range(8)]
            for k in range(0, 8, 2):
                t0, t1 = t[k], t[k + 1]
                aa, ab, bb = sb(t0, k), sb(t1, k), sb(t1, k + 1)
                rec = 1.0 / (aa * bb - ab * ab)
                pair = (sub == k) | (sub == k + 1)
                top = sub == k
                x0, x1 = jnp.where(pair, 0.0, t0), jnp.where(pair, 0.0, t1)
                s0, s1 = lane == base + k, lane == base + k + 1
                r0 = jnp.where(s0, 1.0, jnp.where(s1, 0.0, sb(cur, k)))
                r1 = jnp.where(s1, 1.0, jnp.where(s0, 0.0, sb(cur, k + 1)))
                n0, n1 = bb * r0 - ab * r1, aa * r1 - ab * r0
                cur = jnp.where(pair, 0.0, jnp.where(s0 | s1, 0.0, cur)) - jnp.where(
                    pair, -jnp.where(top, n0, n1), x0 * n0 + x1 * n1
                ) * rec
                for q in range(k + 2, 8):
                    r0, r1 = sb(t[q], k), sb(t[q], k + 1)
                    n0, n1 = bb * r0 - ab * r1, aa * r1 - ab * r0
                    t[q] = jnp.where(pair, 0.0, t[q]) - jnp.where(pair, -jnp.where(top, n0, n1), x0 * n0 + x1 * n1) * rec
            solved_ref[pl.ds(base, 8), :] = jnp.where(lane < base + 8, cur, 0.0)
            after.append(jnp.where((lane >= base + 8) & (lane < end), 0.0, cur))
            rows = [sb(cur, k) for k in range(8)]
            inside = (lane >= base) & (lane < base + 8)
            for i in range(p + 1, first + span):
                acc = jnp.where(inside, 0.0, n[i])
                for k in range(8):
                    acc = acc - lb(n[i], base + k) * rows[k]
                n[i] = acc
        if end < 128:
            b = jnp.concatenate(before, axis=0)
            f = jnp.concatenate(after, axis=0)
            change = lax.dot_general(b, f, (((0,), (0,)), ((), ())), precision=HI, preferred_element_type=jnp.float32)
            keep = (lane < 8 * first) | (lane >= end)
            for i in range(first + span, 16):
                at = pl.ds(8 * i, 8)
                n_ref[at, :] = jnp.where(keep, n_ref[at, :], 0.0) - change[8 * i : 8 * i + 8]

def mm(a, b, ta=False):
    dn = (((0,), (0,)), ((), ())) if ta else (((1,), (0,)), ((), ()))
    return lax.dot_general(a, b, dn, precision=HI, preferred_element_type=F32)


def solve_kernel(alpha, g_ref, d_ref, high_ref, low_ref, a, dg, li, u, w, zero):
    nb = dg.shape[0]
    n = nb * 128
    x = lax.axis_index("mem")
    r = lax.broadcasted_iota(jnp.int32, (128, 128), 0)
    c = lax.broadcasted_iota(jnp.int32, (128, 128), 1)
    zero[...] = jnp.zeros_like(zero)
    first = 0
    for i in range(nb):
        for j in range(i, nb):
            blk = g_ref[pl.ds(first, 16)].reshape(128, 128)
            first += 16
            if i == j:
                dg[i] = blk + jnp.where(r == c, alpha, 0.0)
            else:
                a[i, :, pl.ds(128 * j, 128)] = blk
    unit = jnp.where(r == c, alpha * math.sqrt(n - 1.0), 0.0)
    for i in range(nb):
        a[i, :, pl.ds(n, 128)] = d_ref[pl.ds(16 * i, 16)].reshape(128, 128) + jnp.where(x == i, unit, 0.0)

    def step(b, _):
        factor_block(dg.at[b], li.at[b], u, zero[...])
        for s in range(nb):

            @pl.when(b == s)
            def _():
                cols = a[s, :, pl.ds(128 * (s + 1), 128 * (nb - s))]
                us = mm(li[s], cols)
                ws = mm(u[...], cols)
                w[s, :, pl.ds(128 * (s + 1), 128 * (nb - s))] = ws
                for i in range(s + 1, nb):
                    at = 128 * (i - s - 1)
                    change = mm(us[:, at : at + 128], ws[:, at:], True)
                    dg[i] = dg[i] - change[:, :128]
                    rest = pl.ds(128 * (i + 1), 128 * (nb - i))
                    a[i, :, rest] = a[i, :, rest] - change[:, 128:]

        return 0

    lax.fori_loop(0, nb, step, 0)
    xs = [None] * nb
    for s in reversed(range(nb)):
        acc = w[s, :, pl.ds(n, 128)]
        if s < nb - 1:
            acc = acc - mm(w[s, :, pl.ds(128 * (s + 1), 128 * (nb - 1 - s))], jnp.concatenate(xs[s + 1 :], axis=0))
        xs[s] = mm(li[s], acc, True)
    tot = sum(jnp.sum(v, axis=0, keepdims=True) for v in xs) * (1.0 / n)
    for s in range(nb):
        at = pl.ds(pl.multiple_of(lax.rem(x + nb - s, nb) * 128, 128), 128)
        high_ref[:, at], low_ref[:, at] = halves(((xs[s] - tot) * (1.0 / math.sqrt(n - 1.0)) + 1.0 / n).T)


def solve_scratch(nb):
    block = (128, 128)
    wide = pltpu.VMEM((nb, 128, 128 * (nb + 1)), F32)
    return [
        wide,
        pltpu.VMEM((nb, *block), F32),
        pltpu.VMEM((nb, *block), F32),
        pltpu.VMEM(block, F32),
        wide,
        pltpu.VMEM((8, 128), F32),
    ]


def update_kernel(uh_ref, ul_ref, e_ref, l_ref, o_ref, r_ref, out_ref):
    shape = e_ref.shape
    e = jnp.concatenate([e_ref[...]] + [ref[...].reshape(shape) for ref in (l_ref, o_ref, r_ref)], axis=0)
    eh, el = halves(e)
    out_ref[...] = bdot(uh_ref[...], eh) + bdot(uh_ref[...], el) + bdot(ul_ref[...], eh)


def update(uh, ul, e, left, opp, right):
    rows, width = e.shape
    t = 512
    pair = pl.BlockSpec((2, rows // 2, t), lambda i: (0, 0, i))
    fixed = pl.BlockSpec(uh.shape, lambda i: (0, 0))
    return pl.pallas_call(
        update_kernel,
        grid=(width // t,),
        out_shape=jax.ShapeDtypeStruct(e.shape, F32),
        in_specs=[fixed, fixed, pl.BlockSpec((rows, t), lambda i: (0, i)), pair, pair, pair],
        out_specs=pl.BlockSpec((rows, t), lambda i: (0, i)),
        name="update",
    )(uh, ul, e, left, opp, right)


def shards(ensemble, observed, obs_sigma, obs_index, member_seeds):
    alpha = PLAN[SECTION]
    nx, ny, nz = (lax.axis_size(a) for a in ("mem", "cells_1", "cells_0"))
    own = ensemble.shape[0]
    blocks = own * nx // 128
    width = obs_index.shape[0] // nx
    high, low, left, right, opp = reduce_all(
        (ensemble, obs_index[None, :], member_seeds[None, :], observed[None, :], obs_sigma[None, :]),
        all_fills(nx, alpha),
        all_scratch(own, ensemble.shape[1], width, nx),
        functools.partial(solve_kernel, alpha),
        jax.ShapeDtypeStruct((128, 128 * blocks), BF),
        solve_scratch(blocks),
        ensemble,
        16 * blocks * (blocks + 1) // 2 // (2 * ny * nx),
        16 * blocks // (2 * ny),
        nx,
        ny,
        nz,
    )
    return update(high, low, ensemble, left, opp, right)


def solution(mesh):
    finer = Mesh(mesh.devices.reshape(16, 4, 2, mesh.shape["mem"]), AXES)
    placed = (P("mem", CELLS), P(CELLS), P(CELLS), P(CELLS), P("mem"))
    return jax.shard_map(shards, mesh=finer, in_specs=placed, out_specs=P("mem", CELLS), check_vma=False)
```

```python
import functools
import math

import jax
import jax.numpy as jnp
from jax import lax
from jax.experimental import pallas as pl
from jax.experimental.pallas import tpu as pltpu
from jax.sharding import Mesh
from jax.sharding import PartitionSpec as P

SECTION = 1
CELLS = ("cells_0", "cells_1", "cells_2")
AXES = ("cells_0", "cells_1", "cells_2", "mem")
PLAN = (28.0 / 3.0, 7.0, 4.0, 2.0)
HI = lax.Precision.HIGHEST
BF = jnp.bfloat16
MESH = pl.DeviceIdType.MESH
VM = pl.BlockSpec(memory_space=pltpu.VMEM)
ANY = pl.BlockSpec(memory_space=pl.ANY)
F32 = jnp.float32


def remote(src, dst, send, recv, where):
    return pltpu.make_async_remote_copy(
        src_ref=src, dst_ref=dst, send_sem=send, recv_sem=recv, device_id=where, device_id_type=MESH
    )


def at_axis(axis, index):
    return {axis: index}


def greet(peers):
    barrier = pltpu.get_barrier_semaphore()
    for peer in peers:
        pl.semaphore_signal(barrier, inc=1, device_id=peer, device_id_type=MESH)
    pl.semaphore_wait(barrier, len(peers))


def order_of(n):
    return sorted(range(1, n), key=lambda d: -min(d, n - d))


def mod_prime(v):
    q = jnp.floor(v.astype(F32) * (1.0 / 65521.0)).astype(jnp.int32)
    r = v - q * 65521
    r = jnp.where(r < 0, r + 65521, r)
    return jnp.where(r >= 65521, r - 65521, r)


def cosine(h):
    h = jnp.minimum(h, 65521 - h)
    v = (65521 - 4 * h).astype(F32) * (math.pi / (2.0 * 65521.0))
    s = v * v
    poly = jnp.full_like(s, -1.0 / 39916800.0)
    for k in (9, 7, 5, 3, 1):
        poly = poly * s + (-1.0) ** ((k - 1) // 2) / math.factorial(k)
    return poly * v


def halves(v):
    high = v.astype(BF)
    return high, (v - high.astype(F32)).astype(BF)


def bdot(a, b, dims=((1,), (0,))):
    return lax.dot_general(a, b, (dims, ((), ())), preferred_element_type=F32)


def observe_stages(nx, alpha, e_ref, i_ref, s_ref, o_ref, n_ref, parts, hot, ready, mine_s, seeds, send, recv):
    x = lax.axis_index("mem")
    rows, cells = e_ref.shape
    width = i_ref.shape[1] // nx
    step, lanes = 512, 256

    def split():
        mine_s[...] = jnp.broadcast_to(s_ref[0:1, :].astype(F32), mine_s.shape)

        def block(k, _):
            cols = pl.ds(pl.multiple_of(k * step, step), step)
            v = e_ref[:, cols]
            high, rest = halves(v)
            parts[pl.ds(0, rows), cols] = high
            parts[pl.ds(rows, rows), cols] = rest
            parts[pl.ds(2 * rows, rows), cols] = (v - high.astype(F32) - rest.astype(F32)).astype(BF)
            return 0

        lax.fori_loop(0, cells // step, block, 0)

    def predict(d):
        to = lax.rem(x + d, nx)

        def some(h, _):
            index = i_ref[:, pl.ds(pl.multiple_of(to * width + h * lanes, lanes), lanes)]

            def fill(k, _):
                at = pl.multiple_of(k * step, step)
                cell = lax.broadcasted_iota(jnp.int32, (step, lanes), 0) + at
                hot[pl.ds(at, step), :] = jnp.where(cell == index, 1.0, 0.0).astype(BF)
                return 0

            lax.fori_loop(0, cells // step, fill, 0)
            got = bdot(parts[...], hot[...])
            value = got[:rows] + got[rows : 2 * rows] + got[2 * rows :]
            ready[d, :, pl.ds(pl.multiple_of(h * lanes, lanes), lanes)] = jnp.tanh(value) + 0.5 * value
            return 0

        lax.fori_loop(0, width // lanes, some, 0)

    def copy_of(d, what):
        there = {"mem": lax.rem(x + d, nx)}
        if what:
            return remote(mine_s, seeds.at[x], send.at[1, d], recv.at[1, d], there)
        at = pl.ds(pl.multiple_of(x * rows, rows), rows)
        return remote(ready.at[d], o_ref.at[at, :], send.at[0, d], recv.at[0, d], there)

    def keep():
        o_ref[pl.ds(pl.multiple_of(x * rows, rows), rows), :] = ready[0]
        seeds[x] = mine_s[...]

    def noise():
        base = lax.axis_index(CELLS) * i_ref.shape[1] + x * width
        where = mod_prime(lax.broadcasted_iota(jnp.int32, (1, width), 1) + base)

        def block(b, _):
            at = pl.ds(pl.multiple_of(b * rows, rows), rows)
            seed = jnp.broadcast_to(seeds[b, 0:1, :], (rows, rows)).T.astype(jnp.int32)
            first = mod_prime(seed * 389)
            second = seed - 997 * jnp.floor((seed.astype(F32) + 0.5) * (1.0 / 997.0)).astype(jnp.int32) + 1
            for c in range(width // 128):
                cols = slice(128 * c, 128 * c + 128)
                n_ref[at, cols] = cosine(mod_prime(first + where[:, cols] * second)) * math.sqrt(2.0 * alpha)
            return 0

        lax.fori_loop(0, nx, block, 0)

    return split, predict, copy_of, keep, noise


def product_fills(p_ref, n_ref, ob_ref, sg_ref, gp, dp, sh, sl, mh, ml):
    members, width = p_ref.shape
    blocks = members // 128

    def prepare():
        mean = jnp.sum(p_ref[...], axis=0, keepdims=True) * (1.0 / members)
        part = pl.ds(pl.multiple_of(lax.axis_index("mem") * width, width), width)
        inv = 1.0 / sg_ref[:, part]
        scale = inv * (1.0 / math.sqrt(members - 1.0))
        shift = (ob_ref[:, part] - mean) * inv

        def block(b, _):
            rows = pl.ds(pl.multiple_of(b * 64, 64), 64)
            sh[rows, :], sl[rows, :] = halves((p_ref[rows, :] - mean) * scale)
            mh[rows, :], ml[rows, :] = halves(n_ref[rows, :] + shift)
            return 0

        lax.fori_loop(0, members // 64, block, 0)

    both = ((1,), (1,))

    def fill_d():
        def block(b, _):
            rows = pl.ds(pl.multiple_of(b * 128, 128), 128)
            within = pl.ds(pl.multiple_of(lax.rem(b, 2) * 16, 16), 16)
            d = bdot(sh[rows, :], mh[...], both) + bdot(sh[rows, :], ml[...], both) + bdot(sl[rows, :], mh[...], both)
            for c in range(blocks):
                dp[b // 2, c, within] = d[:, 128 * c : 128 * c + 128].reshape(16, 8, 128)
            return 0

        lax.fori_loop(0, blocks, block, 0)

    def fill_g():
        at = 0
        for b in range(blocks):
            rows, rest = pl.ds(128 * b, 128), pl.ds(128 * b, members - 128 * b)
            g = (
                bdot(sh[rows, :], sh[rest, :], both)
                + bdot(sl[rows, :], sh[rest, :], both)
                + bdot(sh[rows, :], sl[rest, :], both)
                + bdot(sl[rows, :], sl[rest, :], both)
            )
            for c in range(blocks - b):
                gp[pl.ds(at, 16)] = g[:, 128 * c : 128 * c + 128].reshape(16, 8, 128)
                at += 16

    return prepare, fill_d, fill_g


def all_fills(nx, alpha):
    def fills(e_ref, i_ref, s_ref, ob_ref, sg_ref, gp, dp, pred, noi, parts, hot, ready, mine_s, seeds, send, recv, *split):
        stages = observe_stages(nx, alpha, e_ref, i_ref, s_ref, pred, noi, parts, hot, ready, mine_s, seeds, send, recv)
        return stages, product_fills(pred, noi, ob_ref, sg_ref, gp, dp, *split)

    return fills


def all_scratch(rows, cells, width, nx):
    dma = pltpu.SemaphoreType.DMA
    whole = (rows * nx, width)
    return [
        pltpu.VMEM(whole, F32),
        pltpu.VMEM(whole, F32),
        pltpu.VMEM((3 * rows, cells), BF),
        pltpu.VMEM((cells, 256), BF),
        pltpu.VMEM((nx, rows, width), F32),
        pltpu.VMEM((8, rows), F32),
        pltpu.VMEM((nx, 8, rows), F32),
        dma((2, nx)),
        dma((2, nx)),
    ] + [pltpu.VMEM(whole, BF)] * 4


def reduce_kernel(n, fills, n_in, finish, *refs):
    nx, ny, nz = n
    (e_ref, out_ref, high, low, eall, eh, el, go, do, gp, dp, rg0, rd0, sg0, sd0, rg1, rd1, sg1, sd1, rg2, rd2, zs, rz, zg,
     cs, cr, xs, xr, ys, yr, zss, zsr, es, er, gs, gr, heard) = refs[n_in : n_in + 37]
    stages, (prepare, fill_d, fill_g) = fills(*refs[:n_in], gp, dp, *refs[n_in + 37 : -6])
    left, opp, right = eall.at[1], eall.at[2], eall.at[3]
    z, y, c, x = (lax.axis_index(a) for a in AXES)
    oc = 1 - c

    def xat(d):
        return lax.rem(x + d, nx)

    def yat(d):
        return lax.rem(y + d, ny)

    def zat(d):
        return lax.rem(z + d, nz)

    core = {"cells_2": oc}
    beside = [{"cells_0": zat(d)} for d in sorted({1, nz - 1} - {0})] if nz > 1 else []
    peers = (
        [{"mem": xat(d)} for d in range(1, nx)] + [{"cells_1": yat(d)} for d in range(1, ny)] + [core] + beside
    )
    barrier = pltpu.get_barrier_semaphore()
    for peer in peers:
        pl.semaphore_signal(barrier, inc=1, device_id=peer, device_id_type=MESH)
    rounds = list(range(nz // 2 - 1))

    def spread(count=1):
        for r in rounds[:count]:
            for peer in beside:
                pl.semaphore_signal(heard.at[r], inc=1, device_id=peer, device_id_type=MESH)
            pl.semaphore_wait(heard.at[r], len(beside))
        del rounds[:count]

    ox, oy, oz = order_of(nx) + [0], order_of(ny) + [0], order_of(nz)
    sent = []

    def start(copy):
        copy.start()
        sent.append(copy)
        return copy

    td, tg = rd2.shape[1], rg2.shape[1]
    q = zs.shape[0] // nz

    def g_of(core_, yq):
        return pl.ds((core_ * ny + yq) * nx * tg, nx * tg)

    half = e_ref.shape[0] // 2
    eo = {}

    def ensemble(h):
        part = e_ref.at[pl.ds(h * half, half), :]
        eo[0, h] = start(remote(part, left.at[h], es.at[0, h], er.at[0, h], {"mem": xat(1)}))
        other = e_ref.at[pl.ds((1 - h) * half, half), :]
        eo[1, h] = start(remote(other, right.at[1 - h], es.at[1, h], er.at[1, h], {"mem": xat(nx - 1)}))

    split, predict, copy_of, keep, noise = stages
    split()
    of_seeds, of_pred = [], []
    for d in ox[:-1]:
        predict(d)
        if not of_pred:
            pl.semaphore_wait(barrier, len(peers))
            of_seeds = [start(copy_of(k, True)) for k in ox[:-1]]
        of_pred.append(start(copy_of(d, False)))
    ensemble(0)
    spread()
    predict(0)
    spread()
    keep()
    for w in of_seeds:
        w.wait_recv()
    spread()
    noise()
    spread()
    for w in of_pred:
        w.wait_recv()
        spread()
    prepare()
    spread(nz)
    fill_d()
    c0d, c0g = {}, {}
    for d in ox:
        c0d[d] = start(remote(dp.at[oc, xat(d)], rd0.at[xat(d)], cs.at[0, d], cr.at[0, d], core))
    fill_g()
    for d in oy:
        c0g[d] = start(remote(gp.at[g_of(oc, yat(d))], rg0.at[yat(d)], cs.at[1, d], cr.at[1, d], core))
    d1, g1 = {}, {}
    for d in ox:
        c0d[d].wait_recv()
        sd0[xat(d)] = dp[c, xat(d)] + rd0[xat(d)]
        if d:
            d1[d] = start(remote(sd0.at[xat(d)], rd1.at[d], xs.at[0, d], xr.at[0, d], {"mem": xat(d)}))
    for d in oy:
        c0g[d].wait_recv()
        sg0[yat(d)] = gp[g_of(c, yat(d))] + rg0[yat(d)]
        if d:
            g1[d] = start(remote(sg0.at[yat(d)], rg1.at[d], ys.at[0, d], yr.at[0, d], {"cells_1": yat(d)}))
    d2, g2 = {}, {}
    for d in oy[:-1]:
        g1[d].wait_recv()
    for d in ox:
        piece = pl.ds(xat(d) * tg, tg)
        total = sg0[y, piece]
        for k in range(1, ny):
            total = total + rg1[k, piece]
        sg1[xat(d)] = total
        if d:
            g2[d] = start(remote(sg1.at[xat(d)], rg2.at[d], xs.at[1, d], xr.at[1, d], {"mem": xat(d)}))
    for d in ox[:-1]:
        d1[d].wait_recv()
    for d in oy:
        piece = pl.ds(yat(d) * td, td)
        total = sd0[x, piece]
        for k in range(1, nx):
            total = total + rd1[k, piece]
        sd1[yat(d)] = total
        if d:
            d2[d] = start(remote(sd1.at[yat(d)], rd2.at[d], ys.at[1, d], yr.at[1, d], {"cells_1": yat(d)}))
    ensemble(1)
    for t in range(td + tg, nz * q):
        zs[t] = jnp.zeros_like(zs[t])
    for d in ox[:-1]:
        g2[d].wait_recv()
    total = sg1[x]
    for k in range(1, nx):
        total = total + rg2[k]
    zs[pl.ds(td, tg)] = total
    for d in oy[:-1]:
        d2[d].wait_recv()
    total = sd1[y]
    for k in range(1, ny):
        total = total + rd2[k]
    zs[pl.ds(0, td)] = total
    z1 = [
        start(remote(zs.at[pl.ds(zat(d) * q, q)], rz.at[d], zss.at[0, d], zsr.at[0, d], {"cells_0": zat(d)})) for d in oz
    ]

    def parted(d, h):
        rows = pl.ds((2 * d + h) * half, half)

        def block(j, _):
            cols = pl.ds(pl.multiple_of(j * 512, 512), 512)
            source = eall[d, h, :, cols] if d else refs[0][pl.ds(h * half, half), cols]
            eh[rows, cols], el[rows, cols] = halves(source)
            return 0

        lax.fori_loop(0, out_ref.shape[1] // 512, block, 0)

    parted(0, 0)
    parted(0, 1)
    eo[0, 0].wait_recv()
    eo[1, 0].wait_recv()
    parted(1, 0)
    parted(3, 1)
    for w in z1:
        w.wait_recv()
    own = pl.ds(z * q, q)
    total = zs[own]
    for k in range(1, nz):
        total = total + rz[k]
    zg[own] = total
    z2 = [start(remote(zg.at[own], zg.at[own], zss.at[1, d], zsr.at[1, d], {"cells_0": zat(d)})) for d in oz]
    eo[0, 1].wait_recv()
    eo[1, 1].wait_recv()
    parted(1, 1)
    parted(3, 0)
    for w in z2:
        w.wait_recv()

    def go_of(yq):
        return pl.ds((c * ny + yq) * nx * tg, nx * tg)

    def do_of(yq):
        return pl.ds((c * ny + yq) * td, td)

    mine = pl.ds(((c * ny + y) * nx + x) * tg, tg)
    go[mine] = zg[pl.ds(td, tg)]
    do[do_of(y)] = zg[pl.ds(0, td)]
    dy, gxy = {}, {}
    for b in oy:
        for a in ox:
            if a or b:
                there = {"mem": xat(a), "cells_1": yat(b)}
                gxy[a, b] = start(remote(zg.at[pl.ds(td, tg)], go.at[mine], gs.at[b, a], gr.at[b, a], there))
    for d in oy[:-1]:
        dy[d] = start(remote(zg.at[pl.ds(0, td)], do.at[do_of(y)], ys.at[2, d], yr.at[2, d], {"cells_1": yat(d)}))
    last = [start(remote(zg.at[pl.ds(0, td)], do.at[do_of(y)], cs.at[2, 0], cr.at[2, 0], core))]
    far = [
        start(remote(left.at[0], opp.at[0], es.at[2, 0], er.at[2, 0], {"mem": xat(1)})),
        start(remote(right.at[1], opp.at[1], es.at[2, 1], er.at[2, 1], {"mem": xat(nx - 1)})),
    ]
    for d in sorted(oy[:-1]):
        dy[d].wait_recv()
        frm = do_of(yat(ny - d))
        last.append(start(remote(do.at[frm], do.at[frm], cs.at[2, d], cr.at[2, d], core)))
    for b in reversed(oy):
        for a in ox:
            if a or b:
                gxy[a, b].wait_recv()
        frm = go_of(yat(ny - b) if b else y)
        last.append(start(remote(go.at[frm], go.at[frm], cs.at[3, b], cr.at[3, b], core)))
    for w in last:
        w.wait_recv()
    finish(go, do, high, low, *refs[-6:])
    for w in far:
        w.wait_recv()
    parted(2, 0)
    parted(2, 1)
    wide = 512

    def change(j, _):
        cols = pl.ds(pl.multiple_of(j * wide, wide), wide)
        out_ref[:, cols] = (
            bdot(high[...], eh[:, cols]) + bdot(high[...], el[:, cols]) + bdot(low[...], eh[:, cols])
        )
        return 0

    lax.fori_loop(0, out_ref.shape[1] // wide, change, 0)
    for w in sent:
        w.wait_send()


def reduce_all(inputs, fills, extra, finish, result, more, e, tg, td, nx, ny, nz):
    q = -(-(tg + td) // nz)
    tile = (8, 128)
    m = max(nx, ny)
    half = (2, e.shape[0] // 2, e.shape[1])
    dma = pltpu.SemaphoreType.DMA

    def tiles(*lead):
        return pltpu.VMEM((*lead, *tile), F32)

    return pl.pallas_call(
        functools.partial(reduce_kernel, (nx, ny, nz), fills, len(inputs), finish),
        out_shape=jax.ShapeDtypeStruct(e.shape, F32),
        in_specs=[VM] * len(inputs) + [ANY],
        out_specs=VM,
        scratch_shapes=[
            result,
            result,
            pltpu.VMEM((nx, *half), F32),
            pltpu.VMEM((nx * e.shape[0], e.shape[1]), BF),
            pltpu.VMEM((nx * e.shape[0], e.shape[1]), BF),
            tiles(2 * ny * nx * tg),
            tiles(2 * ny * td),
            tiles(2 * ny * nx * tg),
            tiles(2, nx, ny * td),
            tiles(ny, nx * tg),
            tiles(nx, ny * td),
            tiles(ny, nx * tg),
            tiles(nx, ny * td),
            tiles(ny, nx * tg),
            tiles(nx, ny * td),
            tiles(nx, tg),
            tiles(ny, td),
            tiles(nx, tg),
            tiles(ny, td),
            tiles(nz * q),
            tiles(nz, q),
            tiles(nz * q),
            dma((4, m)), dma((4, m)), dma((3, nx)), dma((3, nx)), dma((4, ny)), dma((4, ny)), dma((2, nz)), dma((2, nz)),
            dma((3, 2)), dma((3, 2)), dma((ny, nx)), dma((ny, nx)), pltpu.SemaphoreType.REGULAR((max(nz // 2 - 1, 1),)),
            *extra,
            *more,
        ],
        compiler_params=pltpu.CompilerParams(collective_id=1, has_side_effects=True),
        name="reduce_all",
    )(*inputs, e)


def factor_block(n_ref, low_ref, solved_ref, zero, span=4):
    lane = lax.broadcasted_iota(jnp.int32, (8, 128), 1)
    sub = lax.broadcasted_iota(jnp.int32, (8, 128), 0)

    def lb(v, c):
        return jnp.broadcast_to(v[:, c : c + 1], (8, 128))

    def sb(v, k):
        return jnp.broadcast_to(v[k : k + 1, :], (8, 128))

    for first in range(0, 16, span):
        end = 8 * (first + span)
        n = {i: n_ref[pl.ds(8 * i, 8), :] for i in range(first, first + span)}
        before, after = [], []
        for p in range(first, first + span):
            base = 8 * p
            cur = n[p]
            before.append(jnp.where(lane >= end, cur, 0.0))
            low_ref[pl.ds(base, 8), :] = jnp.where(lane < base, cur, jnp.where(lane == base + sub, 1.0, 0.0))
            t = [lb(cur, base + k) + zero for k in range(8)]
            for k in range(0, 8, 2):
                t0, t1 = t[k], t[k + 1]
                aa, ab, bb = sb(t0, k), sb(t1, k), sb(t1, k + 1)
                rec = 1.0 / (aa * bb - ab * ab)
                pair = (sub == k) | (sub == k + 1)
                top = sub == k
                x0, x1 = jnp.where(pair, 0.0, t0), jnp.where(pair, 0.0, t1)
                s0, s1 = lane == base + k, lane == base + k + 1
                r0 = jnp.where(s0, 1.0, jnp.where(s1, 0.0, sb(cur, k)))
                r1 = jnp.where(s1, 1.0, jnp.where(s0, 0.0, sb(cur, k + 1)))
                n0, n1 = bb * r0 - ab * r1, aa * r1 - ab * r0
                cur = jnp.where(pair, 0.0, jnp.where(s0 | s1, 0.0, cur)) - jnp.where(
                    pair, -jnp.where(top, n0, n1), x0 * n0 + x1 * n1
                ) * rec
                for q in range(k + 2, 8):
                    r0, r1 = sb(t[q], k), sb(t[q], k + 1)
                    n0, n1 = bb * r0 - ab * r1, aa * r1 - ab * r0
                    t[q] = jnp.where(pair, 0.0, t[q]) - jnp.where(pair, -jnp.where(top, n0, n1), x0 * n0 + x1 * n1) * rec
            solved_ref[pl.ds(base, 8), :] = jnp.where(lane < base + 8, cur, 0.0)
            after.append(jnp.where((lane >= base + 8) & (lane < end), 0.0, cur))
            rows = [sb(cur, k) for k in range(8)]
            inside = (lane >= base) & (lane < base + 8)
            for i in range(p + 1, first + span):
                acc = jnp.where(inside, 0.0, n[i])
                for k in range(8):
                    acc = acc - lb(n[i], base + k) * rows[k]
                n[i] = acc
        if end < 128:
            b = jnp.concatenate(before, axis=0)
            f = jnp.concatenate(after, axis=0)
            change = lax.dot_general(b, f, (((0,), (0,)), ((), ())), precision=HI, preferred_element_type=jnp.float32)
            keep = (lane < 8 * first) | (lane >= end)
            for i in range(first + span, 16):
                at = pl.ds(8 * i, 8)
                n_ref[at, :] = jnp.where(keep, n_ref[at, :], 0.0) - change[8 * i : 8 * i + 8]

def mm(a, b, ta=False):
    dn = (((0,), (0,)), ((), ())) if ta else (((1,), (0,)), ((), ()))
    return lax.dot_general(a, b, dn, precision=HI, preferred_element_type=F32)


def solve_kernel(alpha, g_ref, d_ref, high_ref, low_ref, a, dg, li, u, w, zero):
    nb = dg.shape[0]
    n = nb * 128
    x = lax.axis_index("mem")
    r = lax.broadcasted_iota(jnp.int32, (128, 128), 0)
    c = lax.broadcasted_iota(jnp.int32, (128, 128), 1)
    zero[...] = jnp.zeros_like(zero)
    first = 0
    for i in range(nb):
        for j in range(i, nb):
            blk = g_ref[pl.ds(first, 16)].reshape(128, 128)
            first += 16
            if i == j:
                dg[i] = blk + jnp.where(r == c, alpha, 0.0)
            else:
                a[i, :, pl.ds(128 * j, 128)] = blk
    unit = jnp.where(r == c, alpha * math.sqrt(n - 1.0), 0.0)
    for i in range(nb):
        a[i, :, pl.ds(n, 128)] = d_ref[pl.ds(16 * i, 16)].reshape(128, 128) + jnp.where(x == i, unit, 0.0)

    def step(b, _):
        factor_block(dg.at[b], li.at[b], u, zero[...])
        for s in range(nb):

            @pl.when(b == s)
            def _():
                cols = a[s, :, pl.ds(128 * (s + 1), 128 * (nb - s))]
                us = mm(li[s], cols)
                ws = mm(u[...], cols)
                w[s, :, pl.ds(128 * (s + 1), 128 * (nb - s))] = ws
                for i in range(s + 1, nb):
                    at = 128 * (i - s - 1)
                    change = mm(us[:, at : at + 128], ws[:, at:], True)
                    dg[i] = dg[i] - change[:, :128]
                    rest = pl.ds(128 * (i + 1), 128 * (nb - i))
                    a[i, :, rest] = a[i, :, rest] - change[:, 128:]

        return 0

    lax.fori_loop(0, nb, step, 0)
    xs = [None] * nb
    for s in reversed(range(nb)):
        acc = w[s, :, pl.ds(n, 128)]
        if s < nb - 1:
            acc = acc - mm(w[s, :, pl.ds(128 * (s + 1), 128 * (nb - 1 - s))], jnp.concatenate(xs[s + 1 :], axis=0))
        xs[s] = mm(li[s], acc, True)
    tot = sum(jnp.sum(v, axis=0, keepdims=True) for v in xs) * (1.0 / n)
    for s in range(nb):
        at = pl.ds(pl.multiple_of(lax.rem(x + nb - s, nb) * 128, 128), 128)
        high_ref[:, at], low_ref[:, at] = halves(((xs[s] - tot) * (1.0 / math.sqrt(n - 1.0)) + 1.0 / n).T)


def solve_scratch(nb):
    block = (128, 128)
    wide = pltpu.VMEM((nb, 128, 128 * (nb + 1)), F32)
    return [
        wide,
        pltpu.VMEM((nb, *block), F32),
        pltpu.VMEM((nb, *block), F32),
        pltpu.VMEM(block, F32),
        wide,
        pltpu.VMEM((8, 128), F32),
    ]


def shards(ensemble, observed, obs_sigma, obs_index, member_seeds):
    alpha = PLAN[SECTION]
    nx, ny, nz = (lax.axis_size(a) for a in ("mem", "cells_1", "cells_0"))
    own = ensemble.shape[0]
    blocks = own * nx // 128
    width = obs_index.shape[0] // nx
    return reduce_all(
        (ensemble, obs_index[None, :], member_seeds[None, :], observed[None, :], obs_sigma[None, :]),
        all_fills(nx, alpha),
        all_scratch(own, ensemble.shape[1], width, nx),
        functools.partial(solve_kernel, alpha),
        pltpu.VMEM((128, 128 * blocks), BF),
        solve_scratch(blocks),
        ensemble,
        16 * blocks * (blocks + 1) // 2 // (2 * ny * nx),
        16 * blocks // (2 * ny),
        nx,
        ny,
        nz,
    )


def solution(mesh):
    finer = Mesh(mesh.devices.reshape(16, 4, 2, mesh.shape["mem"]), AXES)
    placed = (P("mem", CELLS), P(CELLS), P(CELLS), P(CELLS), P("mem"))
    return jax.shard_map(shards, mesh=finer, in_specs=placed, out_specs=P("mem", CELLS), check_vma=False)
```

```python
import functools
import math

import jax
import jax.numpy as jnp
from jax import lax
from jax.experimental import pallas as pl
from jax.experimental.pallas import tpu as pltpu
from jax.sharding import Mesh
from jax.sharding import PartitionSpec as P

SECTION = 1
CELLS = ("cells_0", "cells_1", "cells_2")
AXES = ("cells_0", "cells_1", "cells_2", "mem")
PLAN = (28.0 / 3.0, 7.0, 4.0, 2.0)
HI = lax.Precision.HIGHEST
BF = jnp.bfloat16
MESH = pl.DeviceIdType.MESH
VM = pl.BlockSpec(memory_space=pltpu.VMEM)
ANY = pl.BlockSpec(memory_space=pl.ANY)
F32 = jnp.float32


def remote(src, dst, send, recv, where):
    return pltpu.make_async_remote_copy(
        src_ref=src, dst_ref=dst, send_sem=send, recv_sem=recv, device_id=where, device_id_type=MESH
    )


def at_axis(axis, index):
    return {axis: index}


def greet(peers):
    barrier = pltpu.get_barrier_semaphore()
    for peer in peers:
        pl.semaphore_signal(barrier, inc=1, device_id=peer, device_id_type=MESH)
    pl.semaphore_wait(barrier, len(peers))


def order_of(n):
    return sorted(range(1, n), key=lambda d: -min(d, n - d))


def mod_prime(v):
    q = jnp.floor(v.astype(F32) * (1.0 / 65521.0)).astype(jnp.int32)
    r = v - q * 65521
    r = jnp.where(r < 0, r + 65521, r)
    return jnp.where(r >= 65521, r - 65521, r)


def cosine(h):
    h = jnp.minimum(h, 65521 - h)
    v = (65521 - 4 * h).astype(F32) * (math.pi / (2.0 * 65521.0))
    s = v * v
    poly = jnp.full_like(s, -1.0 / 39916800.0)
    for k in (9, 7, 5, 3, 1):
        poly = poly * s + (-1.0) ** ((k - 1) // 2) / math.factorial(k)
    return poly * v


def halves(v):
    high = v.astype(BF)
    return high, (v - high.astype(F32)).astype(BF)


def bdot(a, b, dims=((1,), (0,))):
    return lax.dot_general(a, b, (dims, ((), ())), preferred_element_type=F32)


def observe_stages(nx, alpha, e_ref, i_ref, s_ref, o_ref, n_ref, parts, hot, ready, mine_s, seeds, send, recv):
    x = lax.axis_index("mem")
    rows, cells = e_ref.shape
    width = i_ref.shape[1] // nx
    step, lanes = 512, 256

    def split():
        mine_s[...] = jnp.broadcast_to(s_ref[0:1, :].astype(F32), mine_s.shape)

        def block(k, _):
            cols = pl.ds(pl.multiple_of(k * step, step), step)
            v = e_ref[:, cols]
            high, rest = halves(v)
            parts[pl.ds(0, rows), cols] = high
            parts[pl.ds(rows, rows), cols] = rest
            parts[pl.ds(2 * rows, rows), cols] = (v - high.astype(F32) - rest.astype(F32)).astype(BF)
            return 0

        lax.fori_loop(0, cells // step, block, 0)

    def predict(d):
        to = lax.rem(x + d, nx)

        def some(h, _):
            index = i_ref[:, pl.ds(pl.multiple_of(to * width + h * lanes, lanes), lanes)]

            def fill(k, _):
                at = pl.multiple_of(k * step, step)
                cell = lax.broadcasted_iota(jnp.int32, (step, lanes), 0) + at
                hot[pl.ds(at, step), :] = jnp.where(cell == index, 1.0, 0.0).astype(BF)
                return 0

            lax.fori_loop(0, cells // step, fill, 0)
            got = bdot(parts[...], hot[...])
            value = got[:rows] + got[rows : 2 * rows] + got[2 * rows :]
            ready[d, :, pl.ds(pl.multiple_of(h * lanes, lanes), lanes)] = jnp.tanh(value) + 0.5 * value
            return 0

        lax.fori_loop(0, width // lanes, some, 0)

    def copy_of(d, what):
        there = {"mem": lax.rem(x + d, nx)}
        if what:
            return remote(mine_s, seeds.at[x], send.at[1, d], recv.at[1, d], there)
        at = pl.ds(pl.multiple_of(x * rows, rows), rows)
        return remote(ready.at[d], o_ref.at[at, :], send.at[0, d], recv.at[0, d], there)

    def keep():
        o_ref[pl.ds(pl.multiple_of(x * rows, rows), rows), :] = ready[0]
        seeds[x] = mine_s[...]

    def noise():
        base = lax.axis_index(CELLS) * i_ref.shape[1] + x * width
        where = mod_prime(lax.broadcasted_iota(jnp.int32, (1, width), 1) + base)

        def block(b, _):
            at = pl.ds(pl.multiple_of(b * rows, rows), rows)
            seed = jnp.broadcast_to(seeds[b, 0:1, :], (rows, rows)).T.astype(jnp.int32)
            first = mod_prime(seed * 389)
            second = seed - 997 * jnp.floor((seed.astype(F32) + 0.5) * (1.0 / 997.0)).astype(jnp.int32) + 1
            for c in range(width // 128):
                cols = slice(128 * c, 128 * c + 128)
                n_ref[at, cols] = cosine(mod_prime(first + where[:, cols] * second)) * math.sqrt(2.0 * alpha)
            return 0

        lax.fori_loop(0, nx, block, 0)

    return split, predict, copy_of, keep, noise


def product_fills(p_ref, n_ref, ob_ref, sg_ref, gp, dp, sh, sl, mh, ml):
    members, width = p_ref.shape
    blocks = members // 128

    def prepare():
        mean = jnp.sum(p_ref[...], axis=0, keepdims=True) * (1.0 / members)
        part = pl.ds(pl.multiple_of(lax.axis_index("mem") * width, width), width)
        inv = 1.0 / sg_ref[:, part]
        scale = inv * (1.0 / math.sqrt(members - 1.0))
        shift = (ob_ref[:, part] - mean) * inv

        def block(b, _):
            rows = pl.ds(pl.multiple_of(b * 64, 64), 64)
            sh[rows, :], sl[rows, :] = halves((p_ref[rows, :] - mean) * scale)
            mh[rows, :], ml[rows, :] = halves(n_ref[rows, :] + shift)
            return 0

        lax.fori_loop(0, members // 64, block, 0)

    both = ((1,), (1,))

    def fill_d(part):
        def block(k, _):
            b = 2 * part + k
            rows = pl.ds(pl.multiple_of(b * 128, 128), 128)
            within = pl.ds(pl.multiple_of(lax.rem(b, 2) * 16, 16), 16)
            d = bdot(sh[rows, :], mh[...], both) + bdot(sh[rows, :], ml[...], both) + bdot(sl[rows, :], mh[...], both)
            for c in range(blocks):
                dp[b // 2, c, within] = d[:, 128 * c : 128 * c + 128].reshape(16, 8, 128)
            return 0

        lax.fori_loop(0, blocks // 2, block, 0)

    def fill_g():
        at = 0
        for b in range(blocks):
            rows, rest = pl.ds(128 * b, 128), pl.ds(128 * b, members - 128 * b)
            g = (
                bdot(sh[rows, :], sh[rest, :], both)
                + bdot(sl[rows, :], sh[rest, :], both)
                + bdot(sh[rows, :], sl[rest, :], both)
                + bdot(sl[rows, :], sl[rest, :], both)
            )
            for c in range(blocks - b):
                gp[pl.ds(at, 16)] = g[:, 128 * c : 128 * c + 128].reshape(16, 8, 128)
                at += 16

    return prepare, fill_d, fill_g


def all_fills(nx, alpha):
    def fills(e_ref, i_ref, s_ref, ob_ref, sg_ref, gp, dp, pred, noi, parts, hot, ready, mine_s, seeds, send, recv, *split):
        stages = observe_stages(nx, alpha, e_ref, i_ref, s_ref, pred, noi, parts, hot, ready, mine_s, seeds, send, recv)
        return stages, product_fills(pred, noi, ob_ref, sg_ref, gp, dp, *split)

    return fills


def all_scratch(rows, cells, width, nx):
    dma = pltpu.SemaphoreType.DMA
    whole = (rows * nx, width)
    return [
        pltpu.VMEM(whole, F32),
        pltpu.VMEM(whole, F32),
        pltpu.VMEM((3 * rows, cells), BF),
        pltpu.VMEM((cells, 256), BF),
        pltpu.VMEM((nx, rows, width), F32),
        pltpu.VMEM((8, rows), F32),
        pltpu.VMEM((nx, 8, rows), F32),
        dma((2, nx)),
        dma((2, nx)),
    ] + [pltpu.VMEM(whole, BF)] * 4


def reduce_kernel(n, fills, n_in, finish, *refs):
    nx, ny, nz = n
    (e_ref, out_ref, high, low, eall, eh, el, go, do, gp, dp, rg0, rd0, sg0, sd0, rg1, rd1, sg1, sd1, rg2, rd2, zs, rz, zg,
     cs, cr, xs, xr, ys, yr, zss, zsr, es, er, gs, gr, heard) = refs[n_in : n_in + 37]
    stages, (prepare, fill_d, fill_g) = fills(*refs[:n_in], gp, dp, *refs[n_in + 37 : -6])
    left, opp, right = eall.at[1], eall.at[2], eall.at[3]
    z, y, c, x = (lax.axis_index(a) for a in AXES)
    oc = 1 - c

    def xat(d):
        return lax.rem(x + d, nx)

    def yat(d):
        return lax.rem(y + d, ny)

    def zat(d):
        return lax.rem(z + d, nz)

    core = {"cells_2": oc}
    beside = [{"cells_0": zat(d)} for d in sorted({1, nz - 1} - {0})] if nz > 1 else []
    peers = (
        [{"mem": xat(d)} for d in range(1, nx)] + [{"cells_1": yat(d)} for d in range(1, ny)] + [core] + beside
    )
    barrier = pltpu.get_barrier_semaphore()
    for peer in peers:
        pl.semaphore_signal(barrier, inc=1, device_id=peer, device_id_type=MESH)
    rounds = list(range(nz // 2 - 1))

    def spread(count=1):
        for r in rounds[:count]:
            for peer in beside:
                pl.semaphore_signal(heard.at[r], inc=1, device_id=peer, device_id_type=MESH)
            pl.semaphore_wait(heard.at[r], len(beside))
        del rounds[:count]

    ox, oy, oz = order_of(nx) + [0], order_of(ny) + [0], order_of(nz)
    sent = []

    def start(copy):
        copy.start()
        sent.append(copy)
        return copy

    td, tg = rd2.shape[1], rg2.shape[1]
    q = zs.shape[0] // nz

    def g_of(core_, yq):
        return pl.ds((core_ * ny + yq) * nx * tg, nx * tg)

    half = e_ref.shape[0] // 2
    eo = {}

    def ensemble(h):
        part = e_ref.at[pl.ds(h * half, half), :]
        eo[0, h] = start(remote(part, left.at[h], es.at[0, h], er.at[0, h], {"mem": xat(1)}))
        other = e_ref.at[pl.ds((1 - h) * half, half), :]
        eo[1, h] = start(remote(other, right.at[1 - h], es.at[1, h], er.at[1, h], {"mem": xat(nx - 1)}))

    split, predict, copy_of, keep, noise = stages
    split()
    of_seeds, of_pred = [], []
    for d in ox[:-1]:
        predict(d)
        if not of_pred:
            pl.semaphore_wait(barrier, len(peers))
            of_seeds = [start(copy_of(k, True)) for k in ox[:-1]]
        of_pred.append(start(copy_of(d, False)))
    ensemble(0)
    spread()
    predict(0)
    spread()
    keep()
    for w in of_seeds:
        w.wait_recv()
    spread()
    noise()
    spread()
    for w in of_pred:
        w.wait_recv()
        spread()
    prepare()
    spread(nz)
    fill_d(oc)
    c0d, c0g = {}, {}
    for d in ox:
        c0d[d] = start(remote(dp.at[oc, xat(d)], rd0.at[xat(d)], cs.at[0, d], cr.at[0, d], core))
    fill_d(c)
    fill_g()
    for d in oy:
        c0g[d] = start(remote(gp.at[g_of(oc, yat(d))], rg0.at[yat(d)], cs.at[1, d], cr.at[1, d], core))
    d1, g1 = {}, {}
    for d in ox:
        c0d[d].wait_recv()
        sd0[xat(d)] = dp[c, xat(d)] + rd0[xat(d)]
        if d:
            d1[d] = start(remote(sd0.at[xat(d)], rd1.at[d], xs.at[0, d], xr.at[0, d], {"mem": xat(d)}))
    for d in oy:
        c0g[d].wait_recv()
        sg0[yat(d)] = gp[g_of(c, yat(d))] + rg0[yat(d)]
        if d:
            g1[d] = start(remote(sg0.at[yat(d)], rg1.at[d], ys.at[0, d], yr.at[0, d], {"cells_1": yat(d)}))
    d2, g2 = {}, {}
    for d in oy[:-1]:
        g1[d].wait_recv()
    for d in ox:
        piece = pl.ds(xat(d) * tg, tg)
        total = sg0[y, piece]
        for k in range(1, ny):
            total = total + rg1[k, piece]
        sg1[xat(d)] = total
        if d:
            g2[d] = start(remote(sg1.at[xat(d)], rg2.at[d], xs.at[1, d], xr.at[1, d], {"mem": xat(d)}))
    for d in ox[:-1]:
        d1[d].wait_recv()
    for d in oy:
        piece = pl.ds(yat(d) * td, td)
        total = sd0[x, piece]
        for k in range(1, nx):
            total = total + rd1[k, piece]
        sd1[yat(d)] = total
        if d:
            d2[d] = start(remote(sd1.at[yat(d)], rd2.at[d], ys.at[1, d], yr.at[1, d], {"cells_1": yat(d)}))
    ensemble(1)
    for t in range(td + tg, nz * q):
        zs[t] = jnp.zeros_like(zs[t])
    for d in ox[:-1]:
        g2[d].wait_recv()
    total = sg1[x]
    for k in range(1, nx):
        total = total + rg2[k]
    zs[pl.ds(td, tg)] = total
    for d in oy[:-1]:
        d2[d].wait_recv()
    total = sd1[y]
    for k in range(1, ny):
        total = total + rd2[k]
    zs[pl.ds(0, td)] = total
    z1 = [
        start(remote(zs.at[pl.ds(zat(d) * q, q)], rz.at[d], zss.at[0, d], zsr.at[0, d], {"cells_0": zat(d)})) for d in oz
    ]

    def parted(d, h):
        rows = pl.ds((2 * d + h) * half, half)

        def block(j, _):
            cols = pl.ds(pl.multiple_of(j * 512, 512), 512)
            source = eall[d, h, :, cols] if d else refs[0][pl.ds(h * half, half), cols]
            eh[rows, cols], el[rows, cols] = halves(source)
            return 0

        lax.fori_loop(0, out_ref.shape[1] // 512, block, 0)

    parted(0, 0)
    parted(0, 1)
    eo[0, 0].wait_recv()
    eo[1, 0].wait_recv()
    parted(1, 0)
    parted(3, 1)
    for w in z1:
        w.wait_recv()
    own = pl.ds(z * q, q)
    total = zs[own]
    for k in range(1, nz):
        total = total + rz[k]
    zg[own] = total
    z2 = [start(remote(zg.at[own], zg.at[own], zss.at[1, d], zsr.at[1, d], {"cells_0": zat(d)})) for d in oz]
    eo[0, 1].wait_recv()
    eo[1, 1].wait_recv()
    parted(1, 1)
    parted(3, 0)
    for w in z2:
        w.wait_recv()

    def go_of(yq):
        return pl.ds((c * ny + yq) * nx * tg, nx * tg)

    def do_of(yq):
        return pl.ds((c * ny + yq) * td, td)

    mine = pl.ds(((c * ny + y) * nx + x) * tg, tg)
    go[mine] = zg[pl.ds(td, tg)]
    do[do_of(y)] = zg[pl.ds(0, td)]
    dy, gxy = {}, {}
    for b in oy:
        for a in ox:
            if a or b:
                there = {"mem": xat(a), "cells_1": yat(b)}
                gxy[a, b] = start(remote(zg.at[pl.ds(td, tg)], go.at[mine], gs.at[b, a], gr.at[b, a], there))
    for d in oy[:-1]:
        dy[d] = start(remote(zg.at[pl.ds(0, td)], do.at[do_of(y)], ys.at[2, d], yr.at[2, d], {"cells_1": yat(d)}))
    last = [start(remote(zg.at[pl.ds(0, td)], do.at[do_of(y)], cs.at[2, 0], cr.at[2, 0], core))]
    far = [
        start(remote(left.at[0], opp.at[0], es.at[2, 0], er.at[2, 0], {"mem": xat(1)})),
        start(remote(right.at[1], opp.at[1], es.at[2, 1], er.at[2, 1], {"mem": xat(nx - 1)})),
    ]
    for d in sorted(oy[:-1]):
        dy[d].wait_recv()
        frm = do_of(yat(ny - d))
        last.append(start(remote(do.at[frm], do.at[frm], cs.at[2, d], cr.at[2, d], core)))
    for b in reversed(oy):
        for a in ox:
            if a or b:
                gxy[a, b].wait_recv()
        frm = go_of(yat(ny - b) if b else y)
        last.append(start(remote(go.at[frm], go.at[frm], cs.at[3, b], cr.at[3, b], core)))
    for w in last:
        w.wait_recv()
    finish(go, do, high, low, *refs[-6:])
    for w in far:
        w.wait_recv()
    parted(2, 0)
    parted(2, 1)
    wide = 512

    def change(j, _):
        cols = pl.ds(pl.multiple_of(j * wide, wide), wide)
        out_ref[:, cols] = (
            bdot(high[...], eh[:, cols]) + bdot(high[...], el[:, cols]) + bdot(low[...], eh[:, cols])
        )
        return 0

    lax.fori_loop(0, out_ref.shape[1] // wide, change, 0)
    for w in sent:
        w.wait_send()


def reduce_all(inputs, fills, extra, finish, result, more, e, tg, td, nx, ny, nz):
    q = -(-(tg + td) // nz)
    tile = (8, 128)
    m = max(nx, ny)
    half = (2, e.shape[0] // 2, e.shape[1])
    dma = pltpu.SemaphoreType.DMA

    def tiles(*lead):
        return pltpu.VMEM((*lead, *tile), F32)

    return pl.pallas_call(
        functools.partial(reduce_kernel, (nx, ny, nz), fills, len(inputs), finish),
        out_shape=jax.ShapeDtypeStruct(e.shape, F32),
        in_specs=[VM] * len(inputs) + [ANY],
        out_specs=VM,
        scratch_shapes=[
            result,
            result,
            pltpu.VMEM((nx, *half), F32),
            pltpu.VMEM((nx * e.shape[0], e.shape[1]), BF),
            pltpu.VMEM((nx * e.shape[0], e.shape[1]), BF),
            tiles(2 * ny * nx * tg),
            tiles(2 * ny * td),
            tiles(2 * ny * nx * tg),
            tiles(2, nx, ny * td),
            tiles(ny, nx * tg),
            tiles(nx, ny * td),
            tiles(ny, nx * tg),
            tiles(nx, ny * td),
            tiles(ny, nx * tg),
            tiles(nx, ny * td),
            tiles(nx, tg),
            tiles(ny, td),
            tiles(nx, tg),
            tiles(ny, td),
            tiles(nz * q),
            tiles(nz, q),
            tiles(nz * q),
            dma((4, m)), dma((4, m)), dma((3, nx)), dma((3, nx)), dma((4, ny)), dma((4, ny)), dma((2, nz)), dma((2, nz)),
            dma((3, 2)), dma((3, 2)), dma((ny, nx)), dma((ny, nx)), pltpu.SemaphoreType.REGULAR((max(nz // 2 - 1, 1),)),
            *extra,
            *more,
        ],
        compiler_params=pltpu.CompilerParams(collective_id=1, has_side_effects=True),
        name="reduce_all",
    )(*inputs, e)


def factor_block(n_ref, low_ref, solved_ref, zero, span=4):
    lane = lax.broadcasted_iota(jnp.int32, (8, 128), 1)
    sub = lax.broadcasted_iota(jnp.int32, (8, 128), 0)

    def lb(v, c):
        return jnp.broadcast_to(v[:, c : c + 1], (8, 128))

    def sb(v, k):
        return jnp.broadcast_to(v[k : k + 1, :], (8, 128))

    for first in range(0, 16, span):
        end = 8 * (first + span)
        n = {i: n_ref[pl.ds(8 * i, 8), :] for i in range(first, first + span)}
        before, after = [], []
        for p in range(first, first + span):
            base = 8 * p
            cur = n[p]
            before.append(jnp.where(lane >= end, cur, 0.0))
            low_ref[pl.ds(base, 8), :] = jnp.where(lane < base, cur, jnp.where(lane == base + sub, 1.0, 0.0))
            t = [lb(cur, base + k) + zero for k in range(8)]
            for k in range(0, 8, 2):
                t0, t1 = t[k], t[k + 1]
                aa, ab, bb = sb(t0, k), sb(t1, k), sb(t1, k + 1)
                rec = 1.0 / (aa * bb - ab * ab)
                pair = (sub == k) | (sub == k + 1)
                top = sub == k
                x0, x1 = jnp.where(pair, 0.0, t0), jnp.where(pair, 0.0, t1)
                s0, s1 = lane == base + k, lane == base + k + 1
                r0 = jnp.where(s0, 1.0, jnp.where(s1, 0.0, sb(cur, k)))
                r1 = jnp.where(s1, 1.0, jnp.where(s0, 0.0, sb(cur, k + 1)))
                n0, n1 = bb * r0 - ab * r1, aa * r1 - ab * r0
                cur = jnp.where(pair, 0.0, jnp.where(s0 | s1, 0.0, cur)) - jnp.where(
                    pair, -jnp.where(top, n0, n1), x0 * n0 + x1 * n1
                ) * rec
                for q in range(k + 2, 8):
                    r0, r1 = sb(t[q], k), sb(t[q], k + 1)
                    n0, n1 = bb * r0 - ab * r1, aa * r1 - ab * r0
                    t[q] = jnp.where(pair, 0.0, t[q]) - jnp.where(pair, -jnp.where(top, n0, n1), x0 * n0 + x1 * n1) * rec
            solved_ref[pl.ds(base, 8), :] = jnp.where(lane < base + 8, cur, 0.0)
            after.append(jnp.where((lane >= base + 8) & (lane < end), 0.0, cur))
            rows = [sb(cur, k) for k in range(8)]
            inside = (lane >= base) & (lane < base + 8)
            for i in range(p + 1, first + span):
                acc = jnp.where(inside, 0.0, n[i])
                for k in range(8):
                    acc = acc - lb(n[i], base + k) * rows[k]
                n[i] = acc
        if end < 128:
            b = jnp.concatenate(before, axis=0)
            f = jnp.concatenate(after, axis=0)
            change = lax.dot_general(b, f, (((0,), (0,)), ((), ())), precision=HI, preferred_element_type=jnp.float32)
            keep = (lane < 8 * first) | (lane >= end)
            for i in range(first + span, 16):
                at = pl.ds(8 * i, 8)
                n_ref[at, :] = jnp.where(keep, n_ref[at, :], 0.0) - change[8 * i : 8 * i + 8]

def mm(a, b, ta=False):
    dn = (((0,), (0,)), ((), ())) if ta else (((1,), (0,)), ((), ()))
    return lax.dot_general(a, b, dn, precision=HI, preferred_element_type=F32)


def solve_kernel(alpha, g_ref, d_ref, high_ref, low_ref, a, dg, li, u, w, zero):
    nb = dg.shape[0]
    n = nb * 128
    x = lax.axis_index("mem")
    r = lax.broadcasted_iota(jnp.int32, (128, 128), 0)
    c = lax.broadcasted_iota(jnp.int32, (128, 128), 1)
    zero[...] = jnp.zeros_like(zero)
    first = 0
    for i in range(nb):
        for j in range(i, nb):
            blk = g_ref[pl.ds(first, 16)].reshape(128, 128)
            first += 16
            if i == j:
                dg[i] = blk + jnp.where(r == c, alpha, 0.0)
            else:
                a[i, :, pl.ds(128 * j, 128)] = blk
    unit = jnp.where(r == c, alpha * math.sqrt(n - 1.0), 0.0)
    for i in range(nb):
        a[i, :, pl.ds(n, 128)] = d_ref[pl.ds(16 * i, 16)].reshape(128, 128) + jnp.where(x == i, unit, 0.0)

    def step(b, _):
        factor_block(dg.at[b], li.at[b], u, zero[...])
        for s in range(nb):

            @pl.when(b == s)
            def _():
                cols = a[s, :, pl.ds(128 * (s + 1), 128 * (nb - s))]
                us = mm(li[s], cols)
                ws = mm(u[...], cols)
                w[s, :, pl.ds(128 * (s + 1), 128 * (nb - s))] = ws
                for i in range(s + 1, nb):
                    at = 128 * (i - s - 1)
                    change = mm(us[:, at : at + 128], ws[:, at:], True)
                    dg[i] = dg[i] - change[:, :128]
                    rest = pl.ds(128 * (i + 1), 128 * (nb - i))
                    a[i, :, rest] = a[i, :, rest] - change[:, 128:]

        return 0

    lax.fori_loop(0, nb, step, 0)
    xs = [None] * nb
    for s in reversed(range(nb)):
        acc = w[s, :, pl.ds(n, 128)]
        if s < nb - 1:
            acc = acc - mm(w[s, :, pl.ds(128 * (s + 1), 128 * (nb - 1 - s))], jnp.concatenate(xs[s + 1 :], axis=0))
        xs[s] = mm(li[s], acc, True)
    tot = sum(jnp.sum(v, axis=0, keepdims=True) for v in xs) * (1.0 / n)
    for s in range(nb):
        at = pl.ds(pl.multiple_of(lax.rem(x + nb - s, nb) * 128, 128), 128)
        high_ref[:, at], low_ref[:, at] = halves(((xs[s] - tot) * (1.0 / math.sqrt(n - 1.0)) + 1.0 / n).T)


def solve_scratch(nb):
    block = (128, 128)
    wide = pltpu.VMEM((nb, 128, 128 * (nb + 1)), F32)
    return [
        wide,
        pltpu.VMEM((nb, *block), F32),
        pltpu.VMEM((nb, *block), F32),
        pltpu.VMEM(block, F32),
        wide,
        pltpu.VMEM((8, 128), F32),
    ]


def place_kernel(v_ref, out_ref):
    out_ref[...] = v_ref[...]


def place(v):
    rows, width = v.shape
    block = pl.BlockSpec((rows // 2, width), lambda i: (i, 0))
    return pl.pallas_call(
        place_kernel,
        grid=(2,),
        out_shape=jax.ShapeDtypeStruct(v.shape, F32),
        in_specs=[block],
        out_specs=block,
        name="place",
    )(v)


def shards(ensemble, observed, obs_sigma, obs_index, member_seeds):
    alpha = PLAN[SECTION]
    nx, ny, nz = (lax.axis_size(a) for a in ("mem", "cells_1", "cells_0"))
    own = ensemble.shape[0]
    blocks = own * nx // 128
    width = obs_index.shape[0] // nx
    changed = reduce_all(
        (ensemble, obs_index[None, :], member_seeds[None, :], observed[None, :], obs_sigma[None, :]),
        all_fills(nx, alpha),
        all_scratch(own, ensemble.shape[1], width, nx),
        functools.partial(solve_kernel, alpha),
        pltpu.VMEM((128, 128 * blocks), BF),
        solve_scratch(blocks),
        ensemble,
        16 * blocks * (blocks + 1) // 2 // (2 * ny * nx),
        16 * blocks // (2 * ny),
        nx,
        ny,
        nz,
    )
    return place(changed)


def solution(mesh):
    finer = Mesh(mesh.devices.reshape(16, 4, 2, mesh.shape["mem"]), AXES)
    placed = (P("mem", CELLS), P(CELLS), P(CELLS), P(CELLS), P("mem"))
    return jax.shard_map(shards, mesh=finer, in_specs=placed, out_specs=P("mem", CELLS), check_vma=False)
```
